32 devices in a mesh: gx: 8 (over y, x, core), pa: 4 (over z).
Axes of the slice: x: 2, y: 2, z: 4, core: 2. Of those that a mesh axis runs over, the one named last changes fastest.
Arguments:
- block_inverses: float32 [32, 32, 128, 128], P('gx', 'pa'), parts along dimension 1, may hold values from -0.25 to 1.07, as said below
- residual: float32 [32, 32, 128], P('gx', 'pa'), parts along dimension 1, may hold values from -0.3 to 0.3
- material: int32 [32, 32, 128], P('gx', 'pa'), parts along dimension 1, may hold values from 0 to 3
- fin_mask: int32 [32, 32, 128], P('gx', 'pa'), parts along dimension 1, may hold values 0 or 1
- phase_mask: int32 [32, 32, 128], P('gx', 'pa'), parts along dimension 1, may hold values 0 or 1
- k_table: float32 [4], replicated, may hold values from 0.95 to 1.05
Outputs:
- correction: float32 [32, 32, 128], P('gx', 'pa'), parts along dimension 1
- enthalpy_step: float32 [32, 32, 128], P('gx', 'pa'), parts along dimension 1
The draws below stay inside these ranges and needn't reach their ends.
There are 4 independent parts, one for each index of `pa`. The reference program is written for one: setup_inputs(seed, part) draws one part's arguments, and reference() takes and returns one part's arrays. A program takes and returns all parts, laid end to end along the dimension named above; an argument that names none is the same for every part. Nothing has to cross between parts.
Inputs may be any that keep to these rules, and one draw needn't show every extreme that they name: Each block block_inverses[i, t] is a symmetric matrix.
All inputs are finite; a program needn't handle non-finite values. No bound on the sum of `fin_mask` or of `phase_mask` on one device may be relied on, other than what follows from the above.
Results may differ from the reference program's by a relative error of at most 0.0003.
Values sent between devices are 32-bit elements; how exact they have to be, the bound alone decides.
No kernel may reach another device: no remote copies, remote signals or barrier semaphores. Data moves between devices by JAX's collectives and lax.ppermute only.
A program may use at most 128 MiB of HBM per device.

```python
import math
import jax
import jax.numpy as jnp
from jax import lax

B = 128
NMAT = 4
TL = 8
NX = 32


def draw_block_inverses(key, part):
    first_key, second_key = jax.random.split(jax.random.fold_in(key, 7))
    spread_values = 0.22 / math.sqrt(B)
    diagonal = jnp.exp(jax.random.uniform(first_key, (NX, TL, B), jnp.float32, math.log(0.95), math.log(1.07)))
    raw_part = jnp.clip(spread_values * jax.random.normal(second_key, (NX, TL, B, B), jnp.float32), -4.0 * spread_values, 4.0 * spread_values)
    symmetric = (raw_part + jnp.swapaxes(raw_part, -1, -2)) * 0.7071
    on_diagonal = lax.broadcasted_iota(jnp.int32, (B, B), 0) == lax.broadcasted_iota(jnp.int32, (B, B), 1)
    return jnp.where(on_diagonal, diagonal[..., None], symmetric)


def plant(entries, stream_key, least, top_value):
    longest = entries.shape.index(max(entries.shape))
    spots = []
    for shift in (0, 1):
        where = [jax.random.randint(jax.random.fold_in(stream_key, axis), (), 0, length) for axis, length in enumerate(entries.shape)]
        where[longest] = (where[longest] + shift) % entries.shape[longest]
        spots.append(tuple(where))
    return entries.at[spots[0]].set(least).at[spots[1]].set(top_value)


def shard_levels(key, dims, pieces, low, largest):
    level = 1.0
    for axis_at, blocks in pieces:
        draws = jax.random.uniform(jax.random.fold_in(jax.random.fold_in(key, 6), axis_at), (blocks,), jnp.float32, low / len(pieces), largest / len(pieces))
        level = level * jnp.repeat(jnp.exp(draws), dims[axis_at] // blocks).reshape((-1,) + (1,) * (len(dims) - 1 - axis_at))
    return level


def gaussian(rng, dims, scale, bound, cuts=(), kind=jnp.bfloat16):
    loudness = shard_levels(rng, dims, cuts, -0.22, 0.18) if cuts else 1.0
    values = jax.random.normal(rng, dims, jnp.float32) * scale * loudness
    return jnp.minimum(jnp.maximum(values, -bound), bound).astype(kind)


def setup_inputs(seed: int = 0, part: int = 0) -> dict:
    arg_keys = jax.random.split(jax.random.key(seed), 7)
    own_keys = jax.random.split(jax.random.fold_in(arg_keys[6], part), 7)
    return {
        "block_inverses": draw_block_inverses(jax.random.fold_in(jax.random.fold_in(arg_keys[6], part), 71), part),
        "residual": gaussian(own_keys[1], (NX, TL, B), 0.05, 0.3, ((0, 8),), jnp.float32),
        "material": plant(jax.random.randint(own_keys[2], (NX, TL, B), 0, NMAT), jax.random.fold_in(own_keys[2], 1), 0, NMAT - 1).astype(jnp.int32),
        "fin_mask": plant((jax.random.randint(own_keys[3], (NX, TL, B), 0, 3) < 1).astype(jnp.int32), jax.random.fold_in(own_keys[3], 1), 0, 1),
        "phase_mask": plant((jax.random.randint(own_keys[4], (NX, TL, B), 0, 4) < 1).astype(jnp.int32), jax.random.fold_in(own_keys[4], 1), 0, 1),
        "k_table": jnp.clip(jnp.exp(jax.random.uniform(arg_keys[5], (NMAT,), jnp.float32, math.log(0.95), math.log(1.05))), 0.95, 1.05),
    }


def apply_block(pivot_entries, vector):
    return jnp.einsum("tab,tb->ta", pivot_entries, vector, precision=lax.Precision.HIGHEST)


def reference(block_inverses, residual, material, fin_mask, phase_mask, k_table):
    material_codes = jnp.arange(NMAT, dtype=jnp.int32)
    conduct = jnp.sum(jnp.where(material[..., None] == material_codes, k_table, jnp.zeros_like(k_table)), axis=-1)
    earlier = jnp.concatenate([jnp.zeros_like(conduct[:1]), conduct[:-1]], axis=0)
    face_cond = 2.0 * conduct * earlier / (conduct + earlier) * (0.9 + 0.1 * fin_mask.astype(jnp.float32))
    zero_vector = jnp.zeros((TL, B), jnp.float32)

    def forward_step(state_vec, items):
        pivot_entries, source, faces_now = items
        state_vec = apply_block(pivot_entries, source + faces_now * state_vec)
        return state_vec, state_vec

    _, forward_vals = lax.scan(forward_step, zero_vector, (block_inverses, residual, face_cond))

    def backward_step(carried, items):
        pivot_entries, forward_now, faces_now = items
        solved = forward_now + apply_block(pivot_entries, carried)
        return faces_now * solved, solved

    _, correction = lax.scan(backward_step, zero_vector, (block_inverses, forward_vals, face_cond), reverse=True)
    enthalpy_step = correction * (1.0 + 2.0 * phase_mask.astype(jnp.float32))
    return (correction, enthalpy_step)
```

```python
import functools

import jax
import jax.numpy as jnp
from jax import lax
from jax.experimental import pallas as pl
from jax.experimental.pallas import tpu as pltpu
from jax.sharding import PartitionSpec as P

BF16 = jnp.bfloat16
F32 = jnp.float32
ROWS = 8
AXIS = "gx"


def split(x):
    high = x.astype(BF16)
    return high, (x - high.astype(F32)).astype(BF16)


def mul(left, right):
    lh, ll = split(left)
    rh, rl = split(right)
    lhs = jnp.concatenate([lh, ll], axis=1)
    rhs = jnp.concatenate(
        [jnp.concatenate([rh, rl], axis=1), jnp.concatenate([rh, jnp.zeros_like(rl)], axis=1)], axis=0
    )
    both = jnp.dot(lhs, rhs, preferred_element_type=F32)
    width = right.shape[1]
    return both[:, :width] + both[:, width:]


def mul_t(left, right):
    lh, ll = split(left)
    rh, rl = split(right)
    lhs = jnp.concatenate([lh, ll], axis=1)
    rhs = jnp.concatenate(
        [jnp.concatenate([rh, rh], axis=1), jnp.concatenate([rl, jnp.zeros_like(rl)], axis=1)], axis=0
    )
    both = lax.dot_general(lhs, rhs, (((1,), (1,)), ((), ())), preferred_element_type=F32)
    width = right.shape[0]
    return both[:, :width] + both[:, width:]


def face(conduct, earlier, fin_factor):
    return 2.0 * conduct * earlier / (conduct + earlier) * fin_factor


def conductivity(material, k_ref):
    total = jnp.zeros(material.shape, F32)
    for code in range(k_ref.shape[0]):
        total = total + jnp.where(material == code, k_ref[code], 0.0)
    return total


def fin_factor(fin):
    return 0.9 + 0.1 * fin.astype(F32)


def eye_mask(size):
    return lax.broadcasted_iota(jnp.int32, (size, size), 0) == lax.broadcasted_iota(
        jnp.int32, (size, size), 1
    )


def times(matrix, row, eye):
    column = jnp.sum(matrix * row, axis=1, keepdims=True)
    return jnp.sum(jnp.where(eye, column, 0.0), axis=0, keepdims=True)


def times_t(matrix, row, eye):
    column = jnp.sum(jnp.where(eye, row, 0.0), axis=1, keepdims=True)
    return jnp.sum(matrix * column, axis=0, keepdims=True)


def stack_rows(rows, cells):
    at = lax.broadcasted_iota(jnp.int32, (ROWS, cells), 0)
    out = jnp.zeros((ROWS, cells), F32)
    for place, row in enumerate(rows):
        out = jnp.where(at == place, jnp.broadcast_to(row, (ROWS, cells)), out)
    return out


def products(wide, source, faces, g_of, out_ref, ends):
    cells = wide[0].shape[1]
    tiles = range(len(wide))
    total = list(wide)
    for i in range(1, len(source)):
        for j in tiles:
            scaled = wide[j] * faces[i][j : j + 1]
            sh, sl = split(scaled[:cells])
            vh, vl = split(scaled[cells:] + stack_rows([source[i][j : j + 1]], cells))
            gh, gl = split(g_of(i, j))
            zero = jnp.zeros_like(gl)
            both = jnp.dot(
                jnp.concatenate([jnp.concatenate([sh, sl], axis=1), jnp.concatenate([vh, vl], axis=1)], axis=0),
                jnp.concatenate([jnp.concatenate([gh, gl], axis=1), jnp.concatenate([gh, zero], axis=1)], axis=0),
                preferred_element_type=F32,
            )
            wide[j] = both[:, :cells] + both[:, cells:]
            wh, wl = split(wide[j])
            both = lax.dot_general(
                jnp.concatenate([wh, wl], axis=1),
                jnp.concatenate([jnp.concatenate([sh, sh], axis=1), jnp.concatenate([sl, zero], axis=1)], axis=0),
                (((1,), (1,)), ((), ())),
                preferred_element_type=F32,
            )
            total[j] = total[j] + (both[:, :cells] + both[:, cells:])
    for j in tiles:
        out_ref[j, 0:cells] = wide[j][:cells]
        out_ref[j, cells : 2 * cells] = total[j][:cells]
        out_ref[j, 2 * cells :] = stack_rows(
            [wide[j][cells : cells + 1], total[j][cells : cells + 1]] + [end[j : j + 1] for end in ends], cells
        )


def first_kernel(k_hbm, mat_hbm, fin_hbm, res_hbm, g_hbm, out_ref, coef_ref, g_ref, k_ref, ints, sems):
    blocks, tiles, cells = res_hbm.shape
    half = tiles // 2
    lower = lax.axis_index(AXIS) % 2 == 1
    base = jnp.where(lower, 0, half)
    small = [
        pltpu.make_async_copy(k_hbm, k_ref, sems.at[0]),
        pltpu.make_async_copy(mat_hbm, ints.at[0], sems.at[1]),
        pltpu.make_async_copy(fin_hbm, ints.at[1], sems.at[2]),
        pltpu.make_async_copy(res_hbm, coef_ref.at[pl.ds(0, blocks)], sems.at[3]),
    ]
    places = [base + j for j in range(half)] + [half - base + j for j in range(half)]
    large = [
        pltpu.make_async_copy(g_hbm.at[:, at], g_ref.at[:, at], sems.at[4 + n])
        for n, at in enumerate(places)
    ]
    for copy in small + large:
        copy.start()
    for copy in small:
        copy.wait()
    conduct = [conductivity(ints[0, i], k_ref) for i in range(blocks)]
    factor = [fin_factor(ints[1, i]) for i in range(blocks)]
    faces = [None] + [face(conduct[i], conduct[i - 1], factor[i]) for i in range(1, blocks)]
    ends = [conduct[0], conduct[-1], factor[0]]
    for n, row in enumerate(faces[1:] + ends):
        coef_ref[blocks + n] = row

    def pick(x):
        return jnp.where(lower, x[:half], x[half:])

    source = [pick(coef_ref[i]) for i in range(blocks)]
    eye = eye_mask(cells)
    wide = []
    for j in range(half):
        large[j].wait()
        g0 = g_ref[0, base + j]
        wide.append(jnp.concatenate([g0, stack_rows([times(g0, source[0][j : j + 1], eye)], cells)], axis=0))
    products(
        wide, source, [None] + [pick(f) for f in faces[1:]], lambda i, j: g_ref[i, base + j], out_ref,
        [pick(end) for end in ends],
    )
    for copy in large[half:]:
        copy.wait()


def second_kernel(coef_ref, g_ref, out_ref):
    blocks, tiles, cells = g_ref.shape[:3]
    half = tiles // 2
    upper = lax.axis_index(AXIS) % 2 == 1
    base = jnp.where(upper, half, 0)

    def pick(n):
        return jnp.where(upper, coef_ref[n, half:], coef_ref[n, :half])

    source = [pick(i) for i in range(blocks)]
    faces = [None] + [pick(blocks + i) for i in range(blocks - 1)]
    eye = eye_mask(cells)
    wide = []
    for j in range(half):
        g0 = g_ref[0, base + j]
        wide.append(jnp.concatenate([g0, stack_rows([times(g0, source[0][j : j + 1], eye)], cells)], axis=0))
    products(
        wide, source, faces, lambda i, j: g_ref[i, base + j], out_ref,
        [pick(2 * blocks - 1 + n) for n in range(3)],
    )


def response_kernel(coef_ref, keep_ref, got_ref, give_ref, gain_ref, g_ref, out_ref, const_ref):
    blocks, tiles, cells = g_ref.shape[:3]
    half = tiles // 2
    is_second = lax.axis_index(AXIS) % 2 == 1
    base = jnp.where(is_second, half, 0)
    eye = jnp.where(eye_mask(cells), 1.0, 0.0)

    def reorder(x):
        return jnp.where(is_second, jnp.concatenate([x[half:], x[:half]], axis=0), x)

    source = [reorder(coef_ref[i]) for i in range(blocks)]
    faces = [None] + [reorder(coef_ref[blocks + i]) for i in range(blocks - 1)]
    nothing = jnp.zeros((cells, cells), F32)
    for group in range(2):
        own_ref, other_ref = (keep_ref, got_ref) if group == 0 else (give_ref, gain_ref)
        start = base if group == 0 else half - base
        lead, tail, values = {}, {}, {}
        for j in range(half):
            own, other = own_ref[j], other_ref[j]
            first = jnp.where(is_second, other, own)
            last = jnp.where(is_second, own, other)
            va, vb = first[2 * cells :], last[2 * cells :]
            between = face(vb[2:3], va[3:4], vb[4:5])
            scaled = jnp.concatenate([first[:cells], stack_rows([va[0:1]], cells)], axis=0) * between
            back = mul(scaled, last[cells : 2 * cells])
            back_const = back[cells:] + stack_rows([vb[1:2]], cells)
            tail[j] = jnp.concatenate(
                [
                    jnp.where(is_second, 0.0, back[:cells] * between),
                    jnp.where(is_second, eye, last[:cells].T * between),
                    jnp.where(is_second, 0.0, back_const * between),
                ],
                axis=0,
            )
            lead[j] = jnp.concatenate(
                [
                    jnp.where(is_second, scaled[:cells], eye),
                    jnp.where(is_second, scaled[cells:], 0.0)
                    + stack_rows([source[0][group * half + j : group * half + j + 1]], cells),
                ],
                axis=0,
            )
        for i in range(blocks):
            for j in range(half):
                values[i, j] = mul(lead[j], g_ref[i, start + j])
                if i < blocks - 1:
                    at = group * half + j
                    scaled = values[i, j] * faces[i + 1][at : at + 1]
                    below = scaled[cells:] + stack_rows([source[i + 1][at : at + 1]], cells)
                    lead[j] = jnp.concatenate([scaled[:cells], below], axis=0)
        for i in reversed(range(blocks)):
            for j in range(half):
                moved = mul(tail[j], g_ref[i, start + j])
                add = jnp.concatenate([values[i, j][:cells], nothing, values[i, j][cells:]], axis=0)
                solved = moved + add
                out_ref[i, start + j] = solved[: 2 * cells]
                const_ref[i, start + j] = solved[2 * cells :]
                if i:
                    at = group * half + j
                    tail[j] = solved * faces[i][at : at + 1]


def merge_kernel(keep_ref, got_ref, *out_refs):
    half, height, cells = keep_ref.shape
    here = lax.axis_index(AXIS)
    is_second = here % 2 == 1
    chip = (here % (2 * half)) // 2
    for d in range(half):
        tile = chip ^ d
        keep, got = keep_ref[tile], got_ref[tile]
        first = jnp.where(is_second, got, keep)
        second = jnp.where(is_second, keep, got)
        va, vb = first[2 * cells :], second[2 * cells :]
        between = face(vb[2:3], va[3:4], vb[4:5])
        scaled = jnp.concatenate([first[:cells], stack_rows([va[0:1]], cells)], axis=0) * between
        moved = mul(scaled, second[:cells])
        squared = mul(scaled, second[cells : 2 * cells])
        lower = squared[cells:] + stack_rows([vb[1:2]], cells)
        squared = jnp.concatenate([squared[:cells], lower], axis=0)
        total = mul_t(squared, scaled[:cells])
        out_ref = out_refs[d]
        out_ref[0:cells] = moved[:cells]
        out_ref[cells : 2 * cells] = first[cells : 2 * cells] + total[:cells]
        out_ref[2 * cells :] = stack_rows(
            [
                moved[cells : cells + 1] + vb[0:1],
                total[cells : cells + 1] + va[1:2],
                va[2:3],
                vb[3:4],
                va[4:5],
            ],
            cells,
        )


def chain_kernel(with_edge, *refs):
    refs, nodes = refs[:-1], refs[-1]
    if with_edge:
        edge_ref, refs = refs[0], refs[1:]
    count, height, cells = nodes.shape
    refs, out_refs, ends = refs[:count], refs[count:-1], refs[-1]
    chip = (lax.axis_index(AXIS) % (2 * count)) // 2
    for d in range(count):
        nodes[chip ^ d] = refs[d][...]
    eye = eye_mask(cells)
    vectors = [nodes[k, 2 * cells :] for k in range(count)]
    faces = [None] + [
        face(vectors[k][2:3], vectors[k - 1][3:4], vectors[k][4:5]) for k in range(1, count)
    ]
    entering, arriving = [None] * count, [None] * count
    leaving = vectors[0][0:1]
    if with_edge:
        entering[0], arriving[-1] = edge_ref[0:1], edge_ref[1:2]
        leaving = leaving + times_t(nodes[0, 0:cells], entering[0], eye)
    for k in range(1, count):
        entering[k] = faces[k] * leaving
        if k < count - 1:
            leaving = vectors[k][0:1] + times_t(nodes[k, 0:cells], entering[k], eye)
    heads = [None] + [
        vectors[k][1:2] + times(nodes[k, cells : 2 * cells], entering[k], eye) for k in range(1, count)
    ]
    for k in reversed(range(1, count)):
        head = heads[k]
        if arriving[k] is not None:
            head = head + times(nodes[k, 0:cells], arriving[k], eye)
        arriving[k - 1] = faces[k] * head
    zero = jnp.zeros((1, cells), F32)
    for k in range(count):
        ends[k] = stack_rows(
            [zero if entering[k] is None else entering[k], zero if arriving[k] is None else arriving[k]],
            cells,
        )
    for d in range(count):
        out_refs[d][...] = ends[chip ^ d]


def order_kernel(*refs):
    out_ref = refs[-1]
    count = out_ref.shape[0]
    chip = (lax.axis_index(AXIS) % (2 * count)) // 2
    for d in range(count):
        out_ref[chip ^ d] = refs[d][...]


def finish_kernel(mine_ref, theirs_ref, phase_ref, out_ref, const_ref, corr_ref, step_ref, ends_ref):
    blocks, tiles, cells = corr_ref.shape
    half = tiles // 2
    is_second = lax.axis_index(AXIS) % 2 == 1
    ends_ref[:half] = jnp.where(is_second, theirs_ref[...], mine_ref[...])
    ends_ref[half:] = jnp.where(is_second, mine_ref[...], theirs_ref[...])
    eye = eye_mask(cells)
    for j in range(tiles):
        up = jnp.sum(jnp.where(eye, ends_ref[j, 0:1], 0.0), axis=1, keepdims=True)
        down = jnp.sum(jnp.where(eye, ends_ref[j, 1:2], 0.0), axis=1, keepdims=True)
        for i in range(blocks):
            both = out_ref[i, j, 0:cells] * up + out_ref[i, j, cells : 2 * cells] * down
            solved = const_ref[i, j, 0:1] + jnp.sum(both, axis=0, keepdims=True)
            corr_ref[i, j : j + 1] = solved
            step_ref[i, j : j + 1] = solved * (1.0 + 2.0 * phase_ref[i, j : j + 1].astype(F32))


VMEM = pl.BlockSpec(memory_space=pltpu.VMEM)
HBM = pl.BlockSpec(memory_space=pltpu.HBM)
LIMIT = pltpu.CompilerParams(vmem_limit_bytes=16 << 20)


def cost(flops, moved):
    return pl.CostEstimate(flops=flops, bytes_accessed=moved, transcendentals=0)


def send(x, distance):
    return lax.ppermute(x, AXIS, [(i, i ^ distance) for i in range(lax.axis_size(AXIS))])


def exact(left, right):
    return jnp.dot(left, right, precision=lax.Precision.HIGHEST)


def outer_edge(nodes, devices):
    cells = nodes[0].shape[-1]

    def parts(node):
        return node[:cells], node[cells : 2 * cells], node[2 * cells :]

    def join(first, second):
        (ma, qa, va), (mb, qb, vb) = parts(first), parts(second)
        between = face(vb[2], va[3], vb[4])
        scaled, shift = ma * between, va[0] * between
        q = qa + exact(exact(scaled, qb), scaled.T)
        tail = exact(shift, mb) + vb[0]
        lead = va[1] + exact(scaled, exact(qb, shift) + vb[1])
        rest = jnp.zeros((ROWS - 5, cells), F32)
        rows = jnp.stack([tail, lead, va[2], vb[3], va[4]])
        return jnp.concatenate([exact(scaled, mb), q, rows, rest], axis=0)

    groups = lax.axis_size(AXIS) // devices
    whole = functools.reduce(join, [nodes[k] for k in range(nodes.shape[0])])
    members = [[g * devices + q for g in range(groups)] for q in range(devices)]
    every = lax.all_gather(whole, AXIS, axis=0, axis_index_groups=members)
    split_up = [parts(every[g]) for g in range(groups)]
    faces = [face(b[2][2], a[2][3], b[2][4]) for a, b in zip(split_up[:-1], split_up[1:])]
    entering = [jnp.zeros((cells,), F32)]
    for g in range(groups - 1):
        m, _, v = split_up[g]
        entering.append(faces[g] * (exact(entering[g], m) + v[0]))
    arriving = [jnp.zeros((cells,), F32)]
    for g in reversed(range(1, groups)):
        m, q, v = split_up[g]
        arriving.append(faces[g - 1] * (exact(m, arriving[-1]) + exact(q, entering[g]) + v[1]))
    arriving.reverse()
    own = lax.axis_index(AXIS) // devices
    both = jnp.stack([jnp.stack(entering)[own], jnp.stack(arriving)[own]])
    return jnp.concatenate([both, jnp.zeros((ROWS - 2, cells), F32)], axis=0)


def on_device(block_inverses, residual, material, fin_mask, phase_mask, k_table):
    blocks, tiles, cells = residual.shape
    half = tiles // 2
    height = 2 * cells + ROWS
    map_bytes = 4 * height * cells

    map_shape = (half, height, cells)
    work = cost(24 * half * blocks * cells**3, 8 * half * blocks * cells**2)
    given = [pltpu.with_memory_space_constraint(x, pltpu.HBM) for x in (k_table, material, fin_mask, residual, block_inverses)]
    give, coef, inverses = pl.pallas_call(
        first_kernel,
        out_shape=(
            pltpu.VMEM(map_shape, F32),
            pltpu.VMEM((2 * blocks + 2, tiles, cells), F32),
            pltpu.VMEM(block_inverses.shape, F32),
        ),
        in_specs=[HBM] * 5,
        out_specs=(VMEM,) * 3,
        scratch_shapes=[
            pltpu.SMEM(k_table.shape, F32),
            pltpu.VMEM((2, blocks, tiles, cells), jnp.int32),
            pltpu.SemaphoreType.DMA((4 + tiles,)),
        ],
        compiler_params=LIMIT,
        cost_estimate=work,
    )(*given)
    got = send(give, 1)
    keep = pl.pallas_call(
        second_kernel,
        out_shape=jax.ShapeDtypeStruct(map_shape, F32),
        in_specs=[VMEM, VMEM],
        out_specs=VMEM,
        compiler_params=LIMIT,
        cost_estimate=work,
    )(coef, inverses)
    gain = send(keep, 1)
    responses, constants = pl.pallas_call(
        response_kernel,
        out_shape=(
            jax.ShapeDtypeStruct((blocks, tiles, 2 * cells, cells), F32),
            jax.ShapeDtypeStruct((blocks, tiles, ROWS, cells), F32),
        ),
        in_specs=[VMEM] * 6,
        out_specs=(VMEM, VMEM),
        compiler_params=LIMIT,
        cost_estimate=cost(48 * tiles * blocks * cells**3, 16 * tiles * blocks * cells**2),
    )(coef, keep, got, give, gain, inverses)
    node = jax.ShapeDtypeStruct((height, cells), F32)
    joined = pl.pallas_call(
        merge_kernel,
        out_shape=(node,) * half,
        in_specs=[VMEM, VMEM],
        out_specs=(VMEM,) * half,
        compiler_params=LIMIT,
        cost_estimate=cost(24 * half * cells**3, 3 * half * map_bytes),
    )(keep, got)
    arrived = [joined[0]] + [send(joined[d], 2 * d) for d in range(1, half)]
    grouped = lax.axis_size(AXIS) > tiles
    edge = []
    if grouped:
        chip = (lax.axis_index(AXIS) % tiles) // 2
        ordered = jnp.stack(arrived)[jnp.arange(half) ^ chip]
        edge = [outer_edge(ordered, tiles)]
    end = jax.ShapeDtypeStruct((ROWS, cells), F32)
    ends = pl.pallas_call(
        functools.partial(chain_kernel, grouped),
        out_shape=(end,) * half,
        in_specs=[VMEM] * (half + len(edge)),
        out_specs=(VMEM,) * half,
        scratch_shapes=[pltpu.VMEM((half, ROWS, cells), F32), pltpu.VMEM((half, height, cells), F32)],
        compiler_params=LIMIT,
        cost_estimate=cost(8 * half * cells**2, half * map_bytes),
    )(*edge, *arrived)
    ends = [ends[0]] + [send(ends[d], 2 * d) for d in range(1, half)]
    mine = pl.pallas_call(
        order_kernel,
        out_shape=jax.ShapeDtypeStruct((half, ROWS, cells), F32),
        in_specs=[VMEM] * half,
        out_specs=VMEM,
        compiler_params=LIMIT,
        cost_estimate=cost(0, 8 * half * ROWS * cells),
    )(*ends)
    theirs = send(mine, 1)
    shape = jax.ShapeDtypeStruct((blocks, tiles, cells), F32)
    return pl.pallas_call(
        finish_kernel,
        out_shape=(shape, shape),
        in_specs=[VMEM] * 5,
        out_specs=(VMEM, VMEM),
        scratch_shapes=[pltpu.VMEM((tiles, ROWS, cells), F32)],
        compiler_params=LIMIT,
        cost_estimate=cost(4 * blocks * tiles * cells**2, 8 * blocks * tiles * cells**2),
    )(mine, theirs, phase_mask, responses, constants)


def solution(mesh):
    return jax.shard_map(
        on_device,
        mesh=mesh,
        in_specs=(
            P("gx", "pa", None, None),
            P("gx", "pa", None),
            P("gx", "pa", None),
            P("gx", "pa", None),
            P("gx", "pa", None),
            P(),
        ),
        out_specs=(P("gx", "pa", None), P("gx", "pa", None)),
        check_vma=False,
    )
```

```python
import functools

import jax
import jax.numpy as jnp
from jax import lax
from jax.experimental import pallas as pl
from jax.experimental.pallas import tpu as pltpu
from jax.sharding import PartitionSpec as P

BF16 = jnp.bfloat16
F32 = jnp.float32
ROWS = 8
AXIS = "gx"


def split(x):
    high = x.astype(BF16)
    return high, (x - high.astype(F32)).astype(BF16)


def mul(left, right):
    lh, ll = split(left)
    rh, rl = split(right)
    lhs = jnp.concatenate([lh, ll], axis=1)
    rhs = jnp.concatenate(
        [jnp.concatenate([rh, rl], axis=1), jnp.concatenate([rh, jnp.zeros_like(rl)], axis=1)], axis=0
    )
    both = jnp.dot(lhs, rhs, preferred_element_type=F32)
    width = right.shape[1]
    return both[:, :width] + both[:, width:]


def mul_t(left, right):
    lh, ll = split(left)
    rh, rl = split(right)
    lhs = jnp.concatenate([lh, ll], axis=1)
    rhs = jnp.concatenate(
        [jnp.concatenate([rh, rh], axis=1), jnp.concatenate([rl, jnp.zeros_like(rl)], axis=1)], axis=0
    )
    both = lax.dot_general(lhs, rhs, (((1,), (1,)), ((), ())), preferred_element_type=F32)
    width = right.shape[0]
    return both[:, :width] + both[:, width:]


def face(conduct, earlier, fin_factor):
    return 2.0 * conduct * earlier / (conduct + earlier) * fin_factor


def conductivity(material, k_ref):
    total = jnp.zeros(material.shape, F32)
    for code in range(k_ref.shape[0]):
        total = total + jnp.where(material == code, k_ref[code], 0.0)
    return total


def fin_factor(fin):
    return 0.9 + 0.1 * fin.astype(F32)


def eye_mask(size):
    return lax.broadcasted_iota(jnp.int32, (size, size), 0) == lax.broadcasted_iota(
        jnp.int32, (size, size), 1
    )


def times(matrix, row, eye):
    column = jnp.sum(matrix * row, axis=1, keepdims=True)
    return jnp.sum(jnp.where(eye, column, 0.0), axis=0, keepdims=True)


def times_t(matrix, row, eye):
    column = jnp.sum(jnp.where(eye, row, 0.0), axis=1, keepdims=True)
    return jnp.sum(matrix * column, axis=0, keepdims=True)


def stack_rows(rows, cells):
    at = lax.broadcasted_iota(jnp.int32, (ROWS, cells), 0)
    out = jnp.zeros((ROWS, cells), F32)
    for place, row in enumerate(rows):
        out = jnp.where(at == place, jnp.broadcast_to(row, (ROWS, cells)), out)
    return out


def products(wide, source, faces, g_of, out_ref, ends):
    cells = wide[0].shape[1]
    tiles = range(len(wide))
    total = list(wide)
    for i in range(1, len(source)):
        for j in tiles:
            scaled = wide[j] * faces[i][j : j + 1]
            sh, sl = split(scaled[:cells])
            vh, vl = split(scaled[cells:] + stack_rows([source[i][j : j + 1]], cells))
            gh, gl = split(g_of(i, j))
            zero = jnp.zeros_like(gl)
            both = jnp.dot(
                jnp.concatenate([jnp.concatenate([sh, sl], axis=1), jnp.concatenate([vh, vl], axis=1)], axis=0),
                jnp.concatenate([jnp.concatenate([gh, gl], axis=1), jnp.concatenate([gh, zero], axis=1)], axis=0),
                preferred_element_type=F32,
            )
            wide[j] = both[:, :cells] + both[:, cells:]
            wh, wl = split(wide[j])
            both = lax.dot_general(
                jnp.concatenate([wh, wl], axis=1),
                jnp.concatenate([jnp.concatenate([sh, sh], axis=1), jnp.concatenate([sl, zero], axis=1)], axis=0),
                (((1,), (1,)), ((), ())),
                preferred_element_type=F32,
            )
            total[j] = total[j] + (both[:, :cells] + both[:, cells:])
    for j in tiles:
        out_ref[j, 0:cells] = wide[j][:cells]
        out_ref[j, cells : 2 * cells] = total[j][:cells]
        out_ref[j, 2 * cells :] = stack_rows(
            [wide[j][cells : cells + 1], total[j][cells : cells + 1]] + [end[j : j + 1] for end in ends], cells
        )


def first_kernel(k_hbm, mat_hbm, fin_hbm, res_hbm, g_hbm, out_ref, coef_ref, g_ref, k_ref, ints, sems):
    blocks, tiles, cells = res_hbm.shape
    half = tiles // 2
    lower = lax.axis_index(AXIS) % 2 == 1
    base = jnp.where(lower, 0, half)
    small = [
        pltpu.make_async_copy(k_hbm, k_ref, sems.at[0]),
        pltpu.make_async_copy(mat_hbm, ints.at[0], sems.at[1]),
        pltpu.make_async_copy(fin_hbm, ints.at[1], sems.at[2]),
        pltpu.make_async_copy(res_hbm, coef_ref.at[pl.ds(0, blocks)], sems.at[3]),
    ]
    places = [base + j for j in range(half)] + [half - base + j for j in range(half)]
    large = [
        pltpu.make_async_copy(g_hbm.at[:, at], g_ref.at[:, at], sems.at[4 + n])
        for n, at in enumerate(places)
    ]
    for copy in small + large:
        copy.start()
    for copy in small:
        copy.wait()
    conduct = [conductivity(ints[0, i], k_ref) for i in range(blocks)]
    factor = [fin_factor(ints[1, i]) for i in range(blocks)]
    faces = [None] + [face(conduct[i], conduct[i - 1], factor[i]) for i in range(1, blocks)]
    ends = [conduct[0], conduct[-1], factor[0]]
    for n, row in enumerate(faces[1:] + ends):
        coef_ref[blocks + n] = row

    def pick(x):
        return jnp.where(lower, x[:half], x[half:])

    source = [pick(coef_ref[i]) for i in range(blocks)]
    eye = eye_mask(cells)
    wide = []
    for j in range(half):
        large[j].wait()
        g0 = g_ref[0, base + j]
        wide.append(jnp.concatenate([g0, stack_rows([times(g0, source[0][j : j + 1], eye)], cells)], axis=0))
    products(
        wide, source, [None] + [pick(f) for f in faces[1:]], lambda i, j: g_ref[i, base + j], out_ref,
        [pick(end) for end in ends],
    )
    for copy in large[half:]:
        copy.wait()


def second_kernel(coef_ref, g_ref, out_ref):
    blocks, tiles, cells = g_ref.shape[:3]
    half = tiles // 2
    upper = lax.axis_index(AXIS) % 2 == 1
    base = jnp.where(upper, half, 0)

    def pick(n):
        return jnp.where(upper, coef_ref[n, half:], coef_ref[n, :half])

    source = [pick(i) for i in range(blocks)]
    faces = [None] + [pick(blocks + i) for i in range(blocks - 1)]
    eye = eye_mask(cells)
    wide = []
    for j in range(half):
        g0 = g_ref[0, base + j]
        wide.append(jnp.concatenate([g0, stack_rows([times(g0, source[0][j : j + 1], eye)], cells)], axis=0))
    products(
        wide, source, faces, lambda i, j: g_ref[i, base + j], out_ref,
        [pick(2 * blocks - 1 + n) for n in range(3)],
    )


def response_kernel(coef_ref, keep_ref, got_ref, give_ref, gain_ref, g_ref, out_ref, const_ref):
    blocks, tiles, cells = g_ref.shape[:3]
    half = tiles // 2
    is_second = lax.axis_index(AXIS) % 2 == 1
    base = jnp.where(is_second, half, 0)
    eye = jnp.where(eye_mask(cells), 1.0, 0.0)

    def reorder(x):
        return jnp.where(is_second, jnp.concatenate([x[half:], x[:half]], axis=0), x)

    source = [reorder(coef_ref[i]) for i in range(blocks)]
    faces = [None] + [reorder(coef_ref[blocks + i]) for i in range(blocks - 1)]
    nothing = jnp.zeros((cells, cells), F32)
    for group in range(2):
        own_ref, other_ref = (keep_ref, got_ref) if group == 0 else (give_ref, gain_ref)
        start = base if group == 0 else half - base
        lead, tail, values = {}, {}, {}
        for j in range(half):
            own, other = own_ref[j], other_ref[j]
            first = jnp.where(is_second, other, own)
            last = jnp.where(is_second, own, other)
            va, vb = first[2 * cells :], last[2 * cells :]
            between = face(vb[2:3], va[3:4], vb[4:5])
            scaled = jnp.concatenate([first[:cells], stack_rows([va[0:1]], cells)], axis=0) * between
            back = mul(scaled, last[cells : 2 * cells])
            back_const = back[cells:] + stack_rows([vb[1:2]], cells)
            tail[j] = jnp.concatenate(
                [
                    jnp.where(is_second, 0.0, back[:cells] * between),
                    jnp.where(is_second, eye, last[:cells].T * between),
                    jnp.where(is_second, 0.0, back_const * between),
                ],
                axis=0,
            )
            lead[j] = jnp.concatenate(
                [
                    jnp.where(is_second, scaled[:cells], eye),
                    jnp.where(is_second, scaled[cells:], 0.0)
                    + stack_rows([source[0][group * half + j : group * half + j + 1]], cells),
                ],
                axis=0,
            )
        for i in range(blocks):
            for j in range(half):
                values[i, j] = mul(lead[j], g_ref[i, start + j])
                if i < blocks - 1:
                    at = group * half + j
                    scaled = values[i, j] * faces[i + 1][at : at + 1]
                    below = scaled[cells:] + stack_rows([source[i + 1][at : at + 1]], cells)
                    lead[j] = jnp.concatenate([scaled[:cells], below], axis=0)
        for i in reversed(range(blocks)):
            for j in range(half):
                moved = mul(tail[j], g_ref[i, start + j])
                add = jnp.concatenate([values[i, j][:cells], nothing, values[i, j][cells:]], axis=0)
                solved = moved + add
                out_ref[i, start + j] = solved[: 2 * cells]
                const_ref[i, start + j] = solved[2 * cells :]
                if i:
                    at = group * half + j
                    tail[j] = solved * faces[i][at : at + 1]


def merge_kernel(keep_ref, got_ref, *out_refs):
    half, height, cells = keep_ref.shape
    here = lax.axis_index(AXIS)
    is_second = here % 2 == 1
    chip = (here % (2 * half)) // 2
    for d in range(half):
        tile = chip ^ d
        keep, got = keep_ref[tile], got_ref[tile]
        first = jnp.where(is_second, got, keep)
        second = jnp.where(is_second, keep, got)
        va, vb = first[2 * cells :], second[2 * cells :]
        between = face(vb[2:3], va[3:4], vb[4:5])
        scaled = jnp.concatenate([first[:cells], stack_rows([va[0:1]], cells)], axis=0) * between
        moved = mul(scaled, second[:cells])
        squared = mul(scaled, second[cells : 2 * cells])
        lower = squared[cells:] + stack_rows([vb[1:2]], cells)
        squared = jnp.concatenate([squared[:cells], lower], axis=0)
        total = mul_t(squared, scaled[:cells])
        out_ref = out_refs[d]
        out_ref[0:cells] = moved[:cells]
        out_ref[cells : 2 * cells] = first[cells : 2 * cells] + total[:cells]
        out_ref[2 * cells :] = stack_rows(
            [
                moved[cells : cells + 1] + vb[0:1],
                total[cells : cells + 1] + va[1:2],
                va[2:3],
                vb[3:4],
                va[4:5],
            ],
            cells,
        )


def chain_kernel(with_edge, *refs):
    refs, nodes = refs[1:-1], refs[-1]
    if with_edge:
        edge_ref, refs = refs[0], refs[1:]
    count, height, cells = nodes.shape
    refs, out_refs, ends = refs[count - 1 :: -1], refs[count:-1], refs[-1]
    chip = (lax.axis_index(AXIS) % (2 * count)) // 2
    for d in range(count):
        nodes[chip ^ d] = refs[d][...]
    eye = eye_mask(cells)
    vectors = [nodes[k, 2 * cells :] for k in range(count)]
    faces = [None] + [
        face(vectors[k][2:3], vectors[k - 1][3:4], vectors[k][4:5]) for k in range(1, count)
    ]
    entering, arriving = [None] * count, [None] * count
    leaving = vectors[0][0:1]
    if with_edge:
        entering[0], arriving[-1] = edge_ref[0:1], edge_ref[1:2]
        leaving = leaving + times_t(nodes[0, 0:cells], entering[0], eye)
    for k in range(1, count):
        entering[k] = faces[k] * leaving
        if k < count - 1:
            leaving = vectors[k][0:1] + times_t(nodes[k, 0:cells], entering[k], eye)
    heads = [None] + [
        vectors[k][1:2] + times(nodes[k, cells : 2 * cells], entering[k], eye) for k in range(1, count)
    ]
    for k in reversed(range(1, count)):
        head = heads[k]
        if arriving[k] is not None:
            head = head + times(nodes[k, 0:cells], arriving[k], eye)
        arriving[k - 1] = faces[k] * head
    zero = jnp.zeros((1, cells), F32)
    for k in range(count):
        ends[k] = stack_rows(
            [zero if entering[k] is None else entering[k], zero if arriving[k] is None else arriving[k]],
            cells,
        )
    for d in range(count):
        out_refs[d][...] = ends[chip ^ d]


def order_kernel(*refs):
    out_ref = refs[-1]
    count = out_ref.shape[0]
    chip = (lax.axis_index(AXIS) % (2 * count)) // 2
    for d in range(count):
        out_ref[chip ^ d] = refs[count - 1 - d][...]


def finish_kernel(mine_ref, theirs_ref, phase_ref, out_ref, const_ref, corr_ref, step_ref, ends_ref):
    blocks, tiles, cells = corr_ref.shape
    half = tiles // 2
    is_second = lax.axis_index(AXIS) % 2 == 1
    ends_ref[:half] = jnp.where(is_second, theirs_ref[...], mine_ref[...])
    ends_ref[half:] = jnp.where(is_second, mine_ref[...], theirs_ref[...])
    eye = eye_mask(cells)
    for j in range(tiles):
        up = jnp.sum(jnp.where(eye, ends_ref[j, 0:1], 0.0), axis=1, keepdims=True)
        down = jnp.sum(jnp.where(eye, ends_ref[j, 1:2], 0.0), axis=1, keepdims=True)
        for i in range(blocks):
            both = out_ref[i, j, 0:cells] * up + out_ref[i, j, cells : 2 * cells] * down
            solved = const_ref[i, j, 0:1] + jnp.sum(both, axis=0, keepdims=True)
            corr_ref[i, j : j + 1] = solved
            step_ref[i, j : j + 1] = solved * (1.0 + 2.0 * phase_ref[i, j : j + 1].astype(F32))


VMEM = pl.BlockSpec(memory_space=pltpu.VMEM)
HBM = pl.BlockSpec(memory_space=pltpu.HBM)
LIMIT = pltpu.CompilerParams(vmem_limit_bytes=16 << 20)


def cost(flops, moved):
    return pl.CostEstimate(flops=flops, bytes_accessed=moved, transcendentals=0)


def send(x, distance):
    return lax.ppermute(x, AXIS, [(i, i ^ distance) for i in range(lax.axis_size(AXIS))])


def send_all(parts):
    arrived = {0: parts[0]}
    for d in reversed(range(1, len(parts))):
        arrived[d] = send(parts[d], 2 * d)
    return [arrived[d] for d in range(len(parts))]


def exact(left, right):
    return jnp.dot(left, right, precision=lax.Precision.HIGHEST)


def outer_edge(nodes, devices):
    cells = nodes[0].shape[-1]

    def parts(node):
        return node[:cells], node[cells : 2 * cells], node[2 * cells :]

    def join(first, second):
        (ma, qa, va), (mb, qb, vb) = parts(first), parts(second)
        between = face(vb[2], va[3], vb[4])
        scaled, shift = ma * between, va[0] * between
        q = qa + exact(exact(scaled, qb), scaled.T)
        tail = exact(shift, mb) + vb[0]
        lead = va[1] + exact(scaled, exact(qb, shift) + vb[1])
        rest = jnp.zeros((ROWS - 5, cells), F32)
        rows = jnp.stack([tail, lead, va[2], vb[3], va[4]])
        return jnp.concatenate([exact(scaled, mb), q, rows, rest], axis=0)

    groups = lax.axis_size(AXIS) // devices
    whole = functools.reduce(join, [nodes[k] for k in range(nodes.shape[0])])
    members = [[g * devices + q for g in range(groups)] for q in range(devices)]
    every = lax.all_gather(whole, AXIS, axis=0, axis_index_groups=members)
    split_up = [parts(every[g]) for g in range(groups)]
    faces = [face(b[2][2], a[2][3], b[2][4]) for a, b in zip(split_up[:-1], split_up[1:])]
    entering = [jnp.zeros((cells,), F32)]
    for g in range(groups - 1):
        m, _, v = split_up[g]
        entering.append(faces[g] * (exact(entering[g], m) + v[0]))
    arriving = [jnp.zeros((cells,), F32)]
    for g in reversed(range(1, groups)):
        m, q, v = split_up[g]
        arriving.append(faces[g - 1] * (exact(m, arriving[-1]) + exact(q, entering[g]) + v[1]))
    arriving.reverse()
    own = lax.axis_index(AXIS) // devices
    both = jnp.stack([jnp.stack(entering)[own], jnp.stack(arriving)[own]])
    return jnp.concatenate([both, jnp.zeros((ROWS - 2, cells), F32)], axis=0)


def on_device(block_inverses, residual, material, fin_mask, phase_mask, k_table):
    blocks, tiles, cells = residual.shape
    half = tiles // 2
    height = 2 * cells + ROWS
    map_bytes = 4 * height * cells

    map_shape = (half, height, cells)
    work = cost(24 * half * blocks * cells**3, 8 * half * blocks * cells**2)
    given = [pltpu.with_memory_space_constraint(x, pltpu.HBM) for x in (k_table, material, fin_mask, residual, block_inverses)]
    give, coef, inverses = pl.pallas_call(
        first_kernel,
        out_shape=(
            pltpu.VMEM(map_shape, F32),
            pltpu.VMEM((2 * blocks + 2, tiles, cells), F32),
            pltpu.VMEM(block_inverses.shape, F32),
        ),
        in_specs=[HBM] * 5,
        out_specs=(VMEM,) * 3,
        scratch_shapes=[
            pltpu.SMEM(k_table.shape, F32),
            pltpu.VMEM((2, blocks, tiles, cells), jnp.int32),
            pltpu.SemaphoreType.DMA((4 + tiles,)),
        ],
        compiler_params=LIMIT,
        cost_estimate=work,
    )(*given)
    got = send(give, 1)
    keep = pl.pallas_call(
        second_kernel,
        out_shape=jax.ShapeDtypeStruct(map_shape, F32),
        in_specs=[VMEM, VMEM],
        out_specs=VMEM,
        compiler_params=LIMIT,
        cost_estimate=work,
    )(coef, inverses)
    gain = send(keep, 1)
    responses, constants = pl.pallas_call(
        response_kernel,
        out_shape=(
            jax.ShapeDtypeStruct((blocks, tiles, 2 * cells, cells), F32),
            jax.ShapeDtypeStruct((blocks, tiles, ROWS, cells), F32),
        ),
        in_specs=[VMEM] * 6,
        out_specs=(VMEM, VMEM),
        compiler_params=LIMIT,
        cost_estimate=cost(48 * tiles * blocks * cells**3, 16 * tiles * blocks * cells**2),
    )(coef, keep, got, give, gain, inverses)
    node = jax.ShapeDtypeStruct((height, cells), F32)
    joined = pl.pallas_call(
        merge_kernel,
        out_shape=(node,) * half,
        in_specs=[VMEM, VMEM],
        out_specs=(VMEM,) * half,
        compiler_params=LIMIT,
        cost_estimate=cost(24 * half * cells**3, 3 * half * map_bytes),
    )(keep, got)
    arrived = send_all(joined)
    grouped = lax.axis_size(AXIS) > tiles
    edge = []
    if grouped:
        chip = (lax.axis_index(AXIS) % tiles) // 2
        ordered = jnp.stack(arrived)[jnp.arange(half) ^ chip]
        edge = [outer_edge(ordered, tiles)]
    end = jax.ShapeDtypeStruct((ROWS, cells), F32)
    ends = pl.pallas_call(
        functools.partial(chain_kernel, grouped),
        out_shape=(end,) * half,
        in_specs=[pl.BlockSpec(memory_space=pl.ANY)] + [VMEM] * (half + len(edge)),
        out_specs=(VMEM,) * half,
        scratch_shapes=[pltpu.VMEM((half, ROWS, cells), F32), pltpu.VMEM((half, height, cells), F32)],
        compiler_params=LIMIT,
        cost_estimate=cost(8 * half * cells**2, half * map_bytes),
    )(constants, *edge, *arrived[::-1])
    ends = send_all(ends)
    mine = pl.pallas_call(
        order_kernel,
        out_shape=jax.ShapeDtypeStruct((half, ROWS, cells), F32),
        in_specs=[VMEM] * half,
        out_specs=VMEM,
        compiler_params=LIMIT,
        cost_estimate=cost(0, 8 * half * ROWS * cells),
    )(*ends[::-1])
    theirs = send(mine, 1)
    shape = jax.ShapeDtypeStruct((blocks, tiles, cells), F32)
    return pl.pallas_call(
        finish_kernel,
        out_shape=(shape, shape),
        in_specs=[VMEM] * 5,
        out_specs=(VMEM, VMEM),
        scratch_shapes=[pltpu.VMEM((tiles, ROWS, cells), F32)],
        compiler_params=LIMIT,
        cost_estimate=cost(4 * blocks * tiles * cells**2, 8 * blocks * tiles * cells**2),
    )(mine, theirs, phase_mask, responses, constants)


def solution(mesh):
    return jax.shard_map(
        on_device,
        mesh=mesh,
        in_specs=(
            P("gx", "pa", None, None),
            P("gx", "pa", None),
            P("gx", "pa", None),
            P("gx", "pa", None),
            P("gx", "pa", None),
            P(),
        ),
        out_specs=(P("gx", "pa", None), P("gx", "pa", None)),
        check_vma=False,
    )
```

```python
import functools

import jax
import jax.numpy as jnp
from jax import lax
from jax.experimental import pallas as pl
from jax.experimental.pallas import tpu as pltpu
from jax.sharding import PartitionSpec as P

BF16 = jnp.bfloat16
F32 = jnp.float32
ROWS = 8
AXIS = "gx"


def split(x):
    high = x.astype(BF16)
    return high, (x - high.astype(F32)).astype(BF16)


def mul(left, right):
    lh, ll = split(left)
    rh, rl = split(right)
    lhs = jnp.concatenate([lh, ll], axis=1)
    rhs = jnp.concatenate(
        [jnp.concatenate([rh, rl], axis=1), jnp.concatenate([rh, jnp.zeros_like(rl)], axis=1)], axis=0
    )
    both = jnp.dot(lhs, rhs, preferred_element_type=F32)
    width = right.shape[1]
    return both[:, :width] + both[:, width:]


def mul_t(left, right):
    lh, ll = split(left)
    rh, rl = split(right)
    lhs = jnp.concatenate([lh, ll], axis=1)
    rhs = jnp.concatenate(
        [jnp.concatenate([rh, rh], axis=1), jnp.concatenate([rl, jnp.zeros_like(rl)], axis=1)], axis=0
    )
    both = lax.dot_general(lhs, rhs, (((1,), (1,)), ((), ())), preferred_element_type=F32)
    width = right.shape[0]
    return both[:, :width] + both[:, width:]


def face(conduct, earlier, fin_factor):
    return 2.0 * conduct * earlier / (conduct + earlier) * fin_factor


def conductivity(material, k_ref):
    total = jnp.zeros(material.shape, F32)
    for code in range(k_ref.shape[0]):
        total = total + jnp.where(material == code, k_ref[code], 0.0)
    return total


def fin_factor(fin):
    return 0.9 + 0.1 * fin.astype(F32)


def eye_mask(size):
    return lax.broadcasted_iota(jnp.int32, (size, size), 0) == lax.broadcasted_iota(
        jnp.int32, (size, size), 1
    )


def times(matrix, row, eye):
    column = jnp.sum(matrix * row, axis=1, keepdims=True)
    return jnp.sum(jnp.where(eye, column, 0.0), axis=0, keepdims=True)


def times_t(matrix, row, eye):
    column = jnp.sum(jnp.where(eye, row, 0.0), axis=1, keepdims=True)
    return jnp.sum(matrix * column, axis=0, keepdims=True)


def halves(cells):
    shape = (cells // 2, cells)
    return lax.broadcasted_iota(jnp.int32, shape, 0), lax.broadcasted_iota(jnp.int32, shape, 1)


def pack(square):
    middle = square.shape[0] // 2
    row, lane = halves(square.shape[1])
    top, bottom = square[:middle], pltpu.roll(square[middle:], middle, 1)
    return jnp.where(
        (lane >= middle) | (lane < row), top, jnp.where(lane == row, 0.5 * top, bottom)
    )


def unpack(packed, half_diagonal, roll):
    middle, cells = packed.shape
    row, lane = halves(cells)
    top = jnp.where((lane >= middle) | (lane <= row), packed, 0.0)
    bottom = jnp.where(lane - middle > row, roll(packed, middle, 1), 0.0)
    bottom = jnp.where(lane - middle == row, half_diagonal, bottom)
    return jnp.concatenate([top, bottom], axis=0)


def stack_rows(rows, cells):
    at = lax.broadcasted_iota(jnp.int32, (ROWS, cells), 0)
    out = jnp.zeros((ROWS, cells), F32)
    for place, row in enumerate(rows):
        out = jnp.where(at == place, jnp.broadcast_to(row, (ROWS, cells)), out)
    return out


def products(wide, source, faces, g_of, out_ref, ends):
    cells = wide[0].shape[1]
    tiles = range(len(wide))
    total = list(wide)
    for i in range(1, len(source)):
        for j in tiles:
            scaled = wide[j] * faces[i][j : j + 1]
            sh, sl = split(scaled[:cells])
            vh, vl = split(scaled[cells:] + stack_rows([source[i][j : j + 1]], cells))
            gh, gl = split(g_of(i, j))
            zero = jnp.zeros_like(gl)
            both = jnp.dot(
                jnp.concatenate([jnp.concatenate([sh, sl], axis=1), jnp.concatenate([vh, vl], axis=1)], axis=0),
                jnp.concatenate([jnp.concatenate([gh, gl], axis=1), jnp.concatenate([gh, zero], axis=1)], axis=0),
                preferred_element_type=F32,
            )
            wide[j] = both[:, :cells] + both[:, cells:]
            wh, wl = split(wide[j])
            both = lax.dot_general(
                jnp.concatenate([wh, wl], axis=1),
                jnp.concatenate([jnp.concatenate([sh, sh], axis=1), jnp.concatenate([sl, zero], axis=1)], axis=0),
                (((1,), (1,)), ((), ())),
                preferred_element_type=F32,
            )
            total[j] = total[j] + (both[:, :cells] + both[:, cells:])
    for j in tiles:
        out_ref[j, 0:cells] = wide[j][:cells]
        out_ref[j, cells : 2 * cells] = total[j][:cells]
        out_ref[j, 2 * cells :] = stack_rows(
            [wide[j][cells : cells + 1], total[j][cells : cells + 1]] + [end[j : j + 1] for end in ends], cells
        )


def first_kernel(k_hbm, mat_hbm, fin_hbm, res_hbm, g_hbm, out_ref, coef_ref, g_ref, k_ref, ints, sems):
    blocks, tiles, cells = res_hbm.shape
    half = tiles // 2
    lower = lax.axis_index(AXIS) % 2 == 1
    base = jnp.where(lower, 0, half)
    small = [
        pltpu.make_async_copy(k_hbm, k_ref, sems.at[0]),
        pltpu.make_async_copy(mat_hbm, ints.at[0], sems.at[1]),
        pltpu.make_async_copy(fin_hbm, ints.at[1], sems.at[2]),
        pltpu.make_async_copy(res_hbm, coef_ref.at[pl.ds(0, blocks)], sems.at[3]),
    ]
    places = [base + j for j in range(half)] + [half - base + j for j in range(half)]
    large = [
        pltpu.make_async_copy(g_hbm.at[:, at], g_ref.at[:, at], sems.at[4 + n])
        for n, at in enumerate(places)
    ]
    for copy in small + large:
        copy.start()
    for copy in small:
        copy.wait()
    conduct = [conductivity(ints[0, i], k_ref) for i in range(blocks)]
    factor = [fin_factor(ints[1, i]) for i in range(blocks)]
    faces = [None] + [face(conduct[i], conduct[i - 1], factor[i]) for i in range(1, blocks)]
    ends = [conduct[0], conduct[-1], factor[0]]
    for n, row in enumerate(faces[1:] + ends):
        coef_ref[blocks + n] = row

    def pick(x):
        return jnp.where(lower, x[:half], x[half:])

    source = [pick(coef_ref[i]) for i in range(blocks)]
    eye = eye_mask(cells)
    wide = []
    for j in range(half):
        large[j].wait()
        g0 = g_ref[0, base + j]
        wide.append(jnp.concatenate([g0, stack_rows([times(g0, source[0][j : j + 1], eye)], cells)], axis=0))
    products(
        wide, source, [None] + [pick(f) for f in faces[1:]], lambda i, j: g_ref[i, base + j], out_ref,
        [pick(end) for end in ends],
    )
    for copy in large[half:]:
        copy.wait()


def second_kernel(coef_ref, g_ref, out_ref):
    blocks, tiles, cells = g_ref.shape[:3]
    half = tiles // 2
    upper = lax.axis_index(AXIS) % 2 == 1
    base = jnp.where(upper, half, 0)

    def pick(n):
        return jnp.where(upper, coef_ref[n, half:], coef_ref[n, :half])

    source = [pick(i) for i in range(blocks)]
    faces = [None] + [pick(blocks + i) for i in range(blocks - 1)]
    eye = eye_mask(cells)
    wide = []
    for j in range(half):
        g0 = g_ref[0, base + j]
        wide.append(jnp.concatenate([g0, stack_rows([times(g0, source[0][j : j + 1], eye)], cells)], axis=0))
    products(
        wide, source, faces, lambda i, j: g_ref[i, base + j], out_ref,
        [pick(2 * blocks - 1 + n) for n in range(3)],
    )


def response_kernel(coef_ref, keep_ref, got_ref, give_ref, gain_ref, g_ref, out_ref, const_ref):
    blocks, tiles, cells = g_ref.shape[:3]
    half = tiles // 2
    is_second = lax.axis_index(AXIS) % 2 == 1
    base = jnp.where(is_second, half, 0)
    eye = jnp.where(eye_mask(cells), 1.0, 0.0)

    def reorder(x):
        return jnp.where(is_second, jnp.concatenate([x[half:], x[:half]], axis=0), x)

    source = [reorder(coef_ref[i]) for i in range(blocks)]
    faces = [None] + [reorder(coef_ref[blocks + i]) for i in range(blocks - 1)]
    nothing = jnp.zeros((cells, cells), F32)
    for group in range(2):
        own_ref, other_ref = (keep_ref, got_ref) if group == 0 else (give_ref, gain_ref)
        start = base if group == 0 else half - base
        lead, tail, values = {}, {}, {}
        for j in range(half):
            own, other = own_ref[j], other_ref[j]
            first = jnp.where(is_second, other, own)
            last = jnp.where(is_second, own, other)
            va, vb = first[2 * cells :], last[2 * cells :]
            between = face(vb[2:3], va[3:4], vb[4:5])
            scaled = jnp.concatenate([first[:cells], stack_rows([va[0:1]], cells)], axis=0) * between
            back = mul(scaled, last[cells : 2 * cells])
            back_const = back[cells:] + stack_rows([vb[1:2]], cells)
            tail[j] = jnp.concatenate(
                [
                    jnp.where(is_second, 0.0, back[:cells] * between),
                    jnp.where(is_second, eye, last[:cells].T * between),
                    jnp.where(is_second, 0.0, back_const * between),
                ],
                axis=0,
            )
            lead[j] = jnp.concatenate(
                [
                    jnp.where(is_second, scaled[:cells], eye),
                    jnp.where(is_second, scaled[cells:], 0.0)
                    + stack_rows([source[0][group * half + j : group * half + j + 1]], cells),
                ],
                axis=0,
            )
        for i in range(blocks):
            for j in range(half):
                values[i, j] = mul(lead[j], g_ref[i, start + j])
                if i < blocks - 1:
                    at = group * half + j
                    scaled = values[i, j] * faces[i + 1][at : at + 1]
                    below = scaled[cells:] + stack_rows([source[i + 1][at : at + 1]], cells)
                    lead[j] = jnp.concatenate([scaled[:cells], below], axis=0)
        for i in reversed(range(blocks)):
            for j in range(half):
                moved = mul(tail[j], g_ref[i, start + j])
                add = jnp.concatenate([values[i, j][:cells], nothing, values[i, j][cells:]], axis=0)
                solved = moved + add
                out_ref[i, start + j] = solved[: 2 * cells]
                const_ref[i, start + j] = solved[2 * cells :]
                if i:
                    at = group * half + j
                    tail[j] = solved * faces[i][at : at + 1]


def merge_kernel(keep_ref, got_ref, *out_refs):
    half, height, cells = keep_ref.shape
    here = lax.axis_index(AXIS)
    is_second = here % 2 == 1
    chip = (here % (2 * half)) // 2
    eye = eye_mask(cells)
    for d in range(half):
        tile = chip ^ d
        keep, got = keep_ref[tile], got_ref[tile]
        first = jnp.where(is_second, got, keep)
        second = jnp.where(is_second, keep, got)
        va, vb = first[2 * cells :], second[2 * cells :]
        between = face(vb[2:3], va[3:4], vb[4:5])
        scaled = jnp.concatenate([first[:cells], stack_rows([va[0:1]], cells)], axis=0) * between
        moved = mul(scaled, second[:cells])
        squared = mul(scaled, second[cells : 2 * cells])
        lower = squared[cells:] + stack_rows([vb[1:2]], cells)
        squared = jnp.concatenate([squared[:cells], lower], axis=0)
        total = mul_t(squared, scaled[:cells])
        square = first[cells : 2 * cells] + total[:cells]
        out_ref = out_refs[d]
        out_ref[0:cells] = moved[:cells]
        out_ref[cells:-ROWS] = pack(square)
        out_ref[-ROWS:] = stack_rows(
            [
                moved[cells : cells + 1] + vb[0:1],
                total[cells : cells + 1] + va[1:2],
                va[2:3],
                vb[3:4],
                va[4:5],
                0.5 * jnp.sum(jnp.where(eye, square, 0.0), axis=0, keepdims=True),
            ],
            cells,
        )


def chain_kernel(with_edge, *refs):
    refs, nodes = refs[1:-1], refs[-1]
    if with_edge:
        edge_ref, refs = refs[0], refs[1:]
    count, height, cells = nodes.shape
    refs, out_refs, ends = refs[count - 1 :: -1], refs[count:-1], refs[-1]
    chip = (lax.axis_index(AXIS) % (2 * count)) // 2
    for d in range(count):
        nodes[chip ^ d] = refs[d][...]
    eye = eye_mask(cells)
    vectors = [nodes[k, height - ROWS :] for k in range(count)]
    squares = [None] + [
        unpack(nodes[k, cells : height - ROWS], vectors[k][5:6], pltpu.roll) for k in range(1, count)
    ]
    faces = [None] + [
        face(vectors[k][2:3], vectors[k - 1][3:4], vectors[k][4:5]) for k in range(1, count)
    ]
    entering, arriving = [None] * count, [None] * count
    leaving = vectors[0][0:1]
    if with_edge:
        entering[0], arriving[-1] = edge_ref[0:1], edge_ref[1:2]
        leaving = leaving + times_t(nodes[0, 0:cells], entering[0], eye)
    for k in range(1, count):
        entering[k] = faces[k] * leaving
        if k < count - 1:
            leaving = vectors[k][0:1] + times_t(nodes[k, 0:cells], entering[k], eye)
    heads = [None] + [
        vectors[k][1:2] + times(squares[k], entering[k], eye) + times_t(squares[k], entering[k], eye)
        for k in range(1, count)
    ]
    for k in reversed(range(1, count)):
        head = heads[k]
        if arriving[k] is not None:
            head = head + times(nodes[k, 0:cells], arriving[k], eye)
        arriving[k - 1] = faces[k] * head
    zero = jnp.zeros((1, cells), F32)
    for k in range(count):
        ends[k] = stack_rows(
            [zero if entering[k] is None else entering[k], zero if arriving[k] is None else arriving[k]],
            cells,
        )
    for d in range(count):
        out_refs[d][...] = ends[chip ^ d]


def order_kernel(*refs):
    out_ref = refs[-1]
    count = out_ref.shape[0]
    chip = (lax.axis_index(AXIS) % (2 * count)) // 2
    for d in range(count):
        out_ref[chip ^ d] = refs[count - 1 - d][...]


def finish_kernel(mine_ref, theirs_ref, phase_ref, out_ref, const_ref, corr_ref, step_ref, ends_ref):
    blocks, tiles, cells = corr_ref.shape
    half = tiles // 2
    is_second = lax.axis_index(AXIS) % 2 == 1
    ends_ref[:half] = jnp.where(is_second, theirs_ref[...], mine_ref[...])
    ends_ref[half:] = jnp.where(is_second, mine_ref[...], theirs_ref[...])
    eye = eye_mask(cells)
    for j in range(tiles):
        up = jnp.sum(jnp.where(eye, ends_ref[j, 0:1], 0.0), axis=1, keepdims=True)
        down = jnp.sum(jnp.where(eye, ends_ref[j, 1:2], 0.0), axis=1, keepdims=True)
        for i in range(blocks):
            both = out_ref[i, j, 0:cells] * up + out_ref[i, j, cells : 2 * cells] * down
            solved = const_ref[i, j, 0:1] + jnp.sum(both, axis=0, keepdims=True)
            corr_ref[i, j : j + 1] = solved
            step_ref[i, j : j + 1] = solved * (1.0 + 2.0 * phase_ref[i, j : j + 1].astype(F32))


VMEM = pl.BlockSpec(memory_space=pltpu.VMEM)
HBM = pl.BlockSpec(memory_space=pltpu.HBM)
LIMIT = pltpu.CompilerParams(vmem_limit_bytes=16 << 20)


def cost(flops, moved):
    return pl.CostEstimate(flops=flops, bytes_accessed=moved, transcendentals=0)


def send(x, distance):
    return lax.ppermute(x, AXIS, [(i, i ^ distance) for i in range(lax.axis_size(AXIS))])


def send_all(parts):
    arrived = {0: parts[0]}
    for d in reversed(range(1, len(parts))):
        arrived[d] = send(parts[d], 2 * d)
    return [arrived[d] for d in range(len(parts))]


def exact(left, right):
    return jnp.dot(left, right, precision=lax.Precision.HIGHEST)


def outer_edge(nodes, devices):
    cells = nodes[0].shape[-1]

    def parts(node):
        return node[:cells], node[cells : 2 * cells], node[2 * cells :]

    def widen(node):
        part = unpack(node[cells:-ROWS], node[-3:-2], jnp.roll)
        return jnp.concatenate([node[:cells], part + part.T, node[-ROWS:]], axis=0)

    def join(first, second):
        (ma, qa, va), (mb, qb, vb) = parts(first), parts(second)
        between = face(vb[2], va[3], vb[4])
        scaled, shift = ma * between, va[0] * between
        q = qa + exact(exact(scaled, qb), scaled.T)
        tail = exact(shift, mb) + vb[0]
        lead = va[1] + exact(scaled, exact(qb, shift) + vb[1])
        rest = jnp.zeros((ROWS - 5, cells), F32)
        rows = jnp.stack([tail, lead, va[2], vb[3], va[4]])
        return jnp.concatenate([exact(scaled, mb), q, rows, rest], axis=0)

    groups = lax.axis_size(AXIS) // devices
    whole = functools.reduce(join, [widen(nodes[k]) for k in range(nodes.shape[0])])
    members = [[g * devices + q for g in range(groups)] for q in range(devices)]
    every = lax.all_gather(whole, AXIS, axis=0, axis_index_groups=members)
    split_up = [parts(every[g]) for g in range(groups)]
    faces = [face(b[2][2], a[2][3], b[2][4]) for a, b in zip(split_up[:-1], split_up[1:])]
    entering = [jnp.zeros((cells,), F32)]
    for g in range(groups - 1):
        m, _, v = split_up[g]
        entering.append(faces[g] * (exact(entering[g], m) + v[0]))
    arriving = [jnp.zeros((cells,), F32)]
    for g in reversed(range(1, groups)):
        m, q, v = split_up[g]
        arriving.append(faces[g - 1] * (exact(m, arriving[-1]) + exact(q, entering[g]) + v[1]))
    arriving.reverse()
    own = lax.axis_index(AXIS) // devices
    both = jnp.stack([jnp.stack(entering)[own], jnp.stack(arriving)[own]])
    return jnp.concatenate([both, jnp.zeros((ROWS - 2, cells), F32)], axis=0)


def on_device(block_inverses, residual, material, fin_mask, phase_mask, k_table):
    blocks, tiles, cells = residual.shape
    half = tiles // 2
    height = 2 * cells + ROWS
    map_bytes = 4 * height * cells

    map_shape = (half, height, cells)
    work = cost(24 * half * blocks * cells**3, 8 * half * blocks * cells**2)
    given = [pltpu.with_memory_space_constraint(x, pltpu.HBM) for x in (k_table, material, fin_mask, residual, block_inverses)]
    give, coef, inverses = pl.pallas_call(
        first_kernel,
        out_shape=(
            pltpu.VMEM(map_shape, F32),
            pltpu.VMEM((2 * blocks + 2, tiles, cells), F32),
            pltpu.VMEM(block_inverses.shape, F32),
        ),
        in_specs=[HBM] * 5,
        out_specs=(VMEM,) * 3,
        scratch_shapes=[
            pltpu.SMEM(k_table.shape, F32),
            pltpu.VMEM((2, blocks, tiles, cells), jnp.int32),
            pltpu.SemaphoreType.DMA((4 + tiles,)),
        ],
        compiler_params=LIMIT,
        cost_estimate=work,
    )(*given)
    got = send(give, 1)
    keep = pl.pallas_call(
        second_kernel,
        out_shape=jax.ShapeDtypeStruct(map_shape, F32),
        in_specs=[VMEM, VMEM],
        out_specs=VMEM,
        compiler_params=LIMIT,
        cost_estimate=work,
    )(coef, inverses)
    gain = send(keep, 1)
    responses, constants = pl.pallas_call(
        response_kernel,
        out_shape=(
            jax.ShapeDtypeStruct((blocks, tiles, 2 * cells, cells), F32),
            jax.ShapeDtypeStruct((blocks, tiles, ROWS, cells), F32),
        ),
        in_specs=[VMEM] * 6,
        out_specs=(VMEM, VMEM),
        compiler_params=LIMIT,
        cost_estimate=cost(48 * tiles * blocks * cells**3, 16 * tiles * blocks * cells**2),
    )(coef, keep, got, give, gain, inverses)
    short = cells + cells // 2 + ROWS
    node = jax.ShapeDtypeStruct((short, cells), F32)
    joined = pl.pallas_call(
        merge_kernel,
        out_shape=(node,) * half,
        in_specs=[VMEM, VMEM],
        out_specs=(VMEM,) * half,
        compiler_params=LIMIT,
        cost_estimate=cost(24 * half * cells**3, 3 * half * map_bytes),
    )(keep, got)
    arrived = send_all(joined)
    grouped = lax.axis_size(AXIS) > tiles
    edge = []
    if grouped:
        chip = (lax.axis_index(AXIS) % tiles) // 2
        ordered = jnp.stack(arrived)[jnp.arange(half) ^ chip]
        edge = [outer_edge(ordered, tiles)]
    end = jax.ShapeDtypeStruct((ROWS, cells), F32)
    ends = pl.pallas_call(
        functools.partial(chain_kernel, grouped),
        out_shape=(end,) * half,
        in_specs=[pl.BlockSpec(memory_space=pl.ANY)] + [VMEM] * (half + len(edge)),
        out_specs=(VMEM,) * half,
        scratch_shapes=[pltpu.VMEM((half, ROWS, cells), F32), pltpu.VMEM((half, short, cells), F32)],
        compiler_params=LIMIT,
        cost_estimate=cost(8 * half * cells**2, half * map_bytes),
    )(constants, *edge, *arrived[::-1])
    ends = send_all(ends)
    mine = pl.pallas_call(
        order_kernel,
        out_shape=jax.ShapeDtypeStruct((half, ROWS, cells), F32),
        in_specs=[VMEM] * half,
        out_specs=VMEM,
        compiler_params=LIMIT,
        cost_estimate=cost(0, 8 * half * ROWS * cells),
    )(*ends[::-1])
    theirs = send(mine, 1)
    shape = jax.ShapeDtypeStruct((blocks, tiles, cells), F32)
    return pl.pallas_call(
        finish_kernel,
        out_shape=(shape, shape),
        in_specs=[VMEM] * 5,
        out_specs=(VMEM, VMEM),
        scratch_shapes=[pltpu.VMEM((tiles, ROWS, cells), F32)],
        compiler_params=LIMIT,
        cost_estimate=cost(4 * blocks * tiles * cells**2, 8 * blocks * tiles * cells**2),
    )(mine, theirs, phase_mask, responses, constants)


def solution(mesh):
    return jax.shard_map(
        on_device,
        mesh=mesh,
        in_specs=(
            P("gx", "pa", None, None),
            P("gx", "pa", None),
            P("gx", "pa", None),
            P("gx", "pa", None),
            P("gx", "pa", None),
            P(),
        ),
        out_specs=(P("gx", "pa", None), P("gx", "pa", None)),
        check_vma=False,
    )
```

```python
import functools

import jax
import jax.numpy as jnp
from jax import lax
from jax.experimental import pallas as pl
from jax.experimental.pallas import tpu as pltpu
from jax.sharding import PartitionSpec as P

BF16 = jnp.bfloat16
F32 = jnp.float32
ROWS = 8
AXIS = "gx"


def split(x):
    high = x.astype(BF16)
    return high, (x - high.astype(F32)).astype(BF16)


def mul(left, right):
    lh, ll = split(left)
    rh, rl = split(right)
    lhs = jnp.concatenate([lh, ll], axis=1)
    rhs = jnp.concatenate(
        [jnp.concatenate([rh, rl], axis=1), jnp.concatenate([rh, jnp.zeros_like(rl)], axis=1)], axis=0
    )
    both = jnp.dot(lhs, rhs, preferred_element_type=F32)
    width = right.shape[1]
    return both[:, :width] + both[:, width:]


def mul_t(left, right):
    lh, ll = split(left)
    rh, rl = split(right)
    lhs = jnp.concatenate([lh, ll], axis=1)
    rhs = jnp.concatenate(
        [jnp.concatenate([rh, rh], axis=1), jnp.concatenate([rl, jnp.zeros_like(rl)], axis=1)], axis=0
    )
    both = lax.dot_general(lhs, rhs, (((1,), (1,)), ((), ())), preferred_element_type=F32)
    width = right.shape[0]
    return both[:, :width] + both[:, width:]


def face(conduct, earlier, fin_factor):
    return 2.0 * conduct * earlier / (conduct + earlier) * fin_factor


def conductivity(material, k_ref):
    total = jnp.zeros(material.shape, F32)
    for code in range(k_ref.shape[0]):
        total = total + jnp.where(material == code, k_ref[code], 0.0)
    return total


def fin_factor(fin):
    return 0.9 + 0.1 * fin.astype(F32)


def eye_mask(size):
    return lax.broadcasted_iota(jnp.int32, (size, size), 0) == lax.broadcasted_iota(
        jnp.int32, (size, size), 1
    )


def times(matrix, row, eye):
    column = jnp.sum(matrix * row, axis=1, keepdims=True)
    return jnp.sum(jnp.where(eye, column, 0.0), axis=0, keepdims=True)


def times_t(matrix, row, eye):
    column = jnp.sum(jnp.where(eye, row, 0.0), axis=1, keepdims=True)
    return jnp.sum(matrix * column, axis=0, keepdims=True)


def halves(cells):
    shape = (cells // 2, cells)
    return lax.broadcasted_iota(jnp.int32, shape, 0), lax.broadcasted_iota(jnp.int32, shape, 1)


def pack(square):
    middle = square.shape[0] // 2
    row, lane = halves(square.shape[1])
    top, bottom = square[:middle], pltpu.roll(square[middle:], middle, 1)
    return jnp.where(
        (lane >= middle) | (lane < row), top, jnp.where(lane == row, 0.5 * top, bottom)
    )


def unpack(packed, half_diagonal, roll):
    middle, cells = packed.shape
    row, lane = halves(cells)
    top = jnp.where((lane >= middle) | (lane <= row), packed, 0.0)
    bottom = jnp.where(lane - middle > row, roll(packed, middle, 1), 0.0)
    bottom = jnp.where(lane - middle == row, half_diagonal, bottom)
    return jnp.concatenate([top, bottom], axis=0)


def stack_rows(rows, cells):
    at = lax.broadcasted_iota(jnp.int32, (ROWS, cells), 0)
    out = jnp.zeros((ROWS, cells), F32)
    for place, row in enumerate(rows):
        out = jnp.where(at == place, jnp.broadcast_to(row, (ROWS, cells)), out)
    return out


def products(wide, source, faces, g_of, out_ref, ends):
    cells = wide[0].shape[1]
    tiles = range(len(wide))
    total = list(wide)
    for i in range(1, len(source)):
        for j in tiles:
            scaled = wide[j] * faces[i][j : j + 1]
            sh, sl = split(scaled[:cells])
            vh, vl = split(scaled[cells:] + stack_rows([source[i][j : j + 1]], cells))
            gh, gl = split(g_of(i, j))
            zero = jnp.zeros_like(gl)
            both = jnp.dot(
                jnp.concatenate([jnp.concatenate([sh, sl], axis=1), jnp.concatenate([vh, vl], axis=1)], axis=0),
                jnp.concatenate([jnp.concatenate([gh, gl], axis=1), jnp.concatenate([gh, zero], axis=1)], axis=0),
                preferred_element_type=F32,
            )
            wide[j] = both[:, :cells] + both[:, cells:]
            wh, wl = split(wide[j])
            th, tl = split(scaled[:cells].T)
            both = jnp.dot(
                jnp.concatenate([wh, wl], axis=1),
                jnp.concatenate([jnp.concatenate([th, tl], axis=1), jnp.concatenate([th, zero], axis=1)], axis=0),
                preferred_element_type=F32,
            )
            total[j] = total[j] + (both[:, :cells] + both[:, cells:])
    for j in tiles:
        out_ref[j, 0:cells] = wide[j][:cells]
        out_ref[j, cells : 2 * cells] = total[j][:cells]
        out_ref[j, 2 * cells :] = stack_rows(
            [wide[j][cells : cells + 1], total[j][cells : cells + 1]] + [end[j : j + 1] for end in ends], cells
        )


def first_kernel(k_hbm, mat_hbm, fin_hbm, res_hbm, g_hbm, out_ref, coef_ref, g_ref, k_ref, ints, sems):
    blocks, tiles, cells = res_hbm.shape
    half = tiles // 2
    lower = lax.axis_index(AXIS) % 2 == 1
    base = jnp.where(lower, 0, half)
    small = [
        pltpu.make_async_copy(k_hbm, k_ref, sems.at[0]),
        pltpu.make_async_copy(mat_hbm, ints.at[0], sems.at[1]),
        pltpu.make_async_copy(fin_hbm, ints.at[1], sems.at[2]),
        pltpu.make_async_copy(res_hbm, coef_ref.at[pl.ds(0, blocks)], sems.at[3]),
    ]
    places = [base + j for j in range(half)] + [half - base + j for j in range(half)]
    large = [
        pltpu.make_async_copy(g_hbm.at[:, at], g_ref.at[:, at], sems.at[4 + n])
        for n, at in enumerate(places)
    ]
    for copy in small + large:
        copy.start()
    for copy in small:
        copy.wait()
    conduct = [conductivity(ints[0, i], k_ref) for i in range(blocks)]
    factor = [fin_factor(ints[1, i]) for i in range(blocks)]
    faces = [None] + [face(conduct[i], conduct[i - 1], factor[i]) for i in range(1, blocks)]
    ends = [conduct[0], conduct[-1], factor[0]]
    for n, row in enumerate(faces[1:] + ends):
        coef_ref[blocks + n] = row

    def pick(x):
        return jnp.where(lower, x[:half], x[half:])

    source = [pick(coef_ref[i]) for i in range(blocks)]
    eye = eye_mask(cells)
    wide = []
    for j in range(half):
        large[j].wait()
        g0 = g_ref[0, base + j]
        wide.append(jnp.concatenate([g0, stack_rows([times(g0, source[0][j : j + 1], eye)], cells)], axis=0))
    products(
        wide, source, [None] + [pick(f) for f in faces[1:]], lambda i, j: g_ref[i, base + j], out_ref,
        [pick(end) for end in ends],
    )
    for copy in large[half:]:
        copy.wait()


def second_kernel(coef_ref, g_ref, out_ref):
    blocks, tiles, cells = g_ref.shape[:3]
    half = tiles // 2
    upper = lax.axis_index(AXIS) % 2 == 1
    base = jnp.where(upper, half, 0)

    def pick(n):
        return jnp.where(upper, coef_ref[n, half:], coef_ref[n, :half])

    source = [pick(i) for i in range(blocks)]
    faces = [None] + [pick(blocks + i) for i in range(blocks - 1)]
    eye = eye_mask(cells)
    wide = []
    for j in range(half):
        g0 = g_ref[0, base + j]
        wide.append(jnp.concatenate([g0, stack_rows([times(g0, source[0][j : j + 1], eye)], cells)], axis=0))
    products(
        wide, source, faces, lambda i, j: g_ref[i, base + j], out_ref,
        [pick(2 * blocks - 1 + n) for n in range(3)],
    )


def response_kernel(coef_ref, keep_ref, got_ref, give_ref, gain_ref, g_ref, out_ref, const_ref):
    blocks, tiles, cells = g_ref.shape[:3]
    half = tiles // 2
    is_second = lax.axis_index(AXIS) % 2 == 1
    base = jnp.where(is_second, half, 0)
    eye = jnp.where(eye_mask(cells), 1.0, 0.0)

    def reorder(x):
        return jnp.where(is_second, jnp.concatenate([x[half:], x[:half]], axis=0), x)

    source = [reorder(coef_ref[i]) for i in range(blocks)]
    faces = [None] + [reorder(coef_ref[blocks + i]) for i in range(blocks - 1)]
    nothing = jnp.zeros((cells, cells), F32)
    for group in range(2):
        own_ref, other_ref = (keep_ref, got_ref) if group == 0 else (give_ref, gain_ref)
        start = base if group == 0 else half - base
        lead, tail, values = {}, {}, {}
        for j in range(half):
            own, other = own_ref[j], other_ref[j]
            first = jnp.where(is_second, other, own)
            last = jnp.where(is_second, own, other)
            va, vb = first[2 * cells :], last[2 * cells :]
            between = face(vb[2:3], va[3:4], vb[4:5])
            scaled = jnp.concatenate([first[:cells], stack_rows([va[0:1]], cells)], axis=0) * between
            back = mul(scaled, last[cells : 2 * cells])
            back_const = back[cells:] + stack_rows([vb[1:2]], cells)
            tail[j] = jnp.concatenate(
                [
                    jnp.where(is_second, 0.0, back[:cells] * between),
                    jnp.where(is_second, eye, last[:cells].T * between),
                    jnp.where(is_second, 0.0, back_const * between),
                ],
                axis=0,
            )
            lead[j] = jnp.concatenate(
                [
                    jnp.where(is_second, scaled[:cells], eye),
                    jnp.where(is_second, scaled[cells:], 0.0)
                    + stack_rows([source[0][group * half + j : group * half + j + 1]], cells),
                ],
                axis=0,
            )
        for i in range(blocks):
            for j in range(half):
                values[i, j] = mul(lead[j], g_ref[i, start + j])
                if i < blocks - 1:
                    at = group * half + j
                    scaled = values[i, j] * faces[i + 1][at : at + 1]
                    below = scaled[cells:] + stack_rows([source[i + 1][at : at + 1]], cells)
                    lead[j] = jnp.concatenate([scaled[:cells], below], axis=0)
        for i in reversed(range(blocks)):
            for j in range(half):
                moved = mul(tail[j], g_ref[i, start + j])
                add = jnp.concatenate([values[i, j][:cells], nothing, values[i, j][cells:]], axis=0)
                solved = moved + add
                out_ref[i, start + j] = solved[: 2 * cells]
                const_ref[i, start + j] = solved[2 * cells :]
                if i:
                    at = group * half + j
                    tail[j] = solved * faces[i][at : at + 1]


def merge_kernel(keep_ref, got_ref, *out_refs):
    half, height, cells = keep_ref.shape
    here = lax.axis_index(AXIS)
    is_second = here % 2 == 1
    chip = (here % (2 * half)) // 2
    eye = eye_mask(cells)
    order = list(reversed(range(half)))
    first, last, scaled, between, moved, squared = {}, {}, {}, {}, {}, {}
    for d in order:
        keep, got = keep_ref[chip ^ d], got_ref[chip ^ d]
        first[d] = jnp.where(is_second, got, keep)
        last[d] = jnp.where(is_second, keep, got)
        va, vb = first[d][2 * cells :], last[d][2 * cells :]
        between = face(vb[2:3], va[3:4], vb[4:5])
        scaled[d] = jnp.concatenate([first[d][:cells], stack_rows([va[0:1]], cells)], axis=0) * between
    for d in order:
        moved[d] = mul(scaled[d], last[d][:cells])
    for d in order:
        squared[d] = mul(scaled[d], last[d][cells : 2 * cells])
        lower = squared[d][cells:] + stack_rows([last[d][2 * cells + 1 : 2 * cells + 2]], cells)
        squared[d] = jnp.concatenate([squared[d][:cells], lower], axis=0)
    for d in order:
        total = mul(squared[d], scaled[d][:cells].T)
        va, vb = first[d][2 * cells :], last[d][2 * cells :]
        square = first[d][cells : 2 * cells] + total[:cells]
        out_ref = out_refs[d]
        out_ref[0:cells] = moved[d][:cells]
        out_ref[cells:-ROWS] = pack(square)
        out_ref[-ROWS:] = stack_rows(
            [
                moved[d][cells : cells + 1] + vb[0:1],
                total[cells : cells + 1] + va[1:2],
                va[2:3],
                vb[3:4],
                va[4:5],
                0.5 * jnp.sum(jnp.where(eye, square, 0.0), axis=0, keepdims=True),
            ],
            cells,
        )


def chain_kernel(with_edge, *refs):
    refs, nodes = refs[1:-1], refs[-1]
    if with_edge:
        edge_ref, refs = refs[0], refs[1:]
    count, height, cells = nodes.shape
    refs, out_refs, ends = refs[count - 1 :: -1], refs[count:-1], refs[-1]
    chip = (lax.axis_index(AXIS) % (2 * count)) // 2
    for d in range(count):
        nodes[chip ^ d] = refs[d][...]
    eye = eye_mask(cells)
    vectors = [nodes[k, height - ROWS :] for k in range(count)]
    squares = [None] + [
        unpack(nodes[k, cells : height - ROWS], vectors[k][5:6], pltpu.roll) for k in range(1, count)
    ]
    faces = [None] + [
        face(vectors[k][2:3], vectors[k - 1][3:4], vectors[k][4:5]) for k in range(1, count)
    ]
    entering, arriving = [None] * count, [None] * count
    leaving = vectors[0][0:1]
    if with_edge:
        entering[0], arriving[-1] = edge_ref[0:1], edge_ref[1:2]
        leaving = leaving + times_t(nodes[0, 0:cells], entering[0], eye)
    for k in range(1, count):
        entering[k] = faces[k] * leaving
        if k < count - 1:
            leaving = vectors[k][0:1] + times_t(nodes[k, 0:cells], entering[k], eye)
    heads = [None] + [
        vectors[k][1:2] + times(squares[k], entering[k], eye) + times_t(squares[k], entering[k], eye)
        for k in range(1, count)
    ]
    for k in reversed(range(1, count)):
        head = heads[k]
        if arriving[k] is not None:
            head = head + times(nodes[k, 0:cells], arriving[k], eye)
        arriving[k - 1] = faces[k] * head
    zero = jnp.zeros((1, cells), F32)
    for k in range(count):
        ends[k] = stack_rows(
            [zero if entering[k] is None else entering[k], zero if arriving[k] is None else arriving[k]],
            cells,
        )
    for d in range(count):
        out_refs[d][...] = ends[chip ^ d]


def order_kernel(*refs):
    out_ref = refs[-1]
    count = out_ref.shape[0]
    chip = (lax.axis_index(AXIS) % (2 * count)) // 2
    for d in range(count):
        out_ref[chip ^ d] = refs[count - 1 - d][...]


def finish_kernel(mine_ref, theirs_ref, phase_ref, out_ref, const_ref, corr_ref, step_ref, ends_ref):
    blocks, tiles, cells = corr_ref.shape
    half = tiles // 2
    is_second = lax.axis_index(AXIS) % 2 == 1
    ends_ref[:half] = jnp.where(is_second, theirs_ref[...], mine_ref[...])
    ends_ref[half:] = jnp.where(is_second, mine_ref[...], theirs_ref[...])
    eye = eye_mask(cells)
    for j in range(tiles):
        up = jnp.sum(jnp.where(eye, ends_ref[j, 0:1], 0.0), axis=1, keepdims=True)
        down = jnp.sum(jnp.where(eye, ends_ref[j, 1:2], 0.0), axis=1, keepdims=True)
        for i in range(blocks):
            both = out_ref[i, j, 0:cells] * up + out_ref[i, j, cells : 2 * cells] * down
            solved = const_ref[i, j, 0:1] + jnp.sum(both, axis=0, keepdims=True)
            corr_ref[i, j : j + 1] = solved
            step_ref[i, j : j + 1] = solved * (1.0 + 2.0 * phase_ref[i, j : j + 1].astype(F32))


VMEM = pl.BlockSpec(memory_space=pltpu.VMEM)
HBM = pl.BlockSpec(memory_space=pltpu.HBM)
LIMIT = pltpu.CompilerParams(vmem_limit_bytes=16 << 20)


def cost(flops, moved):
    return pl.CostEstimate(flops=flops, bytes_accessed=moved, transcendentals=0)


def send(x, distance):
    return lax.ppermute(x, AXIS, [(i, i ^ distance) for i in range(lax.axis_size(AXIS))])


def send_all(parts):
    arrived = {0: parts[0]}
    for d in reversed(range(1, len(parts))):
        arrived[d] = send(parts[d], 2 * d)
    return [arrived[d] for d in range(len(parts))]


def exact(left, right):
    return jnp.dot(left, right, precision=lax.Precision.HIGHEST)


def outer_edge(nodes, devices):
    cells = nodes[0].shape[-1]

    def parts(node):
        return node[:cells], node[cells : 2 * cells], node[2 * cells :]

    def widen(node):
        part = unpack(node[cells:-ROWS], node[-3:-2], jnp.roll)
        return jnp.concatenate([node[:cells], part + part.T, node[-ROWS:]], axis=0)

    def join(first, second):
        (ma, qa, va), (mb, qb, vb) = parts(first), parts(second)
        between = face(vb[2], va[3], vb[4])
        scaled, shift = ma * between, va[0] * between
        q = qa + exact(exact(scaled, qb), scaled.T)
        tail = exact(shift, mb) + vb[0]
        lead = va[1] + exact(scaled, exact(qb, shift) + vb[1])
        rest = jnp.zeros((ROWS - 5, cells), F32)
        rows = jnp.stack([tail, lead, va[2], vb[3], va[4]])
        return jnp.concatenate([exact(scaled, mb), q, rows, rest], axis=0)

    groups = lax.axis_size(AXIS) // devices
    whole = functools.reduce(join, [widen(nodes[k]) for k in range(nodes.shape[0])])
    members = [[g * devices + q for g in range(groups)] for q in range(devices)]
    every = lax.all_gather(whole, AXIS, axis=0, axis_index_groups=members)
    split_up = [parts(every[g]) for g in range(groups)]
    faces = [face(b[2][2], a[2][3], b[2][4]) for a, b in zip(split_up[:-1], split_up[1:])]
    entering = [jnp.zeros((cells,), F32)]
    for g in range(groups - 1):
        m, _, v = split_up[g]
        entering.append(faces[g] * (exact(entering[g], m) + v[0]))
    arriving = [jnp.zeros((cells,), F32)]
    for g in reversed(range(1, groups)):
        m, q, v = split_up[g]
        arriving.append(faces[g - 1] * (exact(m, arriving[-1]) + exact(q, entering[g]) + v[1]))
    arriving.reverse()
    own = lax.axis_index(AXIS) // devices
    both = jnp.stack([jnp.stack(entering)[own], jnp.stack(arriving)[own]])
    return jnp.concatenate([both, jnp.zeros((ROWS - 2, cells), F32)], axis=0)


def on_device(block_inverses, residual, material, fin_mask, phase_mask, k_table):
    blocks, tiles, cells = residual.shape
    half = tiles // 2
    height = 2 * cells + ROWS
    map_bytes = 4 * height * cells

    map_shape = (half, height, cells)
    work = cost(24 * half * blocks * cells**3, 8 * half * blocks * cells**2)
    given = [pltpu.with_memory_space_constraint(x, pltpu.HBM) for x in (k_table, material, fin_mask, residual, block_inverses)]
    give, coef, inverses = pl.pallas_call(
        first_kernel,
        out_shape=(
            pltpu.VMEM(map_shape, F32),
            pltpu.VMEM((2 * blocks + 2, tiles, cells), F32),
            pltpu.VMEM(block_inverses.shape, F32),
        ),
        in_specs=[HBM] * 5,
        out_specs=(VMEM,) * 3,
        scratch_shapes=[
            pltpu.SMEM(k_table.shape, F32),
            pltpu.VMEM((2, blocks, tiles, cells), jnp.int32),
            pltpu.SemaphoreType.DMA((4 + tiles,)),
        ],
        compiler_params=LIMIT,
        cost_estimate=work,
    )(*given)
    got = send(give, 1)
    keep = pl.pallas_call(
        second_kernel,
        out_shape=jax.ShapeDtypeStruct(map_shape, F32),
        in_specs=[VMEM, VMEM],
        out_specs=VMEM,
        compiler_params=LIMIT,
        cost_estimate=work,
    )(coef, inverses)
    gain = send(keep, 1)
    responses, constants = pl.pallas_call(
        response_kernel,
        out_shape=(
            jax.ShapeDtypeStruct((blocks, tiles, 2 * cells, cells), F32),
            jax.ShapeDtypeStruct((blocks, tiles, ROWS, cells), F32),
        ),
        in_specs=[VMEM] * 6,
        out_specs=(VMEM, VMEM),
        compiler_params=LIMIT,
        cost_estimate=cost(48 * tiles * blocks * cells**3, 16 * tiles * blocks * cells**2),
    )(coef, keep, got, give, gain, inverses)
    short = cells + cells // 2 + ROWS
    node = jax.ShapeDtypeStruct((short, cells), F32)
    joined = pl.pallas_call(
        merge_kernel,
        out_shape=(node,) * half,
        in_specs=[VMEM, VMEM],
        out_specs=(VMEM,) * half,
        compiler_params=LIMIT,
        cost_estimate=cost(24 * half * cells**3, 3 * half * map_bytes),
    )(keep, got)
    arrived = send_all(joined)
    grouped = lax.axis_size(AXIS) > tiles
    edge = []
    if grouped:
        chip = (lax.axis_index(AXIS) % tiles) // 2
        ordered = jnp.stack(arrived)[jnp.arange(half) ^ chip]
        edge = [outer_edge(ordered, tiles)]
    end = jax.ShapeDtypeStruct((ROWS, cells), F32)
    ends = pl.pallas_call(
        functools.partial(chain_kernel, grouped),
        out_shape=(end,) * half,
        in_specs=[pl.BlockSpec(memory_space=pl.ANY)] + [VMEM] * (half + len(edge)),
        out_specs=(VMEM,) * half,
        scratch_shapes=[pltpu.VMEM((half, ROWS, cells), F32), pltpu.VMEM((half, short, cells), F32)],
        compiler_params=LIMIT,
        cost_estimate=cost(8 * half * cells**2, half * map_bytes),
    )(constants, *edge, *arrived[::-1])
    ends = send_all(ends)
    mine = pl.pallas_call(
        order_kernel,
        out_shape=jax.ShapeDtypeStruct((half, ROWS, cells), F32),
        in_specs=[VMEM] * half,
        out_specs=VMEM,
        compiler_params=LIMIT,
        cost_estimate=cost(0, 8 * half * ROWS * cells),
    )(*ends[::-1])
    theirs = send(mine, 1)
    shape = jax.ShapeDtypeStruct((blocks, tiles, cells), F32)
    return pl.pallas_call(
        finish_kernel,
        out_shape=(shape, shape),
        in_specs=[VMEM] * 5,
        out_specs=(VMEM, VMEM),
        scratch_shapes=[pltpu.VMEM((tiles, ROWS, cells), F32)],
        compiler_params=LIMIT,
        cost_estimate=cost(4 * blocks * tiles * cells**2, 8 * blocks * tiles * cells**2),
    )(mine, theirs, phase_mask, responses, constants)


def solution(mesh):
    return jax.shard_map(
        on_device,
        mesh=mesh,
        in_specs=(
            P("gx", "pa", None, None),
            P("gx", "pa", None),
            P("gx", "pa", None),
            P("gx", "pa", None),
            P("gx", "pa", None),
            P(),
        ),
        out_specs=(P("gx", "pa", None), P("gx", "pa", None)),
        check_vma=False,
    )
```

```python
import functools

import jax
import jax.numpy as jnp
from jax import lax
from jax.experimental import pallas as pl
from jax.experimental.pallas import tpu as pltpu
from jax.sharding import PartitionSpec as P

BF16 = jnp.bfloat16
F32 = jnp.float32
ROWS = 8
AXIS = "gx"


def split(x):
    high = x.astype(BF16)
    return high, (x - high.astype(F32)).astype(BF16)


def mul(left, right):
    lh, ll = split(left)
    rh, rl = split(right)
    lhs = jnp.concatenate([lh, ll], axis=1)
    rhs = jnp.concatenate(
        [jnp.concatenate([rh, rl], axis=1), jnp.concatenate([rh, jnp.zeros_like(rl)], axis=1)], axis=0
    )
    both = jnp.dot(lhs, rhs, preferred_element_type=F32)
    width = right.shape[1]
    return both[:, :width] + both[:, width:]


def mul_t(left, right):
    lh, ll = split(left)
    rh, rl = split(right)
    lhs = jnp.concatenate([lh, ll], axis=1)
    rhs = jnp.concatenate(
        [jnp.concatenate([rh, rh], axis=1), jnp.concatenate([rl, jnp.zeros_like(rl)], axis=1)], axis=0
    )
    both = lax.dot_general(lhs, rhs, (((1,), (1,)), ((), ())), preferred_element_type=F32)
    width = right.shape[0]
    return both[:, :width] + both[:, width:]


def face(conduct, earlier, fin_factor):
    return 2.0 * conduct * earlier / (conduct + earlier) * fin_factor


def conductivity(material, k_ref):
    total = jnp.zeros(material.shape, F32)
    for code in range(k_ref.shape[0]):
        total = total + jnp.where(material == code, k_ref[code], 0.0)
    return total


def fin_factor(fin):
    return 0.9 + 0.1 * fin.astype(F32)


def eye_mask(size):
    return lax.broadcasted_iota(jnp.int32, (size, size), 0) == lax.broadcasted_iota(
        jnp.int32, (size, size), 1
    )


def times(matrix, row, eye):
    column = jnp.sum(matrix * row, axis=1, keepdims=True)
    return jnp.sum(jnp.where(eye, column, 0.0), axis=0, keepdims=True)


def times_t(matrix, row, eye):
    column = jnp.sum(jnp.where(eye, row, 0.0), axis=1, keepdims=True)
    return jnp.sum(matrix * column, axis=0, keepdims=True)


def halves(cells):
    shape = (cells // 2, cells)
    return lax.broadcasted_iota(jnp.int32, shape, 0), lax.broadcasted_iota(jnp.int32, shape, 1)


def pack(square):
    middle = square.shape[0] // 2
    row, lane = halves(square.shape[1])
    top, bottom = square[:middle], pltpu.roll(square[middle:], middle, 1)
    return jnp.where(
        (lane >= middle) | (lane < row), top, jnp.where(lane == row, 0.5 * top, bottom)
    )


def unpack(packed, half_diagonal, roll):
    middle, cells = packed.shape
    row, lane = halves(cells)
    top = jnp.where((lane >= middle) | (lane <= row), packed, 0.0)
    bottom = jnp.where(lane - middle > row, roll(packed, middle, 1), 0.0)
    bottom = jnp.where(lane - middle == row, half_diagonal, bottom)
    return jnp.concatenate([top, bottom], axis=0)


def stack_rows(rows, cells):
    at = lax.broadcasted_iota(jnp.int32, (ROWS, cells), 0)
    out = jnp.zeros((ROWS, cells), F32)
    for place, row in enumerate(rows):
        out = jnp.where(at == place, jnp.broadcast_to(row, (ROWS, cells)), out)
    return out


def products(wide, source, faces, g_of, out_ref, ends):
    cells = wide[0].shape[1]
    tiles = range(len(wide))
    total = list(wide)
    for i in range(1, len(source)):
        for j in tiles:
            scaled = wide[j] * faces[i][j : j + 1]
            sh, sl = split(scaled[:cells])
            vh, vl = split(scaled[cells:] + stack_rows([source[i][j : j + 1]], cells))
            gh, gl = split(g_of(i, j))
            zero = jnp.zeros_like(gl)
            both = jnp.dot(
                jnp.concatenate([jnp.concatenate([sh, sl], axis=1), jnp.concatenate([vh, vl], axis=1)], axis=0),
                jnp.concatenate([jnp.concatenate([gh, gl], axis=1), jnp.concatenate([gh, zero], axis=1)], axis=0),
                preferred_element_type=F32,
            )
            wide[j] = both[:, :cells] + both[:, cells:]
            wh, wl = split(wide[j])
            th, tl = split(scaled[:cells].T)
            both = jnp.dot(
                jnp.concatenate([wh, wl], axis=1),
                jnp.concatenate([jnp.concatenate([th, tl], axis=1), jnp.concatenate([th, zero], axis=1)], axis=0),
                preferred_element_type=F32,
            )
            total[j] = total[j] + (both[:, :cells] + both[:, cells:])
    for j in tiles:
        out_ref[j, 0:cells] = wide[j][:cells]
        out_ref[j, cells : 2 * cells] = total[j][:cells]
        out_ref[j, 2 * cells :] = stack_rows(
            [wide[j][cells : cells + 1], total[j][cells : cells + 1]] + [end[j : j + 1] for end in ends], cells
        )


def first_kernel(k_hbm, mat_hbm, fin_hbm, res_hbm, g_hbm, out_ref, coef_ref, g_ref, k_ref, ints, sems):
    blocks, tiles, cells = res_hbm.shape
    half = tiles // 2
    lower = lax.axis_index(AXIS) % 2 == 1
    base = jnp.where(lower, 0, half)
    small = [
        pltpu.make_async_copy(k_hbm, k_ref, sems.at[0]),
        pltpu.make_async_copy(mat_hbm, ints.at[0], sems.at[1]),
        pltpu.make_async_copy(fin_hbm, ints.at[1], sems.at[2]),
        pltpu.make_async_copy(res_hbm, coef_ref.at[pl.ds(0, blocks)], sems.at[3]),
    ]
    large = [
        pltpu.make_async_copy(g_hbm.at[:, pl.ds(start, half)], g_ref.at[:, pl.ds(start, half)], sems.at[4 + n])
        for n, start in enumerate((base, half - base))
    ]
    for copy in small + large:
        copy.start()
    for copy in small:
        copy.wait()
    conduct = [conductivity(ints[0, i], k_ref) for i in range(blocks)]
    factor = [fin_factor(ints[1, i]) for i in range(blocks)]
    faces = [None] + [face(conduct[i], conduct[i - 1], factor[i]) for i in range(1, blocks)]
    ends = [conduct[0], conduct[-1], factor[0]]
    for n, row in enumerate(faces[1:] + ends):
        coef_ref[blocks + n] = row

    def pick(x):
        return jnp.where(lower, x[:half], x[half:])

    source = [pick(coef_ref[i]) for i in range(blocks)]
    eye = eye_mask(cells)
    wide = []
    large[0].wait()
    for j in range(half):
        g0 = g_ref[0, base + j]
        wide.append(jnp.concatenate([g0, stack_rows([times(g0, source[0][j : j + 1], eye)], cells)], axis=0))
    products(
        wide, source, [None] + [pick(f) for f in faces[1:]], lambda i, j: g_ref[i, base + j], out_ref,
        [pick(end) for end in ends],
    )
    large[1].wait()


def second_kernel(coef_ref, g_ref, out_ref):
    blocks, tiles, cells = g_ref.shape[:3]
    half = tiles // 2
    upper = lax.axis_index(AXIS) % 2 == 1
    base = jnp.where(upper, half, 0)

    def pick(n):
        return jnp.where(upper, coef_ref[n, half:], coef_ref[n, :half])

    source = [pick(i) for i in range(blocks)]
    faces = [None] + [pick(blocks + i) for i in range(blocks - 1)]
    eye = eye_mask(cells)
    wide = []
    for j in range(half):
        g0 = g_ref[0, base + j]
        wide.append(jnp.concatenate([g0, stack_rows([times(g0, source[0][j : j + 1], eye)], cells)], axis=0))
    products(
        wide, source, faces, lambda i, j: g_ref[i, base + j], out_ref,
        [pick(2 * blocks - 1 + n) for n in range(3)],
    )


def response_kernel(coef_ref, keep_ref, got_ref, give_ref, gain_ref, g_ref, out_ref, const_ref):
    blocks, tiles, cells = g_ref.shape[:3]
    half = tiles // 2
    is_second = lax.axis_index(AXIS) % 2 == 1
    base = jnp.where(is_second, half, 0)
    eye = jnp.where(eye_mask(cells), 1.0, 0.0)

    def reorder(x):
        return jnp.where(is_second, jnp.concatenate([x[half:], x[:half]], axis=0), x)

    source = [reorder(coef_ref[i]) for i in range(blocks)]
    faces = [None] + [reorder(coef_ref[blocks + i]) for i in range(blocks - 1)]
    nothing = jnp.zeros((cells, cells), F32)
    for group in range(2):
        own_ref, other_ref = (keep_ref, got_ref) if group == 0 else (give_ref, gain_ref)
        start = base if group == 0 else half - base
        lead, tail, values = {}, {}, {}
        for j in range(half):
            own, other = own_ref[j], other_ref[j]
            first = jnp.where(is_second, other, own)
            last = jnp.where(is_second, own, other)
            va, vb = first[2 * cells :], last[2 * cells :]
            between = face(vb[2:3], va[3:4], vb[4:5])
            scaled = jnp.concatenate([first[:cells], stack_rows([va[0:1]], cells)], axis=0) * between
            back = mul(scaled, last[cells : 2 * cells])
            back_const = back[cells:] + stack_rows([vb[1:2]], cells)
            tail[j] = jnp.concatenate(
                [
                    jnp.where(is_second, 0.0, back[:cells] * between),
                    jnp.where(is_second, eye, last[:cells].T * between),
                    jnp.where(is_second, 0.0, back_const * between),
                ],
                axis=0,
            )
            lead[j] = jnp.concatenate(
                [
                    jnp.where(is_second, scaled[:cells], eye),
                    jnp.where(is_second, scaled[cells:], 0.0)
                    + stack_rows([source[0][group * half + j : group * half + j + 1]], cells),
                ],
                axis=0,
            )
        for i in range(blocks):
            for j in range(half):
                values[i, j] = mul(lead[j], g_ref[i, start + j])
                if i < blocks - 1:
                    at = group * half + j
                    scaled = values[i, j] * faces[i + 1][at : at + 1]
                    below = scaled[cells:] + stack_rows([source[i + 1][at : at + 1]], cells)
                    lead[j] = jnp.concatenate([scaled[:cells], below], axis=0)
        for i in reversed(range(blocks)):
            for j in range(half):
                moved = mul(tail[j], g_ref[i, start + j])
                add = jnp.concatenate([values[i, j][:cells], nothing, values[i, j][cells:]], axis=0)
                solved = moved + add
                out_ref[i, start + j] = solved[: 2 * cells]
                const_ref[i, start + j] = solved[2 * cells :]
                if i:
                    at = group * half + j
                    tail[j] = solved * faces[i][at : at + 1]


def merge_kernel(keep_ref, got_ref, *out_refs):
    half, height, cells = keep_ref.shape
    here = lax.axis_index(AXIS)
    is_second = here % 2 == 1
    chip = (here % (2 * half)) // 2
    eye = eye_mask(cells)
    order = list(reversed(range(half)))
    first, last, scaled, between, moved, squared = {}, {}, {}, {}, {}, {}
    for d in order:
        keep, got = keep_ref[chip ^ d], got_ref[chip ^ d]
        first[d] = jnp.where(is_second, got, keep)
        last[d] = jnp.where(is_second, keep, got)
        va, vb = first[d][2 * cells :], last[d][2 * cells :]
        between = face(vb[2:3], va[3:4], vb[4:5])
        scaled[d] = jnp.concatenate([first[d][:cells], stack_rows([va[0:1]], cells)], axis=0) * between
    for d in order:
        moved[d] = mul(scaled[d], last[d][:cells])
    for d in order:
        squared[d] = mul(scaled[d], last[d][cells : 2 * cells])
        lower = squared[d][cells:] + stack_rows([last[d][2 * cells + 1 : 2 * cells + 2]], cells)
        squared[d] = jnp.concatenate([squared[d][:cells], lower], axis=0)
    for d in order:
        total = mul(squared[d], scaled[d][:cells].T)
        va, vb = first[d][2 * cells :], last[d][2 * cells :]
        square = first[d][cells : 2 * cells] + total[:cells]
        out_ref = out_refs[d]
        out_ref[0:cells] = moved[d][:cells]
        out_ref[cells:-ROWS] = pack(square)
        out_ref[-ROWS:] = stack_rows(
            [
                moved[d][cells : cells + 1] + vb[0:1],
                total[cells : cells + 1] + va[1:2],
                va[2:3],
                vb[3:4],
                va[4:5],
                0.5 * jnp.sum(jnp.where(eye, square, 0.0), axis=0, keepdims=True),
            ],
            cells,
        )


def chain_kernel(with_edge, *refs):
    refs, nodes = refs[1:-1], refs[-1]
    if with_edge:
        edge_ref, refs = refs[0], refs[1:]
    count, height, cells = nodes.shape
    refs, out_refs, ends = refs[count - 1 :: -1], refs[count:-1], refs[-1]
    chip = (lax.axis_index(AXIS) % (2 * count)) // 2
    for d in range(count):
        nodes[chip ^ d] = refs[d][...]
    eye = eye_mask(cells)
    vectors = [nodes[k, height - ROWS :] for k in range(count)]
    squares = [None] + [
        unpack(nodes[k, cells : height - ROWS], vectors[k][5:6], pltpu.roll) for k in range(1, count)
    ]
    faces = [None] + [
        face(vectors[k][2:3], vectors[k - 1][3:4], vectors[k][4:5]) for k in range(1, count)
    ]
    entering, arriving = [None] * count, [None] * count
    leaving = vectors[0][0:1]
    if with_edge:
        entering[0], arriving[-1] = edge_ref[0:1], edge_ref[1:2]
        leaving = leaving + times_t(nodes[0, 0:cells], entering[0], eye)
    for k in range(1, count):
        entering[k] = faces[k] * leaving
        if k < count - 1:
            leaving = vectors[k][0:1] + times_t(nodes[k, 0:cells], entering[k], eye)
    heads = [None] + [
        vectors[k][1:2] + times(squares[k], entering[k], eye) + times_t(squares[k], entering[k], eye)
        for k in range(1, count)
    ]
    for k in reversed(range(1, count)):
        head = heads[k]
        if arriving[k] is not None:
            head = head + times(nodes[k, 0:cells], arriving[k], eye)
        arriving[k - 1] = faces[k] * head
    zero = jnp.zeros((1, cells), F32)
    for k in range(count):
        ends[k] = stack_rows(
            [zero if entering[k] is None else entering[k], zero if arriving[k] is None else arriving[k]],
            cells,
        )
    for d in range(count):
        out_refs[d][...] = ends[chip ^ d]


def order_kernel(*refs):
    out_ref = refs[-1]
    count = out_ref.shape[0]
    chip = (lax.axis_index(AXIS) % (2 * count)) // 2
    for d in range(count):
        out_ref[chip ^ d] = refs[count - 1 - d][...]


def finish(ends_ref, start, out_ref, const_ref, put):
    blocks, _, _, cells = out_ref.shape
    eye = eye_mask(cells)
    for j in range(ends_ref.shape[0]):
        up, down = (
            jnp.sum(jnp.where(eye, ends_ref[j, n : n + 1], 0.0), axis=1, keepdims=True) for n in range(2)
        )
        for i in range(blocks):
            both = out_ref[i, start + j, 0:cells] * up + out_ref[i, start + j, cells : 2 * cells] * down
            put(i, j, const_ref[i, start + j, 0:1] + jnp.sum(both, axis=0, keepdims=True))


def own_kernel(mine_ref, out_ref, const_ref, done_ref):
    half = mine_ref.shape[0]

    def put(i, j, row):
        done_ref[i, j : j + 1] = row

    finish(mine_ref, jnp.where(lax.axis_index(AXIS) % 2 == 1, half, 0), out_ref, const_ref, put)


def finish_kernel(theirs_ref, done_ref, phase_ref, out_ref, const_ref, corr_ref, step_ref, rest_ref):
    half = theirs_ref.shape[0]
    is_second = lax.axis_index(AXIS) % 2 == 1

    def put(i, j, row):
        rest_ref[i, j : j + 1] = row

    finish(theirs_ref, jnp.where(is_second, 0, half), out_ref, const_ref, put)
    for i in range(corr_ref.shape[0]):
        own, rest = done_ref[i], rest_ref[i]
        both = jnp.where(
            is_second, jnp.concatenate([rest, own], axis=0), jnp.concatenate([own, rest], axis=0)
        )
        corr_ref[i] = both
        step_ref[i] = both * (1.0 + 2.0 * phase_ref[i].astype(F32))


VMEM = pl.BlockSpec(memory_space=pltpu.VMEM)
HBM = pl.BlockSpec(memory_space=pltpu.HBM)
LIMIT = pltpu.CompilerParams(vmem_limit_bytes=16 << 20)


def cost(flops, moved):
    return pl.CostEstimate(flops=flops, bytes_accessed=moved, transcendentals=0)


def send(x, distance):
    return lax.ppermute(x, AXIS, [(i, i ^ distance) for i in range(lax.axis_size(AXIS))])


def send_all(parts):
    arrived = {0: parts[0]}
    for d in reversed(range(1, len(parts))):
        arrived[d] = send(parts[d], 2 * d)
    return [arrived[d] for d in range(len(parts))]


def exact(left, right):
    return jnp.dot(left, right, precision=lax.Precision.HIGHEST)


def outer_edge(nodes, devices):
    cells = nodes[0].shape[-1]

    def parts(node):
        return node[:cells], node[cells : 2 * cells], node[2 * cells :]

    def widen(node):
        part = unpack(node[cells:-ROWS], node[-3:-2], jnp.roll)
        return jnp.concatenate([node[:cells], part + part.T, node[-ROWS:]], axis=0)

    def join(first, second):
        (ma, qa, va), (mb, qb, vb) = parts(first), parts(second)
        between = face(vb[2], va[3], vb[4])
        scaled, shift = ma * between, va[0] * between
        q = qa + exact(exact(scaled, qb), scaled.T)
        tail = exact(shift, mb) + vb[0]
        lead = va[1] + exact(scaled, exact(qb, shift) + vb[1])
        rest = jnp.zeros((ROWS - 5, cells), F32)
        rows = jnp.stack([tail, lead, va[2], vb[3], va[4]])
        return jnp.concatenate([exact(scaled, mb), q, rows, rest], axis=0)

    groups = lax.axis_size(AXIS) // devices
    whole = functools.reduce(join, [widen(nodes[k]) for k in range(nodes.shape[0])])
    members = [[g * devices + q for g in range(groups)] for q in range(devices)]
    every = lax.all_gather(whole, AXIS, axis=0, axis_index_groups=members)
    split_up = [parts(every[g]) for g in range(groups)]
    faces = [face(b[2][2], a[2][3], b[2][4]) for a, b in zip(split_up[:-1], split_up[1:])]
    entering = [jnp.zeros((cells,), F32)]
    for g in range(groups - 1):
        m, _, v = split_up[g]
        entering.append(faces[g] * (exact(entering[g], m) + v[0]))
    arriving = [jnp.zeros((cells,), F32)]
    for g in reversed(range(1, groups)):
        m, q, v = split_up[g]
        arriving.append(faces[g - 1] * (exact(m, arriving[-1]) + exact(q, entering[g]) + v[1]))
    arriving.reverse()
    own = lax.axis_index(AXIS) // devices
    both = jnp.stack([jnp.stack(entering)[own], jnp.stack(arriving)[own]])
    return jnp.concatenate([both, jnp.zeros((ROWS - 2, cells), F32)], axis=0)


def on_device(block_inverses, residual, material, fin_mask, phase_mask, k_table):
    blocks, tiles, cells = residual.shape
    half = tiles // 2
    height = 2 * cells + ROWS
    map_bytes = 4 * height * cells

    map_shape = (half, height, cells)
    work = cost(24 * half * blocks * cells**3, 8 * half * blocks * cells**2)
    given = [pltpu.with_memory_space_constraint(x, pltpu.HBM) for x in (k_table, material, fin_mask, residual, block_inverses)]
    give, coef, inverses = pl.pallas_call(
        first_kernel,
        out_shape=(
            pltpu.VMEM(map_shape, F32),
            pltpu.VMEM((2 * blocks + 2, tiles, cells), F32),
            pltpu.VMEM(block_inverses.shape, F32),
        ),
        in_specs=[HBM] * 5,
        out_specs=(VMEM,) * 3,
        scratch_shapes=[
            pltpu.SMEM(k_table.shape, F32),
            pltpu.VMEM((2, blocks, tiles, cells), jnp.int32),
            pltpu.SemaphoreType.DMA((6,)),
        ],
        compiler_params=LIMIT,
        cost_estimate=work,
    )(*given)
    got = send(give, 1)
    keep = pl.pallas_call(
        second_kernel,
        out_shape=jax.ShapeDtypeStruct(map_shape, F32),
        in_specs=[VMEM, VMEM],
        out_specs=VMEM,
        compiler_params=LIMIT,
        cost_estimate=work,
    )(coef, inverses)
    gain = send(keep, 1)
    responses, constants = pl.pallas_call(
        response_kernel,
        out_shape=(
            jax.ShapeDtypeStruct((blocks, tiles, 2 * cells, cells), F32),
            jax.ShapeDtypeStruct((blocks, tiles, ROWS, cells), F32),
        ),
        in_specs=[VMEM] * 6,
        out_specs=(VMEM, VMEM),
        compiler_params=LIMIT,
        cost_estimate=cost(48 * tiles * blocks * cells**3, 16 * tiles * blocks * cells**2),
    )(coef, keep, got, give, gain, inverses)
    short = cells + cells // 2 + ROWS
    node = jax.ShapeDtypeStruct((short, cells), F32)
    joined = pl.pallas_call(
        merge_kernel,
        out_shape=(node,) * half,
        in_specs=[VMEM, VMEM],
        out_specs=(VMEM,) * half,
        compiler_params=LIMIT,
        cost_estimate=cost(24 * half * cells**3, 3 * half * map_bytes),
    )(keep, got)
    arrived = send_all(joined)
    grouped = lax.axis_size(AXIS) > tiles
    edge = []
    if grouped:
        chip = (lax.axis_index(AXIS) % tiles) // 2
        ordered = jnp.stack(arrived)[jnp.arange(half) ^ chip]
        edge = [outer_edge(ordered, tiles)]
    end = jax.ShapeDtypeStruct((ROWS, cells), F32)
    ends = pl.pallas_call(
        functools.partial(chain_kernel, grouped),
        out_shape=(end,) * half,
        in_specs=[pl.BlockSpec(memory_space=pl.ANY)] + [VMEM] * (half + len(edge)),
        out_specs=(VMEM,) * half,
        scratch_shapes=[pltpu.VMEM((half, ROWS, cells), F32), pltpu.VMEM((half, short, cells), F32)],
        compiler_params=LIMIT,
        cost_estimate=cost(8 * half * cells**2, half * map_bytes),
    )(constants, *edge, *arrived[::-1])
    ends = send_all(ends)
    mine = pl.pallas_call(
        order_kernel,
        out_shape=jax.ShapeDtypeStruct((half, ROWS, cells), F32),
        in_specs=[VMEM] * half,
        out_specs=VMEM,
        compiler_params=LIMIT,
        cost_estimate=cost(0, 8 * half * ROWS * cells),
    )(*ends[::-1])
    theirs = send(mine, 1)
    half_shape = (blocks, half, cells)
    work = cost(2 * blocks * tiles * cells**2, 4 * blocks * tiles * cells**2)
    done = pl.pallas_call(
        own_kernel,
        out_shape=jax.ShapeDtypeStruct(half_shape, F32),
        in_specs=[VMEM] * 3,
        out_specs=VMEM,
        compiler_params=LIMIT,
        cost_estimate=work,
    )(mine, responses, constants)
    shape = jax.ShapeDtypeStruct((blocks, tiles, cells), F32)
    return pl.pallas_call(
        finish_kernel,
        out_shape=(shape, shape),
        in_specs=[VMEM] * 5,
        out_specs=(VMEM, VMEM),
        scratch_shapes=[pltpu.VMEM(half_shape, F32)],
        compiler_params=LIMIT,
        cost_estimate=work,
    )(theirs, done, phase_mask, responses, constants)


def solution(mesh):
    return jax.shard_map(
        on_device,
        mesh=mesh,
        in_specs=(
            P("gx", "pa", None, None),
            P("gx", "pa", None),
            P("gx", "pa", None),
            P("gx", "pa", None),
            P("gx", "pa", None),
            P(),
        ),
        out_specs=(P("gx", "pa", None), P("gx", "pa", None)),
        check_vma=False,
    )
```

```python
import functools

import jax
import jax.numpy as jnp
from jax import lax
from jax.experimental import pallas as pl
from jax.experimental.pallas import tpu as pltpu
from jax.sharding import PartitionSpec as P

BF16 = jnp.bfloat16
F32 = jnp.float32
ROWS = 8
AXIS = "gx"


def split(x):
    high = x.astype(BF16)
    return high, (x - high.astype(F32)).astype(BF16)


def mul(left, right):
    lh, ll = split(left)
    rh, rl = split(right)
    lhs = jnp.concatenate([lh, ll], axis=1)
    rhs = jnp.concatenate(
        [jnp.concatenate([rh, rl], axis=1), jnp.concatenate([rh, jnp.zeros_like(rl)], axis=1)], axis=0
    )
    both = jnp.dot(lhs, rhs, preferred_element_type=F32)
    width = right.shape[1]
    return both[:, :width] + both[:, width:]


def mul_t(left, right):
    lh, ll = split(left)
    rh, rl = split(right)
    lhs = jnp.concatenate([lh, ll], axis=1)
    rhs = jnp.concatenate(
        [jnp.concatenate([rh, rh], axis=1), jnp.concatenate([rl, jnp.zeros_like(rl)], axis=1)], axis=0
    )
    both = lax.dot_general(lhs, rhs, (((1,), (1,)), ((), ())), preferred_element_type=F32)
    width = right.shape[0]
    return both[:, :width] + both[:, width:]


def face(conduct, earlier, fin_factor):
    return 2.0 * conduct * earlier / (conduct + earlier) * fin_factor


def conductivity(material, k_ref):
    total = jnp.zeros(material.shape, F32)
    for code in range(k_ref.shape[0]):
        total = total + jnp.where(material == code, k_ref[code], 0.0)
    return total


def fin_factor(fin):
    return 0.9 + 0.1 * fin.astype(F32)


def eye_mask(size):
    return lax.broadcasted_iota(jnp.int32, (size, size), 0) == lax.broadcasted_iota(
        jnp.int32, (size, size), 1
    )


def times(matrix, row, eye):
    column = jnp.sum(matrix * row, axis=1, keepdims=True)
    return jnp.sum(jnp.where(eye, column, 0.0), axis=0, keepdims=True)


def times_t(matrix, row, eye):
    column = jnp.sum(jnp.where(eye, row, 0.0), axis=1, keepdims=True)
    return jnp.sum(matrix * column, axis=0, keepdims=True)


def halves(cells):
    shape = (cells // 2, cells)
    return lax.broadcasted_iota(jnp.int32, shape, 0), lax.broadcasted_iota(jnp.int32, shape, 1)


def pack(square):
    middle = square.shape[0] // 2
    row, lane = halves(square.shape[1])
    top, bottom = square[:middle], pltpu.roll(square[middle:], middle, 1)
    return jnp.where(
        (lane >= middle) | (lane < row), top, jnp.where(lane == row, 0.5 * top, bottom)
    )


def unpack(packed, half_diagonal, roll):
    middle, cells = packed.shape
    row, lane = halves(cells)
    top = jnp.where((lane >= middle) | (lane <= row), packed, 0.0)
    bottom = jnp.where(lane - middle > row, roll(packed, middle, 1), 0.0)
    bottom = jnp.where(lane - middle == row, half_diagonal, bottom)
    return jnp.concatenate([top, bottom], axis=0)


def stack_rows(rows, cells):
    at = lax.broadcasted_iota(jnp.int32, (ROWS, cells), 0)
    out = jnp.zeros((ROWS, cells), F32)
    for place, row in enumerate(rows):
        out = jnp.where(at == place, jnp.broadcast_to(row, (ROWS, cells)), out)
    return out


def products(wide, source, faces, g_of, out_ref, ends):
    cells = wide[0].shape[1]
    tiles = range(len(wide))
    total = list(wide)
    for i in range(1, len(source)):
        for j in tiles:
            scaled = wide[j] * faces[i][j : j + 1]
            sh, sl = split(scaled[:cells])
            vh, vl = split(scaled[cells:] + stack_rows([source[i][j : j + 1]], cells))
            gh, gl = split(g_of(i, j))
            zero = jnp.zeros_like(gl)
            both = jnp.dot(
                jnp.concatenate([jnp.concatenate([sh, sl], axis=1), jnp.concatenate([vh, vl], axis=1)], axis=0),
                jnp.concatenate([jnp.concatenate([gh, gl], axis=1), jnp.concatenate([gh, zero], axis=1)], axis=0),
                preferred_element_type=F32,
            )
            wide[j] = both[:, :cells] + both[:, cells:]
            wh, wl = split(wide[j])
            th, tl = split(scaled[:cells].T)
            both = jnp.dot(
                jnp.concatenate([wh, wl], axis=1),
                jnp.concatenate([jnp.concatenate([th, tl], axis=1), jnp.concatenate([th, zero], axis=1)], axis=0),
                preferred_element_type=F32,
            )
            total[j] = total[j] + (both[:, :cells] + both[:, cells:])
    for j in tiles:
        out_ref[j, 0:cells] = wide[j][:cells]
        out_ref[j, cells : 2 * cells] = total[j][:cells]
        out_ref[j, 2 * cells :] = stack_rows(
            [wide[j][cells : cells + 1], total[j][cells : cells + 1]] + [end[j : j + 1] for end in ends], cells
        )


def first_kernel(k_hbm, mat_hbm, fin_hbm, res_hbm, g_hbm, out_ref, coef_ref, g_ref, k_ref, ints, sems):
    blocks, tiles, cells = res_hbm.shape
    half = tiles // 2
    lower = lax.axis_index(AXIS) % 2 == 1
    base = jnp.where(lower, 0, half)
    small = [
        pltpu.make_async_copy(k_hbm, k_ref, sems.at[0]),
        pltpu.make_async_copy(mat_hbm, ints.at[0], sems.at[1]),
        pltpu.make_async_copy(fin_hbm, ints.at[1], sems.at[2]),
        pltpu.make_async_copy(res_hbm, coef_ref.at[pl.ds(0, blocks)], sems.at[3]),
    ]
    large = [
        pltpu.make_async_copy(g_hbm.at[:, pl.ds(start, half)], g_ref.at[:, pl.ds(start, half)], sems.at[4 + n])
        for n, start in enumerate((base, half - base))
    ]
    for copy in small + large:
        copy.start()
    for copy in small:
        copy.wait()
    conduct = [conductivity(ints[0, i], k_ref) for i in range(blocks)]
    factor = [fin_factor(ints[1, i]) for i in range(blocks)]
    faces = [None] + [face(conduct[i], conduct[i - 1], factor[i]) for i in range(1, blocks)]
    ends = [conduct[0], conduct[-1], factor[0]]
    for n, row in enumerate(faces[1:] + ends):
        coef_ref[blocks + n] = row

    def pick(x):
        return jnp.where(lower, x[:half], x[half:])

    source = [pick(coef_ref[i]) for i in range(blocks)]
    eye = eye_mask(cells)
    wide = []
    large[0].wait()
    for j in range(half):
        g0 = g_ref[0, base + j]
        wide.append(jnp.concatenate([g0, stack_rows([times(g0, source[0][j : j + 1], eye)], cells)], axis=0))
    products(
        wide, source, [None] + [pick(f) for f in faces[1:]], lambda i, j: g_ref[i, base + j], out_ref,
        [pick(end) for end in ends],
    )
    large[1].wait()


def second_kernel(coef_ref, g_ref, out_ref):
    blocks, tiles, cells = g_ref.shape[:3]
    half = tiles // 2
    upper = lax.axis_index(AXIS) % 2 == 1
    base = jnp.where(upper, half, 0)

    def pick(n):
        return jnp.where(upper, coef_ref[n, half:], coef_ref[n, :half])

    source = [pick(i) for i in range(blocks)]
    faces = [None] + [pick(blocks + i) for i in range(blocks - 1)]
    eye = eye_mask(cells)
    wide = []
    for j in range(half):
        g0 = g_ref[0, base + j]
        wide.append(jnp.concatenate([g0, stack_rows([times(g0, source[0][j : j + 1], eye)], cells)], axis=0))
    products(
        wide, source, faces, lambda i, j: g_ref[i, base + j], out_ref,
        [pick(2 * blocks - 1 + n) for n in range(3)],
    )


def response_kernel(coef_ref, keep_ref, got_ref, give_ref, gain_ref, g_ref, out_ref, const_ref):
    blocks, tiles, cells = g_ref.shape[:3]
    half = tiles // 2
    is_second = lax.axis_index(AXIS) % 2 == 1
    base = jnp.where(is_second, half, 0)
    eye = jnp.where(eye_mask(cells), 1.0, 0.0)

    def reorder(x):
        return jnp.where(is_second, jnp.concatenate([x[half:], x[:half]], axis=0), x)

    source = [reorder(coef_ref[i]) for i in range(blocks)]
    faces = [None] + [reorder(coef_ref[blocks + i]) for i in range(blocks - 1)]
    nothing = jnp.zeros((cells, cells), F32)
    for group in range(2):
        own_ref, other_ref = (keep_ref, got_ref) if group == 0 else (give_ref, gain_ref)
        start = base if group == 0 else half - base
        lead, tail, values = {}, {}, {}
        for j in range(half):
            own, other = own_ref[j], other_ref[j]
            first = jnp.where(is_second, other, own)
            last = jnp.where(is_second, own, other)
            va, vb = first[2 * cells :], last[2 * cells :]
            between = face(vb[2:3], va[3:4], vb[4:5])
            scaled = jnp.concatenate([first[:cells], stack_rows([va[0:1]], cells)], axis=0) * between
            back = mul(scaled, last[cells : 2 * cells])
            back_const = back[cells:] + stack_rows([vb[1:2]], cells)
            tail[j] = jnp.concatenate(
                [
                    jnp.where(is_second, 0.0, back[:cells] * between),
                    jnp.where(is_second, eye, last[:cells].T * between),
                    jnp.where(is_second, 0.0, back_const * between),
                ],
                axis=0,
            )
            lead[j] = jnp.concatenate(
                [
                    jnp.where(is_second, scaled[:cells], eye),
                    jnp.where(is_second, scaled[cells:], 0.0)
                    + stack_rows([source[0][group * half + j : group * half + j + 1]], cells),
                ],
                axis=0,
            )
        for i in range(blocks):
            for j in range(half):
                values[i, j] = mul(lead[j], g_ref[i, start + j])
                if i < blocks - 1:
                    at = group * half + j
                    scaled = values[i, j] * faces[i + 1][at : at + 1]
                    below = scaled[cells:] + stack_rows([source[i + 1][at : at + 1]], cells)
                    lead[j] = jnp.concatenate([scaled[:cells], below], axis=0)
        for i in reversed(range(blocks)):
            for j in range(half):
                moved = mul(tail[j], g_ref[i, start + j])
                add = jnp.concatenate([values[i, j][:cells], nothing, values[i, j][cells:]], axis=0)
                solved = moved + add
                out_ref[i, start + j] = solved[: 2 * cells]
                const_ref[i, start + j] = solved[2 * cells :]
                if i:
                    at = group * half + j
                    tail[j] = solved * faces[i][at : at + 1]


def merge_kernel(order, keep_ref, got_ref, *rest):
    half, height, cells = keep_ref.shape
    out_refs = rest[-len(order) :]
    here = lax.axis_index(AXIS)
    is_second = here % 2 == 1
    chip = (here % (2 * half)) // 2
    eye = eye_mask(cells)
    first, last, scaled, between, moved, squared = {}, {}, {}, {}, {}, {}
    for d in order:
        keep, got = keep_ref[chip ^ d], got_ref[chip ^ d]
        first[d] = jnp.where(is_second, got, keep)
        last[d] = jnp.where(is_second, keep, got)
        va, vb = first[d][2 * cells :], last[d][2 * cells :]
        between = face(vb[2:3], va[3:4], vb[4:5])
        scaled[d] = jnp.concatenate([first[d][:cells], stack_rows([va[0:1]], cells)], axis=0) * between
    for d in order:
        moved[d] = mul(scaled[d], last[d][:cells])
    for d in order:
        squared[d] = mul(scaled[d], last[d][cells : 2 * cells])
        lower = squared[d][cells:] + stack_rows([last[d][2 * cells + 1 : 2 * cells + 2]], cells)
        squared[d] = jnp.concatenate([squared[d][:cells], lower], axis=0)
    for d in order:
        total = mul(squared[d], scaled[d][:cells].T)
        va, vb = first[d][2 * cells :], last[d][2 * cells :]
        square = first[d][cells : 2 * cells] + total[:cells]
        out_ref = out_refs[order.index(d)]
        out_ref[0:cells] = moved[d][:cells]
        out_ref[cells:-ROWS] = pack(square)
        out_ref[-ROWS:] = stack_rows(
            [
                moved[d][cells : cells + 1] + vb[0:1],
                total[cells : cells + 1] + va[1:2],
                va[2:3],
                vb[3:4],
                va[4:5],
                0.5 * jnp.sum(jnp.where(eye, square, 0.0), axis=0, keepdims=True),
            ],
            cells,
        )


def chain_kernel(with_edge, *refs):
    refs, nodes = refs[1:-1], refs[-1]
    if with_edge:
        edge_ref, refs = refs[0], refs[1:]
    count, height, cells = nodes.shape
    refs, out_refs, ends = refs[count - 1 :: -1], refs[count:-1], refs[-1]
    chip = (lax.axis_index(AXIS) % (2 * count)) // 2
    for d in range(count):
        nodes[chip ^ d] = refs[d][...]
    eye = eye_mask(cells)
    vectors = [nodes[k, height - ROWS :] for k in range(count)]
    squares = [None] + [
        unpack(nodes[k, cells : height - ROWS], vectors[k][5:6], pltpu.roll) for k in range(1, count)
    ]
    faces = [None] + [
        face(vectors[k][2:3], vectors[k - 1][3:4], vectors[k][4:5]) for k in range(1, count)
    ]
    entering, arriving = [None] * count, [None] * count
    leaving = vectors[0][0:1]
    if with_edge:
        entering[0], arriving[-1] = edge_ref[0:1], edge_ref[1:2]
        leaving = leaving + times_t(nodes[0, 0:cells], entering[0], eye)
    for k in range(1, count):
        entering[k] = faces[k] * leaving
        if k < count - 1:
            leaving = vectors[k][0:1] + times_t(nodes[k, 0:cells], entering[k], eye)
    heads = [None] + [
        vectors[k][1:2] + times(squares[k], entering[k], eye) + times_t(squares[k], entering[k], eye)
        for k in range(1, count)
    ]
    for k in reversed(range(1, count)):
        head = heads[k]
        if arriving[k] is not None:
            head = head + times(nodes[k, 0:cells], arriving[k], eye)
        arriving[k - 1] = faces[k] * head
    zero = jnp.zeros((1, cells), F32)
    for k in range(count):
        ends[k] = stack_rows(
            [zero if entering[k] is None else entering[k], zero if arriving[k] is None else arriving[k]],
            cells,
        )
    for d in range(count):
        out_refs[d][...] = ends[chip ^ d]


def order_kernel(*refs):
    out_ref = refs[-1]
    count = out_ref.shape[0]
    chip = (lax.axis_index(AXIS) % (2 * count)) // 2
    for d in range(count):
        out_ref[chip ^ d] = refs[count - 1 - d][...]


def finish(ends_ref, start, out_ref, const_ref, put):
    blocks, _, _, cells = out_ref.shape
    eye = eye_mask(cells)
    for j in range(ends_ref.shape[0]):
        up, down = (
            jnp.sum(jnp.where(eye, ends_ref[j, n : n + 1], 0.0), axis=1, keepdims=True) for n in range(2)
        )
        for i in range(blocks):
            both = out_ref[i, start + j, 0:cells] * up + out_ref[i, start + j, cells : 2 * cells] * down
            put(i, j, const_ref[i, start + j, 0:1] + jnp.sum(both, axis=0, keepdims=True))


def own_kernel(mine_ref, out_ref, const_ref, done_ref):
    half = mine_ref.shape[0]

    def put(i, j, row):
        done_ref[i, j : j + 1] = row

    finish(mine_ref, jnp.where(lax.axis_index(AXIS) % 2 == 1, half, 0), out_ref, const_ref, put)


def finish_kernel(theirs_ref, done_ref, phase_ref, out_ref, const_ref, corr_ref, step_ref, rest_ref):
    half = theirs_ref.shape[0]
    is_second = lax.axis_index(AXIS) % 2 == 1

    def put(i, j, row):
        rest_ref[i, j : j + 1] = row

    finish(theirs_ref, jnp.where(is_second, 0, half), out_ref, const_ref, put)
    for i in range(corr_ref.shape[0]):
        own, rest = done_ref[i], rest_ref[i]
        both = jnp.where(
            is_second, jnp.concatenate([rest, own], axis=0), jnp.concatenate([own, rest], axis=0)
        )
        corr_ref[i] = both
        step_ref[i] = both * (1.0 + 2.0 * phase_ref[i].astype(F32))


VMEM = pl.BlockSpec(memory_space=pltpu.VMEM)
HBM = pl.BlockSpec(memory_space=pltpu.HBM)
LIMIT = pltpu.CompilerParams(vmem_limit_bytes=16 << 20)


def cost(flops, moved):
    return pl.CostEstimate(flops=flops, bytes_accessed=moved, transcendentals=0)


def send(x, distance):
    return lax.ppermute(x, AXIS, [(i, i ^ distance) for i in range(lax.axis_size(AXIS))])


def send_all(parts):
    arrived = {0: parts[0]}
    for d in reversed(range(1, len(parts))):
        arrived[d] = send(parts[d], 2 * d)
    return [arrived[d] for d in range(len(parts))]


def exact(left, right):
    return jnp.dot(left, right, precision=lax.Precision.HIGHEST)


def outer_edge(nodes, devices):
    cells = nodes[0].shape[-1]

    def parts(node):
        return node[:cells], node[cells : 2 * cells], node[2 * cells :]

    def widen(node):
        part = unpack(node[cells:-ROWS], node[-3:-2], jnp.roll)
        return jnp.concatenate([node[:cells], part + part.T, node[-ROWS:]], axis=0)

    def join(first, second):
        (ma, qa, va), (mb, qb, vb) = parts(first), parts(second)
        between = face(vb[2], va[3], vb[4])
        scaled, shift = ma * between, va[0] * between
        q = qa + exact(exact(scaled, qb), scaled.T)
        tail = exact(shift, mb) + vb[0]
        lead = va[1] + exact(scaled, exact(qb, shift) + vb[1])
        rest = jnp.zeros((ROWS - 5, cells), F32)
        rows = jnp.stack([tail, lead, va[2], vb[3], va[4]])
        return jnp.concatenate([exact(scaled, mb), q, rows, rest], axis=0)

    groups = lax.axis_size(AXIS) // devices
    whole = functools.reduce(join, [widen(nodes[k]) for k in range(nodes.shape[0])])
    members = [[g * devices + q for g in range(groups)] for q in range(devices)]
    every = lax.all_gather(whole, AXIS, axis=0, axis_index_groups=members)
    split_up = [parts(every[g]) for g in range(groups)]
    faces = [face(b[2][2], a[2][3], b[2][4]) for a, b in zip(split_up[:-1], split_up[1:])]
    entering = [jnp.zeros((cells,), F32)]
    for g in range(groups - 1):
        m, _, v = split_up[g]
        entering.append(faces[g] * (exact(entering[g], m) + v[0]))
    arriving = [jnp.zeros((cells,), F32)]
    for g in reversed(range(1, groups)):
        m, q, v = split_up[g]
        arriving.append(faces[g - 1] * (exact(m, arriving[-1]) + exact(q, entering[g]) + v[1]))
    arriving.reverse()
    own = lax.axis_index(AXIS) // devices
    both = jnp.stack([jnp.stack(entering)[own], jnp.stack(arriving)[own]])
    return jnp.concatenate([both, jnp.zeros((ROWS - 2, cells), F32)], axis=0)


def on_device(block_inverses, residual, material, fin_mask, phase_mask, k_table):
    blocks, tiles, cells = residual.shape
    half = tiles // 2
    height = 2 * cells + ROWS
    map_bytes = 4 * height * cells

    map_shape = (half, height, cells)
    work = cost(24 * half * blocks * cells**3, 8 * half * blocks * cells**2)
    given = [pltpu.with_memory_space_constraint(x, pltpu.HBM) for x in (k_table, material, fin_mask, residual, block_inverses)]
    give, coef, inverses = pl.pallas_call(
        first_kernel,
        out_shape=(
            pltpu.VMEM(map_shape, F32),
            pltpu.VMEM((2 * blocks + 2, tiles, cells), F32),
            pltpu.VMEM(block_inverses.shape, F32),
        ),
        in_specs=[HBM] * 5,
        out_specs=(VMEM,) * 3,
        scratch_shapes=[
            pltpu.SMEM(k_table.shape, F32),
            pltpu.VMEM((2, blocks, tiles, cells), jnp.int32),
            pltpu.SemaphoreType.DMA((6,)),
        ],
        compiler_params=LIMIT,
        cost_estimate=work,
    )(*given)
    got = send(give, 1)
    keep = pl.pallas_call(
        second_kernel,
        out_shape=jax.ShapeDtypeStruct(map_shape, F32),
        in_specs=[VMEM, VMEM],
        out_specs=VMEM,
        compiler_params=LIMIT,
        cost_estimate=work,
    )(coef, inverses)
    gain = send(keep, 1)
    responses, constants = pl.pallas_call(
        response_kernel,
        out_shape=(
            jax.ShapeDtypeStruct((blocks, tiles, 2 * cells, cells), F32),
            jax.ShapeDtypeStruct((blocks, tiles, ROWS, cells), F32),
        ),
        in_specs=[VMEM] * 6,
        out_specs=(VMEM, VMEM),
        compiler_params=LIMIT,
        cost_estimate=cost(48 * tiles * blocks * cells**3, 16 * tiles * blocks * cells**2),
    )(coef, keep, got, give, gain, inverses)
    short = cells + cells // 2 + ROWS
    node = jax.ShapeDtypeStruct((short, cells), F32)

    def join(order, *after):
        return pl.pallas_call(
            functools.partial(merge_kernel, order),
            out_shape=(node,) * len(order),
            in_specs=[VMEM, VMEM] + [pl.BlockSpec(memory_space=pl.ANY)] * len(after),
            out_specs=(VMEM,) * len(order),
            compiler_params=LIMIT,
            cost_estimate=cost(24 * len(order) * cells**3, 3 * len(order) * map_bytes),
        )(keep, got, *after)

    near = list(reversed(range(half - 1)))
    far = join([half - 1])
    joined = [*far, *join(near, *far)][::-1]
    arrived = send_all(joined)
    grouped = lax.axis_size(AXIS) > tiles
    edge = []
    if grouped:
        chip = (lax.axis_index(AXIS) % tiles) // 2
        ordered = jnp.stack(arrived)[jnp.arange(half) ^ chip]
        edge = [outer_edge(ordered, tiles)]
    end = jax.ShapeDtypeStruct((ROWS, cells), F32)
    ends = pl.pallas_call(
        functools.partial(chain_kernel, grouped),
        out_shape=(end,) * half,
        in_specs=[pl.BlockSpec(memory_space=pl.ANY)] + [VMEM] * (half + len(edge)),
        out_specs=(VMEM,) * half,
        scratch_shapes=[pltpu.VMEM((half, ROWS, cells), F32), pltpu.VMEM((half, short, cells), F32)],
        compiler_params=LIMIT,
        cost_estimate=cost(8 * half * cells**2, half * map_bytes),
    )(constants, *edge, *arrived[::-1])
    ends = send_all(ends)
    mine = pl.pallas_call(
        order_kernel,
        out_shape=jax.ShapeDtypeStruct((half, ROWS, cells), F32),
        in_specs=[VMEM] * half,
        out_specs=VMEM,
        compiler_params=LIMIT,
        cost_estimate=cost(0, 8 * half * ROWS * cells),
    )(*ends[::-1])
    theirs = send(mine, 1)
    half_shape = (blocks, half, cells)
    work = cost(2 * blocks * tiles * cells**2, 4 * blocks * tiles * cells**2)
    done = pl.pallas_call(
        own_kernel,
        out_shape=jax.ShapeDtypeStruct(half_shape, F32),
        in_specs=[VMEM] * 3,
        out_specs=VMEM,
        compiler_params=LIMIT,
        cost_estimate=work,
    )(mine, responses, constants)
    shape = jax.ShapeDtypeStruct((blocks, tiles, cells), F32)
    return pl.pallas_call(
        finish_kernel,
        out_shape=(shape, shape),
        in_specs=[VMEM] * 5,
        out_specs=(VMEM, VMEM),
        scratch_shapes=[pltpu.VMEM(half_shape, F32)],
        compiler_params=LIMIT,
        cost_estimate=work,
    )(theirs, done, phase_mask, responses, constants)


def solution(mesh):
    return jax.shard_map(
        on_device,
        mesh=mesh,
        in_specs=(
            P("gx", "pa", None, None),
            P("gx", "pa", None),
            P("gx", "pa", None),
            P("gx", "pa", None),
            P("gx", "pa", None),
            P(),
        ),
        out_specs=(P("gx", "pa", None), P("gx", "pa", None)),
        check_vma=False,
    )
```

```python
import functools

import jax
import jax.numpy as jnp
from jax import lax
from jax.experimental import pallas as pl
from jax.experimental.pallas import tpu as pltpu
from jax.sharding import PartitionSpec as P

BF16 = jnp.bfloat16
F32 = jnp.float32
ROWS = 8
AXIS = "gx"


def split(x):
    high = x.astype(BF16)
    return high, (x - high.astype(F32)).astype(BF16)


def mul(left, right):
    lh, ll = split(left)
    rh, rl = split(right)
    lhs = jnp.concatenate([lh, ll], axis=1)
    rhs = jnp.concatenate(
        [jnp.concatenate([rh, rl], axis=1), jnp.concatenate([rh, jnp.zeros_like(rl)], axis=1)], axis=0
    )
    both = jnp.dot(lhs, rhs, preferred_element_type=F32)
    width = right.shape[1]
    return both[:, :width] + both[:, width:]


def mul_t(left, right):
    lh, ll = split(left)
    rh, rl = split(right)
    lhs = jnp.concatenate([lh, ll], axis=1)
    rhs = jnp.concatenate(
        [jnp.concatenate([rh, rh], axis=1), jnp.concatenate([rl, jnp.zeros_like(rl)], axis=1)], axis=0
    )
    both = lax.dot_general(lhs, rhs, (((1,), (1,)), ((), ())), preferred_element_type=F32)
    width = right.shape[0]
    return both[:, :width] + both[:, width:]


def face(conduct, earlier, fin_factor):
    return 2.0 * conduct * earlier / (conduct + earlier) * fin_factor


def conductivity(material, k_ref):
    total = jnp.zeros(material.shape, F32)
    for code in range(k_ref.shape[0]):
        total = total + jnp.where(material == code, k_ref[code], 0.0)
    return total


def fin_factor(fin):
    return 0.9 + 0.1 * fin.astype(F32)


def eye_mask(size):
    return lax.broadcasted_iota(jnp.int32, (size, size), 0) == lax.broadcasted_iota(
        jnp.int32, (size, size), 1
    )


def times(matrix, row, eye):
    column = jnp.sum(matrix * row, axis=1, keepdims=True)
    return jnp.sum(jnp.where(eye, column, 0.0), axis=0, keepdims=True)


def times_t(matrix, row, eye):
    column = jnp.sum(jnp.where(eye, row, 0.0), axis=1, keepdims=True)
    return jnp.sum(matrix * column, axis=0, keepdims=True)


def halves(cells):
    shape = (cells // 2, cells)
    return lax.broadcasted_iota(jnp.int32, shape, 0), lax.broadcasted_iota(jnp.int32, shape, 1)


def pack(square):
    middle = square.shape[0] // 2
    row, lane = halves(square.shape[1])
    top, bottom = square[:middle], pltpu.roll(square[middle:], middle, 1)
    return jnp.where(
        (lane >= middle) | (lane < row), top, jnp.where(lane == row, 0.5 * top, bottom)
    )


def unpack(packed, half_diagonal, roll):
    middle, cells = packed.shape
    row, lane = halves(cells)
    top = jnp.where((lane >= middle) | (lane <= row), packed, 0.0)
    bottom = jnp.where(lane - middle > row, roll(packed, middle, 1), 0.0)
    bottom = jnp.where(lane - middle == row, half_diagonal, bottom)
    return jnp.concatenate([top, bottom], axis=0)


def stack_rows(rows, cells):
    at = lax.broadcasted_iota(jnp.int32, (ROWS, cells), 0)
    out = jnp.zeros((ROWS, cells), F32)
    for place, row in enumerate(rows):
        out = jnp.where(at == place, jnp.broadcast_to(row, (ROWS, cells)), out)
    return out


def products(wide, source, faces, g_of, out_ref, ends):
    cells = wide[0].shape[1]
    tiles = range(len(wide))
    total = list(wide)
    for i in range(1, len(source)):
        for j in tiles:
            scaled = wide[j] * faces[i][j : j + 1]
            sh, sl = split(scaled[:cells])
            vh, vl = split(scaled[cells:] + stack_rows([source[i][j : j + 1]], cells))
            gh, gl = split(g_of(i, j))
            zero = jnp.zeros_like(gl)
            both = jnp.dot(
                jnp.concatenate([jnp.concatenate([sh, sl], axis=1), jnp.concatenate([vh, vl], axis=1)], axis=0),
                jnp.concatenate([jnp.concatenate([gh, gl], axis=1), jnp.concatenate([gh, zero], axis=1)], axis=0),
                preferred_element_type=F32,
            )
            wide[j] = both[:, :cells] + both[:, cells:]
            wh, wl = split(wide[j])
            th, tl = split(scaled[:cells].T)
            both = jnp.dot(
                jnp.concatenate([wh, wl], axis=1),
                jnp.concatenate([jnp.concatenate([th, tl], axis=1), jnp.concatenate([th, zero], axis=1)], axis=0),
                preferred_element_type=F32,
            )
            total[j] = total[j] + (both[:, :cells] + both[:, cells:])
    for j in tiles:
        out_ref[j, 0:cells] = wide[j][:cells]
        out_ref[j, cells : 2 * cells] = total[j][:cells]
        out_ref[j, 2 * cells :] = stack_rows(
            [wide[j][cells : cells + 1], total[j][cells : cells + 1]] + [end[j : j + 1] for end in ends], cells
        )


def first_kernel(k_hbm, mat_hbm, fin_hbm, res_hbm, g_hbm, out_ref, coef_ref, g_ref, k_ref, ints, sems):
    blocks, tiles, cells = res_hbm.shape
    half = tiles // 2
    lower = lax.axis_index(AXIS) % 2 == 1
    base = jnp.where(lower, 0, half)
    small = [
        pltpu.make_async_copy(k_hbm, k_ref, sems.at[0]),
        pltpu.make_async_copy(mat_hbm, ints.at[0], sems.at[1]),
        pltpu.make_async_copy(fin_hbm, ints.at[1], sems.at[2]),
        pltpu.make_async_copy(res_hbm, coef_ref.at[pl.ds(0, blocks)], sems.at[3]),
    ]
    large = [
        pltpu.make_async_copy(g_hbm.at[:, pl.ds(start, half)], g_ref.at[:, pl.ds(start, half)], sems.at[4 + n])
        for n, start in enumerate((base, half - base))
    ]
    for copy in small + large:
        copy.start()
    for copy in small:
        copy.wait()
    conduct = [conductivity(ints[0, i], k_ref) for i in range(blocks)]
    factor = [fin_factor(ints[1, i]) for i in range(blocks)]
    faces = [None] + [face(conduct[i], conduct[i - 1], factor[i]) for i in range(1, blocks)]
    ends = [conduct[0], conduct[-1], factor[0]]
    for n, row in enumerate(faces[1:] + ends):
        coef_ref[blocks + n] = row

    def pick(x):
        return jnp.where(lower, x[:half], x[half:])

    source = [pick(coef_ref[i]) for i in range(blocks)]
    eye = eye_mask(cells)
    wide = []
    large[0].wait()
    for j in range(half):
        g0 = g_ref[0, base + j]
        wide.append(jnp.concatenate([g0, stack_rows([times(g0, source[0][j : j + 1], eye)], cells)], axis=0))
    products(
        wide, source, [None] + [pick(f) for f in faces[1:]], lambda i, j: g_ref[i, base + j], out_ref,
        [pick(end) for end in ends],
    )
    large[1].wait()


def second_kernel(coef_ref, g_ref, out_ref):
    blocks, tiles, cells = g_ref.shape[:3]
    half = tiles // 2
    upper = lax.axis_index(AXIS) % 2 == 1
    base = jnp.where(upper, half, 0)

    def pick(n):
        return jnp.where(upper, coef_ref[n, half:], coef_ref[n, :half])

    source = [pick(i) for i in range(blocks)]
    faces = [None] + [pick(blocks + i) for i in range(blocks - 1)]
    eye = eye_mask(cells)
    wide = []
    for j in range(half):
        g0 = g_ref[0, base + j]
        wide.append(jnp.concatenate([g0, stack_rows([times(g0, source[0][j : j + 1], eye)], cells)], axis=0))
    products(
        wide, source, faces, lambda i, j: g_ref[i, base + j], out_ref,
        [pick(2 * blocks - 1 + n) for n in range(3)],
    )


def response_kernel(coef_ref, keep_ref, got_ref, give_ref, gain_ref, g_ref, out_ref, const_ref):
    blocks, tiles, cells = g_ref.shape[:3]
    half = tiles // 2
    is_second = lax.axis_index(AXIS) % 2 == 1
    base = jnp.where(is_second, half, 0)
    eye = jnp.where(eye_mask(cells), 1.0, 0.0)

    def reorder(x):
        return jnp.where(is_second, jnp.concatenate([x[half:], x[:half]], axis=0), x)

    source = [reorder(coef_ref[i]) for i in range(blocks)]
    faces = [None] + [reorder(coef_ref[blocks + i]) for i in range(blocks - 1)]
    nothing = jnp.zeros((cells, cells), F32)
    for group in range(2):
        own_ref, other_ref = (keep_ref, got_ref) if group == 0 else (give_ref, gain_ref)
        start = base if group == 0 else half - base
        lead, tail, values = {}, {}, {}
        for j in range(half):
            own, other = own_ref[j], other_ref[j]
            first = jnp.where(is_second, other, own)
            last = jnp.where(is_second, own, other)
            va, vb = first[2 * cells :], last[2 * cells :]
            between = face(vb[2:3], va[3:4], vb[4:5])
            scaled = jnp.concatenate([first[:cells], stack_rows([va[0:1]], cells)], axis=0) * between
            back = mul(scaled, last[cells : 2 * cells])
            back_const = back[cells:] + stack_rows([vb[1:2]], cells)
            tail[j] = jnp.concatenate(
                [
                    jnp.where(is_second, 0.0, back[:cells] * between),
                    jnp.where(is_second, eye, last[:cells].T * between),
                    jnp.where(is_second, 0.0, back_const * between),
                ],
                axis=0,
            )
            lead[j] = jnp.concatenate(
                [
                    jnp.where(is_second, scaled[:cells], eye),
                    jnp.where(is_second, scaled[cells:], 0.0)
                    + stack_rows([source[0][group * half + j : group * half + j + 1]], cells),
                ],
                axis=0,
            )
        for i in range(blocks):
            for j in range(half):
                values[i, j] = mul(lead[j], g_ref[i, start + j])
                if i < blocks - 1:
                    at = group * half + j
                    scaled = values[i, j] * faces[i + 1][at : at + 1]
                    below = scaled[cells:] + stack_rows([source[i + 1][at : at + 1]], cells)
                    lead[j] = jnp.concatenate([scaled[:cells], below], axis=0)
        for i in reversed(range(blocks)):
            for j in range(half):
                moved = mul(tail[j], g_ref[i, start + j])
                add = jnp.concatenate([values[i, j][:cells], nothing, values[i, j][cells:]], axis=0)
                solved = moved + add
                out_ref[i, start + j] = solved[: 2 * cells]
                const_ref[i, start + j] = solved[2 * cells :]
                if i:
                    at = group * half + j
                    tail[j] = solved * faces[i][at : at + 1]


def merge_kernel(order, keep_ref, got_ref, *rest):
    half, height, cells = keep_ref.shape
    out_refs = rest[-len(order) :]
    here = lax.axis_index(AXIS)
    is_second = here % 2 == 1
    chip = (here % (2 * half)) // 2
    eye = eye_mask(cells)
    first, last, scaled, between, moved, squared = {}, {}, {}, {}, {}, {}
    for d in order:
        keep, got = keep_ref[chip ^ d], got_ref[chip ^ d]
        first[d] = jnp.where(is_second, got, keep)
        last[d] = jnp.where(is_second, keep, got)
        va, vb = first[d][2 * cells :], last[d][2 * cells :]
        between = face(vb[2:3], va[3:4], vb[4:5])
        scaled[d] = jnp.concatenate([first[d][:cells], stack_rows([va[0:1]], cells)], axis=0) * between
    for d in order:
        moved[d] = mul(scaled[d], last[d][:cells])
    for d in order:
        squared[d] = mul(scaled[d], last[d][cells : 2 * cells])
        lower = squared[d][cells:] + stack_rows([last[d][2 * cells + 1 : 2 * cells + 2]], cells)
        squared[d] = jnp.concatenate([squared[d][:cells], lower], axis=0)
    for d in order:
        total = mul(squared[d], scaled[d][:cells].T)
        va, vb = first[d][2 * cells :], last[d][2 * cells :]
        square = first[d][cells : 2 * cells] + total[:cells]
        out_ref = out_refs[order.index(d)]
        out_ref[0:cells] = moved[d][:cells]
        out_ref[cells:-ROWS] = pack(square)
        out_ref[-ROWS:] = stack_rows(
            [
                moved[d][cells : cells + 1] + vb[0:1],
                total[cells : cells + 1] + va[1:2],
                va[2:3],
                vb[3:4],
                va[4:5],
                0.5 * jnp.sum(jnp.where(eye, square, 0.0), axis=0, keepdims=True),
            ],
            cells,
        )


def by_place(parts, chip):
    step = 1
    while step < len(parts):
        swap = (chip & step) != 0
        parts = [jnp.where(swap, parts[d ^ step], parts[d]) for d in range(len(parts))]
        step *= 2
    return parts


def chain_kernel(with_edge, count, *refs):
    refs = refs[1:]
    if with_edge:
        edge_ref, refs = refs[0], refs[1:]
    refs, out_refs = refs[count - 1 :: -1], refs[count:]
    height, cells = refs[0].shape
    chip = (lax.axis_index(AXIS) % (2 * count)) // 2
    eye = eye_mask(cells)

    def column(row):
        return jnp.sum(jnp.where(eye, row, 0.0), axis=1, keepdims=True)

    vectors = by_place([ref[height - ROWS :] for ref in refs], chip)
    maps_t = by_place([ref[0:cells] for ref in refs], chip)
    packed = by_place([ref[cells : height - ROWS] for ref in refs], chip)
    faces = [None] + [
        face(vectors[k][2:3], vectors[k - 1][3:4], vectors[k][4:5]) for k in range(1, count)
    ]
    zero = jnp.zeros((1, cells), F32)
    entering, sideways, arriving = [zero] + [None] * (count - 1), [None] * count, [zero] * count
    leaving = vectors[0][0:1]
    if with_edge:
        entering[0], arriving[-1] = edge_ref[0:1], edge_ref[1:2]
        leaving = leaving + times_t(maps_t[0], entering[0], eye)
    for k in range(1, count):
        entering[k] = faces[k] * leaving
        sideways[k] = column(entering[k])
        if k < count - 1:
            leaving = vectors[k][0:1] + jnp.sum(maps_t[k] * sideways[k], axis=0, keepdims=True)
    carried = arriving[-1] if with_edge else None
    for k in reversed(range(1, count)):
        part = unpack(packed[k], vectors[k][5:6], pltpu.roll)
        square = part + part.T
        if (count - k) % 2:
            terms = square * entering[k]
            if carried is not None:
                terms = terms + maps_t[k] * carried
            carried = column(faces[k]) * (column(vectors[k][1:2]) + jnp.sum(terms, axis=1, keepdims=True))
            arriving[k - 1] = jnp.sum(jnp.where(eye, carried, 0.0), axis=0, keepdims=True)
        else:
            terms = square * sideways[k] + maps_t[k].T * carried
            carried = faces[k] * (vectors[k][1:2] + jnp.sum(terms, axis=0, keepdims=True))
            arriving[k - 1] = carried
    ends = by_place([stack_rows([entering[k], arriving[k]], cells) for k in range(count)], chip)
    for d in range(count):
        out_refs[d][...] = ends[d]


def order_kernel(*refs):
    out_ref = refs[-1]
    count = out_ref.shape[0]
    chip = (lax.axis_index(AXIS) % (2 * count)) // 2
    for d in range(count):
        out_ref[chip ^ d] = refs[count - 1 - d][...]


def finish(ends_ref, start, out_ref, const_ref, put):
    blocks, _, _, cells = out_ref.shape
    eye = eye_mask(cells)
    for j in range(ends_ref.shape[0]):
        up, down = (
            jnp.sum(jnp.where(eye, ends_ref[j, n : n + 1], 0.0), axis=1, keepdims=True) for n in range(2)
        )
        for i in range(blocks):
            both = out_ref[i, start + j, 0:cells] * up + out_ref[i, start + j, cells : 2 * cells] * down
            put(i, j, const_ref[i, start + j, 0:1] + jnp.sum(both, axis=0, keepdims=True))


def own_kernel(mine_ref, out_ref, const_ref, done_ref):
    half = mine_ref.shape[0]

    def put(i, j, row):
        done_ref[i, j : j + 1] = row

    finish(mine_ref, jnp.where(lax.axis_index(AXIS) % 2 == 1, half, 0), out_ref, const_ref, put)


def finish_kernel(theirs_ref, done_ref, phase_ref, out_ref, const_ref, corr_ref, step_ref, rest_ref):
    half = theirs_ref.shape[0]
    is_second = lax.axis_index(AXIS) % 2 == 1

    def put(i, j, row):
        rest_ref[i, j : j + 1] = row

    finish(theirs_ref, jnp.where(is_second, 0, half), out_ref, const_ref, put)
    for i in range(corr_ref.shape[0]):
        own, rest = done_ref[i], rest_ref[i]
        both = jnp.where(
            is_second, jnp.concatenate([rest, own], axis=0), jnp.concatenate([own, rest], axis=0)
        )
        corr_ref[i] = both
        step_ref[i] = both * (1.0 + 2.0 * phase_ref[i].astype(F32))


VMEM = pl.BlockSpec(memory_space=pltpu.VMEM)
HBM = pl.BlockSpec(memory_space=pltpu.HBM)
LIMIT = pltpu.CompilerParams(vmem_limit_bytes=16 << 20)


def cost(flops, moved):
    return pl.CostEstimate(flops=flops, bytes_accessed=moved, transcendentals=0)


def send(x, distance):
    return lax.ppermute(x, AXIS, [(i, i ^ distance) for i in range(lax.axis_size(AXIS))])


def send_all(parts):
    arrived = {0: parts[0]}
    for d in reversed(range(1, len(parts))):
        arrived[d] = send(parts[d], 2 * d)
    return [arrived[d] for d in range(len(parts))]


def exact(left, right):
    return jnp.dot(left, right, precision=lax.Precision.HIGHEST)


def outer_edge(nodes, devices):
    cells = nodes[0].shape[-1]

    def parts(node):
        return node[:cells], node[cells : 2 * cells], node[2 * cells :]

    def widen(node):
        part = unpack(node[cells:-ROWS], node[-3:-2], jnp.roll)
        return jnp.concatenate([node[:cells], part + part.T, node[-ROWS:]], axis=0)

    def join(first, second):
        (ma, qa, va), (mb, qb, vb) = parts(first), parts(second)
        between = face(vb[2], va[3], vb[4])
        scaled, shift = ma * between, va[0] * between
        q = qa + exact(exact(scaled, qb), scaled.T)
        tail = exact(shift, mb) + vb[0]
        lead = va[1] + exact(scaled, exact(qb, shift) + vb[1])
        rest = jnp.zeros((ROWS - 5, cells), F32)
        rows = jnp.stack([tail, lead, va[2], vb[3], va[4]])
        return jnp.concatenate([exact(scaled, mb), q, rows, rest], axis=0)

    groups = lax.axis_size(AXIS) // devices
    whole = functools.reduce(join, [widen(nodes[k]) for k in range(nodes.shape[0])])
    members = [[g * devices + q for g in range(groups)] for q in range(devices)]
    every = lax.all_gather(whole, AXIS, axis=0, axis_index_groups=members)
    split_up = [parts(every[g]) for g in range(groups)]
    faces = [face(b[2][2], a[2][3], b[2][4]) for a, b in zip(split_up[:-1], split_up[1:])]
    entering = [jnp.zeros((cells,), F32)]
    for g in range(groups - 1):
        m, _, v = split_up[g]
        entering.append(faces[g] * (exact(entering[g], m) + v[0]))
    arriving = [jnp.zeros((cells,), F32)]
    for g in reversed(range(1, groups)):
        m, q, v = split_up[g]
        arriving.append(faces[g - 1] * (exact(m, arriving[-1]) + exact(q, entering[g]) + v[1]))
    arriving.reverse()
    own = lax.axis_index(AXIS) // devices
    both = jnp.stack([jnp.stack(entering)[own], jnp.stack(arriving)[own]])
    return jnp.concatenate([both, jnp.zeros((ROWS - 2, cells), F32)], axis=0)


def on_device(block_inverses, residual, material, fin_mask, phase_mask, k_table):
    blocks, tiles, cells = residual.shape
    half = tiles // 2
    height = 2 * cells + ROWS
    map_bytes = 4 * height * cells

    map_shape = (half, height, cells)
    work = cost(24 * half * blocks * cells**3, 8 * half * blocks * cells**2)
    given = [pltpu.with_memory_space_constraint(x, pltpu.HBM) for x in (k_table, material, fin_mask, residual, block_inverses)]
    give, coef, inverses = pl.pallas_call(
        first_kernel,
        out_shape=(
            pltpu.VMEM(map_shape, F32),
            pltpu.VMEM((2 * blocks + 2, tiles, cells), F32),
            pltpu.VMEM(block_inverses.shape, F32),
        ),
        in_specs=[HBM] * 5,
        out_specs=(VMEM,) * 3,
        scratch_shapes=[
            pltpu.SMEM(k_table.shape, F32),
            pltpu.VMEM((2, blocks, tiles, cells), jnp.int32),
            pltpu.SemaphoreType.DMA((6,)),
        ],
        compiler_params=LIMIT,
        cost_estimate=work,
    )(*given)
    got = send(give, 1)
    keep = pl.pallas_call(
        second_kernel,
        out_shape=jax.ShapeDtypeStruct(map_shape, F32),
        in_specs=[VMEM, VMEM],
        out_specs=VMEM,
        compiler_params=LIMIT,
        cost_estimate=work,
    )(coef, inverses)
    gain = send(keep, 1)
    responses, constants = pl.pallas_call(
        response_kernel,
        out_shape=(
            jax.ShapeDtypeStruct((blocks, tiles, 2 * cells, cells), F32),
            jax.ShapeDtypeStruct((blocks, tiles, ROWS, cells), F32),
        ),
        in_specs=[VMEM] * 6,
        out_specs=(VMEM, VMEM),
        compiler_params=LIMIT,
        cost_estimate=cost(48 * tiles * blocks * cells**3, 16 * tiles * blocks * cells**2),
    )(coef, keep, got, give, gain, inverses)
    short = cells + cells // 2 + ROWS
    node = jax.ShapeDtypeStruct((short, cells), F32)

    def join(order, *after):
        return pl.pallas_call(
            functools.partial(merge_kernel, order),
            out_shape=(node,) * len(order),
            in_specs=[VMEM, VMEM] + [pl.BlockSpec(memory_space=pl.ANY)] * len(after),
            out_specs=(VMEM,) * len(order),
            compiler_params=LIMIT,
            cost_estimate=cost(24 * len(order) * cells**3, 3 * len(order) * map_bytes),
        )(keep, got, *after)

    near = list(reversed(range(half - 1)))
    far = join([half - 1])
    joined = [*far, *join(near, *far)][::-1]
    arrived = send_all(joined)
    grouped = lax.axis_size(AXIS) > tiles
    edge = []
    if grouped:
        chip = (lax.axis_index(AXIS) % tiles) // 2
        ordered = jnp.stack(arrived)[jnp.arange(half) ^ chip]
        edge = [outer_edge(ordered, tiles)]
    end = jax.ShapeDtypeStruct((ROWS, cells), F32)
    ends = pl.pallas_call(
        functools.partial(chain_kernel, grouped, half),
        out_shape=(end,) * half,
        in_specs=[pl.BlockSpec(memory_space=pl.ANY)] + [VMEM] * (half + len(edge)),
        out_specs=(VMEM,) * half,
        compiler_params=LIMIT,
        cost_estimate=cost(8 * half * cells**2, half * map_bytes),
    )(constants, *edge, *arrived[::-1])
    ends = send_all(ends)
    mine = pl.pallas_call(
        order_kernel,
        out_shape=jax.ShapeDtypeStruct((half, ROWS, cells), F32),
        in_specs=[VMEM] * half,
        out_specs=VMEM,
        compiler_params=LIMIT,
        cost_estimate=cost(0, 8 * half * ROWS * cells),
    )(*ends[::-1])
    theirs = send(mine, 1)
    half_shape = (blocks, half, cells)
    work = cost(2 * blocks * tiles * cells**2, 4 * blocks * tiles * cells**2)
    done = pl.pallas_call(
        own_kernel,
        out_shape=jax.ShapeDtypeStruct(half_shape, F32),
        in_specs=[VMEM] * 3,
        out_specs=VMEM,
        compiler_params=LIMIT,
        cost_estimate=work,
    )(mine, responses, constants)
    shape = jax.ShapeDtypeStruct((blocks, tiles, cells), F32)
    return pl.pallas_call(
        finish_kernel,
        out_shape=(shape, shape),
        in_specs=[VMEM] * 5,
        out_specs=(VMEM, VMEM),
        scratch_shapes=[pltpu.VMEM(half_shape, F32)],
        compiler_params=LIMIT,
        cost_estimate=work,
    )(theirs, done, phase_mask, responses, constants)


def solution(mesh):
    return jax.shard_map(
        on_device,
        mesh=mesh,
        in_specs=(
            P("gx", "pa", None, None),
            P("gx", "pa", None),
            P("gx", "pa", None),
            P("gx", "pa", None),
            P("gx", "pa", None),
            P(),
        ),
        out_specs=(P("gx", "pa", None), P("gx", "pa", None)),
        check_vma=False,
    )
```

```python
import functools

import jax
import jax.numpy as jnp
from jax import lax
from jax.experimental import pallas as pl
from jax.experimental.pallas import tpu as pltpu
from jax.sharding import PartitionSpec as P

BF16 = jnp.bfloat16
F32 = jnp.float32
ROWS = 8
AXIS = "gx"


def split(x):
    high = x.astype(BF16)
    return high, (x - high.astype(F32)).astype(BF16)


def mul(left, right):
    lh, ll = split(left)
    rh, rl = split(right)
    lhs = jnp.concatenate([lh, ll], axis=1)
    rhs = jnp.concatenate(
        [jnp.concatenate([rh, rl], axis=1), jnp.concatenate([rh, jnp.zeros_like(rl)], axis=1)], axis=0
    )
    both = jnp.dot(lhs, rhs, preferred_element_type=F32)
    width = right.shape[1]
    return both[:, :width] + both[:, width:]


def mul_t(left, right):
    lh, ll = split(left)
    rh, rl = split(right)
    lhs = jnp.concatenate([lh, ll], axis=1)
    rhs = jnp.concatenate(
        [jnp.concatenate([rh, rh], axis=1), jnp.concatenate([rl, jnp.zeros_like(rl)], axis=1)], axis=0
    )
    both = lax.dot_general(lhs, rhs, (((1,), (1,)), ((), ())), preferred_element_type=F32)
    width = right.shape[0]
    return both[:, :width] + both[:, width:]


def face(conduct, earlier, fin_factor):
    return 2.0 * conduct * earlier / (conduct + earlier) * fin_factor


def conductivity(material, k_ref):
    total = jnp.zeros(material.shape, F32)
    for code in range(k_ref.shape[0]):
        total = total + jnp.where(material == code, k_ref[code], 0.0)
    return total


def fin_factor(fin):
    return 0.9 + 0.1 * fin.astype(F32)


def eye_mask(size):
    return lax.broadcasted_iota(jnp.int32, (size, size), 0) == lax.broadcasted_iota(
        jnp.int32, (size, size), 1
    )


def times(matrix, row, eye):
    column = jnp.sum(matrix * row, axis=1, keepdims=True)
    return jnp.sum(jnp.where(eye, column, 0.0), axis=0, keepdims=True)


def times_t(matrix, row, eye):
    column = jnp.sum(jnp.where(eye, row, 0.0), axis=1, keepdims=True)
    return jnp.sum(matrix * column, axis=0, keepdims=True)


def halves(cells):
    shape = (cells // 2, cells)
    return lax.broadcasted_iota(jnp.int32, shape, 0), lax.broadcasted_iota(jnp.int32, shape, 1)


def pack(square):
    middle = square.shape[0] // 2
    row, lane = halves(square.shape[1])
    top, bottom = square[:middle], pltpu.roll(square[middle:], middle, 1)
    return jnp.where(
        (lane >= middle) | (lane < row), top, jnp.where(lane == row, 0.5 * top, bottom)
    )


def unpack(packed, half_diagonal, roll):
    middle, cells = packed.shape
    row, lane = halves(cells)
    top = jnp.where((lane >= middle) | (lane <= row), packed, 0.0)
    bottom = jnp.where(lane - middle > row, roll(packed, middle, 1), 0.0)
    bottom = jnp.where(lane - middle == row, half_diagonal, bottom)
    return jnp.concatenate([top, bottom], axis=0)


def stack_rows(rows, cells):
    at = lax.broadcasted_iota(jnp.int32, (ROWS, cells), 0)
    out = jnp.zeros((ROWS, cells), F32)
    for place, row in enumerate(rows):
        out = jnp.where(at == place, jnp.broadcast_to(row, (ROWS, cells)), out)
    return out


def products(wide, source, faces, g_of, out_ref, ends):
    cells = wide[0].shape[1]
    tiles = range(len(wide))
    total = list(wide)
    for i in range(1, len(source)):
        for j in tiles:
            scaled = wide[j] * faces[i][j : j + 1]
            sh, sl = split(scaled[:cells])
            vh, vl = split(scaled[cells:] + stack_rows([source[i][j : j + 1]], cells))
            gh, gl = split(g_of(i, j))
            zero = jnp.zeros_like(gl)
            both = jnp.dot(
                jnp.concatenate([jnp.concatenate([sh, sl], axis=1), jnp.concatenate([vh, vl], axis=1)], axis=0),
                jnp.concatenate([jnp.concatenate([gh, gl], axis=1), jnp.concatenate([gh, zero], axis=1)], axis=0),
                preferred_element_type=F32,
            )
            wide[j] = both[:, :cells] + both[:, cells:]
            wh, wl = split(wide[j])
            th, tl = split(scaled[:cells].T)
            both = jnp.dot(
                jnp.concatenate([wh, wl], axis=1),
                jnp.concatenate([jnp.concatenate([th, tl], axis=1), jnp.concatenate([th, zero], axis=1)], axis=0),
                preferred_element_type=F32,
            )
            total[j] = total[j] + (both[:, :cells] + both[:, cells:])
    for j in tiles:
        out_ref[j, 0:cells] = wide[j][:cells]
        out_ref[j, cells : 2 * cells] = total[j][:cells]
        out_ref[j, 2 * cells :] = stack_rows(
            [wide[j][cells : cells + 1], total[j][cells : cells + 1]] + [end[j : j + 1] for end in ends], cells
        )


def first_kernel(k_hbm, mat_hbm, fin_hbm, res_hbm, g_hbm, out_ref, coef_ref, g_ref, k_ref, ints, sems):
    blocks, tiles, cells = res_hbm.shape
    half = tiles // 2
    lower = lax.axis_index(AXIS) % 2 == 1
    base = jnp.where(lower, 0, half)
    small = [
        pltpu.make_async_copy(k_hbm, k_ref, sems.at[0]),
        pltpu.make_async_copy(mat_hbm, ints.at[0], sems.at[1]),
        pltpu.make_async_copy(fin_hbm, ints.at[1], sems.at[2]),
        pltpu.make_async_copy(res_hbm, coef_ref.at[pl.ds(0, blocks)], sems.at[3]),
    ]
    large = [
        pltpu.make_async_copy(g_hbm.at[:, pl.ds(start, half)], g_ref.at[:, pl.ds(start, half)], sems.at[4 + n])
        for n, start in enumerate((base, half - base))
    ]
    for copy in small + large:
        copy.start()
    for copy in small:
        copy.wait()
    conduct = [conductivity(ints[0, i], k_ref) for i in range(blocks)]
    factor = [fin_factor(ints[1, i]) for i in range(blocks)]
    faces = [None] + [face(conduct[i], conduct[i - 1], factor[i]) for i in range(1, blocks)]
    ends = [conduct[0], conduct[-1], factor[0]]
    for n, row in enumerate(faces[1:] + ends):
        coef_ref[blocks + n] = row

    def pick(x):
        return jnp.where(lower, x[:half], x[half:])

    source = [pick(coef_ref[i]) for i in range(blocks)]
    eye = eye_mask(cells)
    wide = []
    large[0].wait()
    for j in range(half):
        g0 = g_ref[0, base + j]
        wide.append(jnp.concatenate([g0, stack_rows([times(g0, source[0][j : j + 1], eye)], cells)], axis=0))
    products(
        wide, source, [None] + [pick(f) for f in faces[1:]], lambda i, j: g_ref[i, base + j], out_ref,
        [pick(end) for end in ends],
    )
    large[1].wait()


def second_kernel(coef_ref, g_ref, out_ref):
    blocks, tiles, cells = g_ref.shape[:3]
    half = tiles // 2
    upper = lax.axis_index(AXIS) % 2 == 1
    base = jnp.where(upper, half, 0)

    def pick(n):
        return jnp.where(upper, coef_ref[n, half:], coef_ref[n, :half])

    source = [pick(i) for i in range(blocks)]
    faces = [None] + [pick(blocks + i) for i in range(blocks - 1)]
    eye = eye_mask(cells)
    wide = []
    for j in range(half):
        g0 = g_ref[0, base + j]
        wide.append(jnp.concatenate([g0, stack_rows([times(g0, source[0][j : j + 1], eye)], cells)], axis=0))
    products(
        wide, source, faces, lambda i, j: g_ref[i, base + j], out_ref,
        [pick(2 * blocks - 1 + n) for n in range(3)],
    )


def response_kernel(coef_ref, keep_ref, got_ref, give_ref, gain_ref, g_ref, out_ref, const_ref):
    blocks, tiles, cells = g_ref.shape[:3]
    half = tiles // 2
    is_second = lax.axis_index(AXIS) % 2 == 1
    base = jnp.where(is_second, half, 0)
    eye = jnp.where(eye_mask(cells), 1.0, 0.0)

    def reorder(x):
        return jnp.where(is_second, jnp.concatenate([x[half:], x[:half]], axis=0), x)

    source = [reorder(coef_ref[i]) for i in range(blocks)]
    faces = [None] + [reorder(coef_ref[blocks + i]) for i in range(blocks - 1)]
    nothing = jnp.zeros((cells, cells), F32)
    for group in range(2):
        own_ref, other_ref = (keep_ref, got_ref) if group == 0 else (give_ref, gain_ref)
        start = base if group == 0 else half - base
        lead, tail, values = {}, {}, {}
        for j in range(half):
            own, other = own_ref[j], other_ref[j]
            first = jnp.where(is_second, other, own)
            last = jnp.where(is_second, own, other)
            va, vb = first[2 * cells :], last[2 * cells :]
            between = face(vb[2:3], va[3:4], vb[4:5])
            scaled = jnp.concatenate([first[:cells], stack_rows([va[0:1]], cells)], axis=0) * between
            back = mul(scaled, last[cells : 2 * cells])
            back_const = back[cells:] + stack_rows([vb[1:2]], cells)
            tail[j] = jnp.concatenate(
                [
                    jnp.where(is_second, 0.0, back[:cells] * between),
                    jnp.where(is_second, eye, last[:cells].T * between),
                    jnp.where(is_second, 0.0, back_const * between),
                ],
                axis=0,
            )
            lead[j] = jnp.concatenate(
                [
                    jnp.where(is_second, scaled[:cells], eye),
                    jnp.where(is_second, scaled[cells:], 0.0)
                    + stack_rows([source[0][group * half + j : group * half + j + 1]], cells),
                ],
                axis=0,
            )
        for i in range(blocks):
            for j in range(half):
                values[i, j] = mul(lead[j], g_ref[i, start + j])
                if i < blocks - 1:
                    at = group * half + j
                    scaled = values[i, j] * faces[i + 1][at : at + 1]
                    below = scaled[cells:] + stack_rows([source[i + 1][at : at + 1]], cells)
                    lead[j] = jnp.concatenate([scaled[:cells], below], axis=0)
        for i in reversed(range(blocks)):
            for j in range(half):
                moved = mul(tail[j], g_ref[i, start + j])
                add = jnp.concatenate([values[i, j][:cells], nothing, values[i, j][cells:]], axis=0)
                solved = moved + add
                out_ref[i, start + j] = solved[: 2 * cells]
                const_ref[i, start + j] = solved[2 * cells :]
                if i:
                    at = group * half + j
                    tail[j] = solved * faces[i][at : at + 1]


def merge_kernel(order, keep_ref, got_ref, *rest):
    half, height, cells = keep_ref.shape
    out_refs = rest[-len(order) :]
    here = lax.axis_index(AXIS)
    is_second = here % 2 == 1
    chip = (here % (2 * half)) // 2
    eye = eye_mask(cells)
    first, last, scaled, between, moved, squared = {}, {}, {}, {}, {}, {}
    for d in order:
        keep, got = keep_ref[chip ^ d], got_ref[chip ^ d]
        first[d] = jnp.where(is_second, got, keep)
        last[d] = jnp.where(is_second, keep, got)
        va, vb = first[d][2 * cells :], last[d][2 * cells :]
        between = face(vb[2:3], va[3:4], vb[4:5])
        scaled[d] = jnp.concatenate([first[d][:cells], stack_rows([va[0:1]], cells)], axis=0) * between
    for d in order:
        moved[d] = mul(scaled[d], last[d][:cells])
    for d in order:
        squared[d] = mul(scaled[d], last[d][cells : 2 * cells])
        lower = squared[d][cells:] + stack_rows([last[d][2 * cells + 1 : 2 * cells + 2]], cells)
        squared[d] = jnp.concatenate([squared[d][:cells], lower], axis=0)
    for d in order:
        total = mul(squared[d], scaled[d][:cells].T)
        va, vb = first[d][2 * cells :], last[d][2 * cells :]
        square = first[d][cells : 2 * cells] + total[:cells]
        out_ref = out_refs[order.index(d)]
        out_ref[0:cells] = moved[d][:cells]
        out_ref[cells:-ROWS] = pack(square)
        out_ref[-ROWS:] = stack_rows(
            [
                moved[d][cells : cells + 1] + vb[0:1],
                total[cells : cells + 1] + va[1:2],
                va[2:3],
                vb[3:4],
                va[4:5],
                0.5 * jnp.sum(jnp.where(eye, square, 0.0), axis=0, keepdims=True),
            ],
            cells,
        )


def by_place(parts, chip):
    step = 1
    while step < len(parts):
        swap = (chip & step) != 0
        parts = [jnp.where(swap, parts[d ^ step], parts[d]) for d in range(len(parts))]
        step *= 2
    return parts


def chain_kernel(with_edge, count, *refs):
    refs = refs[1:]
    if with_edge:
        edge_ref, refs = refs[0], refs[1:]
    refs, out_refs = refs[count - 1 :: -1], refs[count:]
    height, cells = refs[0].shape
    chip = (lax.axis_index(AXIS) % (2 * count)) // 2
    eye = eye_mask(cells)

    def column(row):
        return jnp.sum(jnp.where(eye, row, 0.0), axis=1, keepdims=True)

    vectors = by_place([ref[height - ROWS :] for ref in refs], chip)
    maps_t = by_place([ref[0:cells] for ref in refs], chip)
    packed = by_place([ref[cells : height - ROWS] for ref in refs], chip)
    faces = [None] + [
        face(vectors[k][2:3], vectors[k - 1][3:4], vectors[k][4:5]) for k in range(1, count)
    ]
    zero = jnp.zeros((1, cells), F32)
    entering, sideways, arriving = [zero] + [None] * (count - 1), [None] * count, [zero] * count
    leaving = vectors[0][0:1]
    if with_edge:
        entering[0], arriving[-1] = edge_ref[0:1], edge_ref[1:2]
        leaving = leaving + times_t(maps_t[0], entering[0], eye)
    for k in range(1, count):
        entering[k] = faces[k] * leaving
        sideways[k] = column(entering[k])
        if k < count - 1:
            leaving = vectors[k][0:1] + jnp.sum(maps_t[k] * sideways[k], axis=0, keepdims=True)
    carried = arriving[-1] if with_edge else None
    for k in reversed(range(1, count)):
        part = unpack(packed[k], vectors[k][5:6], pltpu.roll)
        square = part + part.T
        if (count - k) % 2:
            terms = square * entering[k]
            if carried is not None:
                terms = terms + maps_t[k] * carried
            carried = column(faces[k]) * (column(vectors[k][1:2]) + jnp.sum(terms, axis=1, keepdims=True))
            arriving[k - 1] = jnp.sum(jnp.where(eye, carried, 0.0), axis=0, keepdims=True)
        else:
            terms = square * sideways[k] + maps_t[k].T * carried
            carried = faces[k] * (vectors[k][1:2] + jnp.sum(terms, axis=0, keepdims=True))
            arriving[k - 1] = carried
    ends = by_place([stack_rows([entering[k], arriving[k]], cells) for k in range(count)], chip)
    for d in range(count):
        out_refs[d][...] = ends[d]


def order_kernel(*refs):
    out_ref = refs[-1]
    count = out_ref.shape[0]
    chip = (lax.axis_index(AXIS) % (2 * count)) // 2
    for d in range(count):
        out_ref[chip ^ d] = refs[count - 1 - d][...]


def finish(ends_ref, start, out_ref, const_ref, put):
    blocks, _, _, cells = out_ref.shape
    eye = eye_mask(cells)
    for j in range(ends_ref.shape[0]):
        up, down = (
            jnp.sum(jnp.where(eye, ends_ref[j, n : n + 1], 0.0), axis=1, keepdims=True) for n in range(2)
        )
        for i in range(blocks):
            both = out_ref[i, start + j, 0:cells] * up + out_ref[i, start + j, cells : 2 * cells] * down
            put(i, j, const_ref[i, start + j, 0:1] + jnp.sum(both, axis=0, keepdims=True))


def own_kernel(mine_ref, out_ref, const_ref, done_ref):
    half = mine_ref.shape[0]

    def put(i, j, row):
        done_ref[i, j : j + 1] = row

    finish(mine_ref, jnp.where(lax.axis_index(AXIS) % 2 == 1, half, 0), out_ref, const_ref, put)


def finish_kernel(theirs_ref, done_ref, phase_ref, out_ref, const_ref, corr_ref, step_ref, rest_ref):
    half = theirs_ref.shape[0]
    is_second = lax.axis_index(AXIS) % 2 == 1

    def put(i, j, row):
        rest_ref[i, j : j + 1] = row

    finish(theirs_ref, jnp.where(is_second, 0, half), out_ref, const_ref, put)
    for i in range(corr_ref.shape[0]):
        own, rest = done_ref[i], rest_ref[i]
        both = jnp.where(
            is_second, jnp.concatenate([rest, own], axis=0), jnp.concatenate([own, rest], axis=0)
        )
        corr_ref[i] = both
        step_ref[i] = both * (1.0 + 2.0 * phase_ref[i].astype(F32))


VMEM = pl.BlockSpec(memory_space=pltpu.VMEM)
HBM = pl.BlockSpec(memory_space=pltpu.HBM)
LIMIT = pltpu.CompilerParams(vmem_limit_bytes=16 << 20)


def cost(flops, moved):
    return pl.CostEstimate(flops=flops, bytes_accessed=moved, transcendentals=0)


def send(x, distance):
    return lax.ppermute(x, AXIS, [(i, i ^ distance) for i in range(lax.axis_size(AXIS))])


def send_all(parts):
    arrived = {0: parts[0]}
    for d in reversed(range(1, len(parts))):
        arrived[d] = send(parts[d], 2 * d)
    return [arrived[d] for d in range(len(parts))]


def exact(left, right):
    return jnp.dot(left, right, precision=lax.Precision.HIGHEST)


def outer_edge(nodes, devices):
    cells = nodes[0].shape[-1]

    def parts(node):
        return node[:cells], node[cells : 2 * cells], node[2 * cells :]

    def widen(node):
        part = unpack(node[cells:-ROWS], node[-3:-2], jnp.roll)
        return jnp.concatenate([node[:cells], part + part.T, node[-ROWS:]], axis=0)

    def join(first, second):
        (ma, qa, va), (mb, qb, vb) = parts(first), parts(second)
        between = face(vb[2], va[3], vb[4])
        scaled, shift = ma * between, va[0] * between
        q = qa + exact(exact(scaled, qb), scaled.T)
        tail = exact(shift, mb) + vb[0]
        lead = va[1] + exact(scaled, exact(qb, shift) + vb[1])
        rest = jnp.zeros((ROWS - 5, cells), F32)
        rows = jnp.stack([tail, lead, va[2], vb[3], va[4]])
        return jnp.concatenate([exact(scaled, mb), q, rows, rest], axis=0)

    groups = lax.axis_size(AXIS) // devices
    whole = functools.reduce(join, [widen(nodes[k]) for k in range(nodes.shape[0])])
    members = [[g * devices + q for g in range(groups)] for q in range(devices)]
    every = lax.all_gather(whole, AXIS, axis=0, axis_index_groups=members)
    split_up = [parts(every[g]) for g in range(groups)]
    faces = [face(b[2][2], a[2][3], b[2][4]) for a, b in zip(split_up[:-1], split_up[1:])]
    entering = [jnp.zeros((cells,), F32)]
    for g in range(groups - 1):
        m, _, v = split_up[g]
        entering.append(faces[g] * (exact(entering[g], m) + v[0]))
    arriving = [jnp.zeros((cells,), F32)]
    for g in reversed(range(1, groups)):
        m, q, v = split_up[g]
        arriving.append(faces[g - 1] * (exact(m, arriving[-1]) + exact(q, entering[g]) + v[1]))
    arriving.reverse()
    own = lax.axis_index(AXIS) // devices
    both = jnp.stack([jnp.stack(entering)[own], jnp.stack(arriving)[own]])
    return jnp.concatenate([both, jnp.zeros((ROWS - 2, cells), F32)], axis=0)


def on_device(block_inverses, residual, material, fin_mask, phase_mask, k_table):
    blocks, tiles, cells = residual.shape
    half = tiles // 2
    height = 2 * cells + ROWS
    map_bytes = 4 * height * cells

    map_shape = (half, height, cells)
    work = cost(24 * half * blocks * cells**3, 8 * half * blocks * cells**2)
    given = [pltpu.with_memory_space_constraint(x, pltpu.HBM) for x in (k_table, material, fin_mask, residual, block_inverses)]
    give, coef, inverses = pl.pallas_call(
        first_kernel,
        out_shape=(
            pltpu.VMEM(map_shape, F32),
            pltpu.VMEM((2 * blocks + 2, tiles, cells), F32),
            pltpu.VMEM(block_inverses.shape, F32),
        ),
        in_specs=[HBM] * 5,
        out_specs=(VMEM,) * 3,
        scratch_shapes=[
            pltpu.SMEM(k_table.shape, F32),
            pltpu.VMEM((2, blocks, tiles, cells), jnp.int32),
            pltpu.SemaphoreType.DMA((6,)),
        ],
        compiler_params=LIMIT,
        cost_estimate=work,
    )(*given)
    got = send(give, 1)
    keep = pl.pallas_call(
        second_kernel,
        out_shape=jax.ShapeDtypeStruct(map_shape, F32),
        in_specs=[VMEM, VMEM],
        out_specs=VMEM,
        compiler_params=LIMIT,
        cost_estimate=work,
    )(coef, inverses)
    gain = send(keep, 1)
    responses, constants = pl.pallas_call(
        response_kernel,
        out_shape=(
            jax.ShapeDtypeStruct((blocks, tiles, 2 * cells, cells), F32),
            jax.ShapeDtypeStruct((blocks, tiles, ROWS, cells), F32),
        ),
        in_specs=[VMEM] * 6,
        out_specs=(VMEM, VMEM),
        compiler_params=LIMIT,
        cost_estimate=cost(48 * tiles * blocks * cells**3, 16 * tiles * blocks * cells**2),
    )(coef, keep, got, give, gain, inverses)
    short = cells + cells // 2 + ROWS
    node = jax.ShapeDtypeStruct((short, cells), F32)

    def join(order, *after):
        return pl.pallas_call(
            functools.partial(merge_kernel, order),
            out_shape=(node,) * len(order),
            in_specs=[VMEM, VMEM] + [pl.BlockSpec(memory_space=pl.ANY)] * len(after),
            out_specs=(VMEM,) * len(order),
            compiler_params=LIMIT,
            cost_estimate=cost(24 * len(order) * cells**3, 3 * len(order) * map_bytes),
        )(keep, got, *after)

    far = join([half - 1])
    near = join(list(reversed(range(1, half - 1))), *far)
    joined = [*join([0], *near[:1]), *near[::-1], *far]
    arrived = send_all(joined)
    grouped = lax.axis_size(AXIS) > tiles
    edge = []
    if grouped:
        chip = (lax.axis_index(AXIS) % tiles) // 2
        ordered = jnp.stack(arrived)[jnp.arange(half) ^ chip]
        edge = [outer_edge(ordered, tiles)]
    end = jax.ShapeDtypeStruct((ROWS, cells), F32)
    ends = pl.pallas_call(
        functools.partial(chain_kernel, grouped, half),
        out_shape=(end,) * half,
        in_specs=[pl.BlockSpec(memory_space=pl.ANY)] + [VMEM] * (half + len(edge)),
        out_specs=(VMEM,) * half,
        compiler_params=LIMIT,
        cost_estimate=cost(8 * half * cells**2, half * map_bytes),
    )(constants, *edge, *arrived[::-1])
    ends = send_all(ends)
    mine = pl.pallas_call(
        order_kernel,
        out_shape=jax.ShapeDtypeStruct((half, ROWS, cells), F32),
        in_specs=[VMEM] * half,
        out_specs=VMEM,
        compiler_params=LIMIT,
        cost_estimate=cost(0, 8 * half * ROWS * cells),
    )(*ends[::-1])
    theirs = send(mine, 1)
    half_shape = (blocks, half, cells)
    work = cost(2 * blocks * tiles * cells**2, 4 * blocks * tiles * cells**2)
    done = pl.pallas_call(
        own_kernel,
        out_shape=jax.ShapeDtypeStruct(half_shape, F32),
        in_specs=[VMEM] * 3,
        out_specs=VMEM,
        compiler_params=LIMIT,
        cost_estimate=work,
    )(mine, responses, constants)
    shape = jax.ShapeDtypeStruct((blocks, tiles, cells), F32)
    return pl.pallas_call(
        finish_kernel,
        out_shape=(shape, shape),
        in_specs=[VMEM] * 5,
        out_specs=(VMEM, VMEM),
        scratch_shapes=[pltpu.VMEM(half_shape, F32)],
        compiler_params=LIMIT,
        cost_estimate=work,
    )(theirs, done, phase_mask, responses, constants)


def solution(mesh):
    return jax.shard_map(
        on_device,
        mesh=mesh,
        in_specs=(
            P("gx", "pa", None, None),
            P("gx", "pa", None),
            P("gx", "pa", None),
            P("gx", "pa", None),
            P("gx", "pa", None),
            P(),
        ),
        out_specs=(P("gx", "pa", None), P("gx", "pa", None)),
        check_vma=False,
    )
```

```python
import functools

import jax
import jax.numpy as jnp
from jax import lax
from jax.experimental import pallas as pl
from jax.experimental.pallas import tpu as pltpu
from jax.sharding import PartitionSpec as P

BF16 = jnp.bfloat16
F32 = jnp.float32
ROWS = 8
AXIS = "gx"


def split(x):
    high = x.astype(BF16)
    return high, (x - high.astype(F32)).astype(BF16)


def mul(left, right):
    lh, ll = split(left)
    rh, rl = split(right)
    lhs = jnp.concatenate([lh, ll], axis=1)
    rhs = jnp.concatenate(
        [jnp.concatenate([rh, rl], axis=1), jnp.concatenate([rh, jnp.zeros_like(rl)], axis=1)], axis=0
    )
    both = jnp.dot(lhs, rhs, preferred_element_type=F32)
    width = right.shape[1]
    return both[:, :width] + both[:, width:]


def mul_t(left, right):
    lh, ll = split(left)
    rh, rl = split(right)
    lhs = jnp.concatenate([lh, ll], axis=1)
    rhs = jnp.concatenate(
        [jnp.concatenate([rh, rh], axis=1), jnp.concatenate([rl, jnp.zeros_like(rl)], axis=1)], axis=0
    )
    both = lax.dot_general(lhs, rhs, (((1,), (1,)), ((), ())), preferred_element_type=F32)
    width = right.shape[0]
    return both[:, :width] + both[:, width:]


def face(conduct, earlier, fin_factor):
    return 2.0 * conduct * earlier / (conduct + earlier) * fin_factor


def conductivity(material, k_ref):
    total = jnp.zeros(material.shape, F32)
    for code in range(k_ref.shape[0]):
        total = total + jnp.where(material == code, k_ref[code], 0.0)
    return total


def fin_factor(fin):
    return 0.9 + 0.1 * fin.astype(F32)


def eye_mask(size):
    return lax.broadcasted_iota(jnp.int32, (size, size), 0) == lax.broadcasted_iota(
        jnp.int32, (size, size), 1
    )


def times(matrix, row, eye):
    column = jnp.sum(matrix * row, axis=1, keepdims=True)
    return jnp.sum(jnp.where(eye, column, 0.0), axis=0, keepdims=True)


def times_t(matrix, row, eye):
    column = jnp.sum(jnp.where(eye, row, 0.0), axis=1, keepdims=True)
    return jnp.sum(matrix * column, axis=0, keepdims=True)


def halves(cells):
    shape = (cells // 2, cells)
    return lax.broadcasted_iota(jnp.int32, shape, 0), lax.broadcasted_iota(jnp.int32, shape, 1)


def pack(square):
    middle = square.shape[0] // 2
    row, lane = halves(square.shape[1])
    top, bottom = square[:middle], pltpu.roll(square[middle:], middle, 1)
    return jnp.where(
        (lane >= middle) | (lane < row), top, jnp.where(lane == row, 0.5 * top, bottom)
    )


def unpack(packed, half_diagonal, roll):
    middle, cells = packed.shape
    row, lane = halves(cells)
    top = jnp.where((lane >= middle) | (lane <= row), packed, 0.0)
    bottom = jnp.where(lane - middle > row, roll(packed, middle, 1), 0.0)
    bottom = jnp.where(lane - middle == row, half_diagonal, bottom)
    return jnp.concatenate([top, bottom], axis=0)


def stack_rows(rows, cells):
    at = lax.broadcasted_iota(jnp.int32, (ROWS, cells), 0)
    out = jnp.zeros((ROWS, cells), F32)
    for place, row in enumerate(rows):
        out = jnp.where(at == place, jnp.broadcast_to(row, (ROWS, cells)), out)
    return out


def products(wide, source, faces, g_of, out_ref, ends):
    cells = wide[0].shape[1]
    tiles = range(len(wide))
    total = list(wide)
    for i in range(1, len(source)):
        for j in tiles:
            scaled = wide[j] * faces[i][j : j + 1]
            sh, sl = split(scaled[:cells])
            vh, vl = split(scaled[cells:] + stack_rows([source[i][j : j + 1]], cells))
            gh, gl = split(g_of(i, j))
            zero = jnp.zeros_like(gl)
            both = jnp.dot(
                jnp.concatenate([jnp.concatenate([sh, sl], axis=1), jnp.concatenate([vh, vl], axis=1)], axis=0),
                jnp.concatenate([jnp.concatenate([gh, gl], axis=1), jnp.concatenate([gh, zero], axis=1)], axis=0),
                preferred_element_type=F32,
            )
            wide[j] = both[:, :cells] + both[:, cells:]
            wh, wl = split(wide[j])
            th, tl = split(scaled[:cells].T)
            both = jnp.dot(
                jnp.concatenate([wh, wl], axis=1),
                jnp.concatenate([jnp.concatenate([th, tl], axis=1), jnp.concatenate([th, zero], axis=1)], axis=0),
                preferred_element_type=F32,
            )
            total[j] = total[j] + (both[:, :cells] + both[:, cells:])
    for j in tiles:
        out_ref[j, 0:cells] = wide[j][:cells]
        out_ref[j, cells : 2 * cells] = total[j][:cells]
        out_ref[j, 2 * cells :] = stack_rows(
            [wide[j][cells : cells + 1], total[j][cells : cells + 1]] + [end[j : j + 1] for end in ends], cells
        )


def first_kernel(k_hbm, mat_hbm, fin_hbm, res_hbm, g_hbm, out_ref, coef_ref, g_ref, k_ref, ints, sems):
    blocks, tiles, cells = res_hbm.shape
    half = tiles // 2
    lower = lax.axis_index(AXIS) % 2 == 1
    base = jnp.where(lower, 0, half)
    small = [
        pltpu.make_async_copy(k_hbm, k_ref, sems.at[0]),
        pltpu.make_async_copy(mat_hbm, ints.at[0], sems.at[1]),
        pltpu.make_async_copy(fin_hbm, ints.at[1], sems.at[2]),
        pltpu.make_async_copy(res_hbm, coef_ref.at[pl.ds(0, blocks)], sems.at[3]),
    ]
    large = [
        pltpu.make_async_copy(g_hbm.at[:, pl.ds(start, half)], g_ref.at[:, pl.ds(start, half)], sems.at[4 + n])
        for n, start in enumerate((base, half - base))
    ]
    for copy in small + large:
        copy.start()
    for copy in small:
        copy.wait()
    conduct = [conductivity(ints[0, i], k_ref) for i in range(blocks)]
    factor = [fin_factor(ints[1, i]) for i in range(blocks)]
    faces = [None] + [face(conduct[i], conduct[i - 1], factor[i]) for i in range(1, blocks)]
    ends = [conduct[0], conduct[-1], factor[0]]
    for n, row in enumerate(faces[1:] + ends):
        coef_ref[blocks + n] = row

    def pick(x):
        return jnp.where(lower, x[:half], x[half:])

    source = [pick(coef_ref[i]) for i in range(blocks)]
    eye = eye_mask(cells)
    wide = []
    large[0].wait()
    for j in range(half):
        g0 = g_ref[0, base + j]
        wide.append(jnp.concatenate([g0, stack_rows([times(g0, source[0][j : j + 1], eye)], cells)], axis=0))
    products(
        wide, source, [None] + [pick(f) for f in faces[1:]], lambda i, j: g_ref[i, base + j], out_ref,
        [pick(end) for end in ends],
    )
    large[1].wait()


def second_kernel(coef_ref, g_ref, out_ref):
    blocks, tiles, cells = g_ref.shape[:3]
    half = tiles // 2
    upper = lax.axis_index(AXIS) % 2 == 1
    base = jnp.where(upper, half, 0)

    def pick(n):
        return jnp.where(upper, coef_ref[n, half:], coef_ref[n, :half])

    source = [pick(i) for i in range(blocks)]
    faces = [None] + [pick(blocks + i) for i in range(blocks - 1)]
    eye = eye_mask(cells)
    wide = []
    for j in range(half):
        g0 = g_ref[0, base + j]
        wide.append(jnp.concatenate([g0, stack_rows([times(g0, source[0][j : j + 1], eye)], cells)], axis=0))
    products(
        wide, source, faces, lambda i, j: g_ref[i, base + j], out_ref,
        [pick(2 * blocks - 1 + n) for n in range(3)],
    )


def response_kernel(coef_ref, keep_ref, got_ref, give_ref, gain_ref, g_ref, out_ref, const_ref):
    blocks, tiles, cells = g_ref.shape[:3]
    half = tiles // 2
    is_second = lax.axis_index(AXIS) % 2 == 1
    base = jnp.where(is_second, half, 0)
    eye = jnp.where(eye_mask(cells), 1.0, 0.0)

    def reorder(x):
        return jnp.where(is_second, jnp.concatenate([x[half:], x[:half]], axis=0), x)

    source = [reorder(coef_ref[i]) for i in range(blocks)]
    faces = [None] + [reorder(coef_ref[blocks + i]) for i in range(blocks - 1)]
    nothing = jnp.zeros((cells, cells), F32)
    for group in range(2):
        own_ref, other_ref = (keep_ref, got_ref) if group == 0 else (give_ref, gain_ref)
        start = base if group == 0 else half - base
        lead, tail, values = {}, {}, {}
        for j in range(half):
            own, other = own_ref[j], other_ref[j]
            first = jnp.where(is_second, other, own)
            last = jnp.where(is_second, own, other)
            va, vb = first[2 * cells :], last[2 * cells :]
            between = face(vb[2:3], va[3:4], vb[4:5])
            scaled = jnp.concatenate([first[:cells], stack_rows([va[0:1]], cells)], axis=0) * between
            back = mul(scaled, last[cells : 2 * cells])
            back_const = back[cells:] + stack_rows([vb[1:2]], cells)
            tail[j] = jnp.concatenate(
                [
                    jnp.where(is_second, 0.0, back[:cells] * between),
                    jnp.where(is_second, eye, last[:cells].T * between),
                    jnp.where(is_second, 0.0, back_const * between),
                ],
                axis=0,
            )
            lead[j] = jnp.concatenate(
                [
                    jnp.where(is_second, scaled[:cells], eye),
                    jnp.where(is_second, scaled[cells:], 0.0)
                    + stack_rows([source[0][group * half + j : group * half + j + 1]], cells),
                ],
                axis=0,
            )
        for i in range(blocks):
            for j in range(half):
                values[i, j] = mul(lead[j], g_ref[i, start + j])
                if i < blocks - 1:
                    at = group * half + j
                    scaled = values[i, j] * faces[i + 1][at : at + 1]
                    below = scaled[cells:] + stack_rows([source[i + 1][at : at + 1]], cells)
                    lead[j] = jnp.concatenate([scaled[:cells], below], axis=0)
        for i in reversed(range(blocks)):
            for j in range(half):
                moved = mul(tail[j], g_ref[i, start + j])
                add = jnp.concatenate([values[i, j][:cells], nothing, values[i, j][cells:]], axis=0)
                solved = moved + add
                out_ref[i, start + j] = solved[: 2 * cells]
                const_ref[i, start + j] = solved[2 * cells :]
                if i:
                    at = group * half + j
                    tail[j] = solved * faces[i][at : at + 1]


def merge_kernel(order, keep_ref, got_ref, *rest):
    half, height, cells = keep_ref.shape
    out_refs = rest[-len(order) :]
    here = lax.axis_index(AXIS)
    is_second = here % 2 == 1
    chip = (here % (2 * half)) // 2
    eye = eye_mask(cells)
    first, last, scaled, between, moved, squared = {}, {}, {}, {}, {}, {}
    for d in order:
        keep, got = keep_ref[chip ^ d], got_ref[chip ^ d]
        first[d] = jnp.where(is_second, got, keep)
        last[d] = jnp.where(is_second, keep, got)
        va, vb = first[d][2 * cells :], last[d][2 * cells :]
        between = face(vb[2:3], va[3:4], vb[4:5])
        scaled[d] = jnp.concatenate([first[d][:cells], stack_rows([va[0:1]], cells)], axis=0) * between
    for d in order:
        moved[d] = mul(scaled[d], last[d][:cells])
    for d in order:
        squared[d] = mul(scaled[d], last[d][cells : 2 * cells])
        lower = squared[d][cells:] + stack_rows([last[d][2 * cells + 1 : 2 * cells + 2]], cells)
        squared[d] = jnp.concatenate([squared[d][:cells], lower], axis=0)
    for d in order:
        total = mul(squared[d], scaled[d][:cells].T)
        va, vb = first[d][2 * cells :], last[d][2 * cells :]
        square = first[d][cells : 2 * cells] + total[:cells]
        out_ref = out_refs[order.index(d)]
        out_ref[0:cells] = moved[d][:cells]
        out_ref[cells:-ROWS] = pack(square)
        out_ref[-ROWS:] = stack_rows(
            [
                moved[d][cells : cells + 1] + vb[0:1],
                total[cells : cells + 1] + va[1:2],
                va[2:3],
                vb[3:4],
                va[4:5],
                0.5 * jnp.sum(jnp.where(eye, square, 0.0), axis=0, keepdims=True),
            ],
            cells,
        )


def by_place(parts, chip):
    step = 1
    while step < len(parts):
        swap = (chip & step) != 0
        parts = [jnp.where(swap, parts[d ^ step], parts[d]) for d in range(len(parts))]
        step *= 2
    return parts


def chain_kernel(with_edge, count, *refs):
    refs = refs[1:]
    if with_edge:
        edge_ref, refs = refs[0], refs[1:]
    refs, out_refs = refs[count - 1 :: -1], refs[count:]
    height, cells = refs[0].shape
    chip = (lax.axis_index(AXIS) % (2 * count)) // 2
    eye = eye_mask(cells)

    def column(row):
        return jnp.sum(jnp.where(eye, row, 0.0), axis=1, keepdims=True)

    vectors = by_place([ref[height - ROWS :] for ref in refs], chip)
    maps_t = by_place([ref[0:cells] for ref in refs], chip)
    packed = by_place([ref[cells : height - ROWS] for ref in refs], chip)
    faces = [None] + [
        face(vectors[k][2:3], vectors[k - 1][3:4], vectors[k][4:5]) for k in range(1, count)
    ]
    zero = jnp.zeros((1, cells), F32)
    entering, sideways, arriving = [zero] + [None] * (count - 1), [None] * count, [zero] * count
    leaving = vectors[0][0:1]
    if with_edge:
        entering[0], arriving[-1] = edge_ref[0:1], edge_ref[1:2]
        leaving = leaving + times_t(maps_t[0], entering[0], eye)
    for k in range(1, count):
        entering[k] = faces[k] * leaving
        sideways[k] = column(entering[k])
        if k < count - 1:
            leaving = vectors[k][0:1] + jnp.sum(maps_t[k] * sideways[k], axis=0, keepdims=True)
    carried = arriving[-1] if with_edge else None
    for k in reversed(range(1, count)):
        part = unpack(packed[k], vectors[k][5:6], pltpu.roll)
        square = part + part.T
        if (count - k) % 2:
            terms = square * entering[k]
            if carried is not None:
                terms = terms + maps_t[k] * carried
            carried = column(faces[k]) * (column(vectors[k][1:2]) + jnp.sum(terms, axis=1, keepdims=True))
            arriving[k - 1] = jnp.sum(jnp.where(eye, carried, 0.0), axis=0, keepdims=True)
        else:
            terms = square * sideways[k] + maps_t[k].T * carried
            carried = faces[k] * (vectors[k][1:2] + jnp.sum(terms, axis=0, keepdims=True))
            arriving[k - 1] = carried
    ends = by_place([stack_rows([entering[k], arriving[k]], cells) for k in range(count)], chip)
    for d in range(count):
        out_refs[d][...] = ends[d][0:2]


def order_kernel(*refs):
    out_ref = refs[-1]
    count = out_ref.shape[0]
    chip = (lax.axis_index(AXIS) % (2 * count)) // 2
    for d in range(count):
        out_ref[chip ^ d] = refs[count - 1 - d][...]


def finish(ends_ref, start, out_ref, const_ref, put):
    blocks, _, _, cells = out_ref.shape
    eye = eye_mask(cells)
    for j in range(ends_ref.shape[0]):
        up, down = (
            jnp.sum(jnp.where(eye, ends_ref[j, n : n + 1], 0.0), axis=1, keepdims=True) for n in range(2)
        )
        for i in range(blocks):
            both = out_ref[i, start + j, 0:cells] * up + out_ref[i, start + j, cells : 2 * cells] * down
            put(i, j, const_ref[i, start + j, 0:1] + jnp.sum(both, axis=0, keepdims=True))


def own_kernel(mine_ref, out_ref, const_ref, done_ref):
    half = mine_ref.shape[0]

    def put(i, j, row):
        done_ref[i, j : j + 1] = row

    finish(mine_ref, jnp.where(lax.axis_index(AXIS) % 2 == 1, half, 0), out_ref, const_ref, put)


def finish_kernel(theirs_ref, done_ref, phase_ref, out_ref, const_ref, corr_ref, step_ref, rest_ref):
    half = theirs_ref.shape[0]
    is_second = lax.axis_index(AXIS) % 2 == 1

    def put(i, j, row):
        rest_ref[i, j : j + 1] = row

    finish(theirs_ref, jnp.where(is_second, 0, half), out_ref, const_ref, put)
    for i in range(corr_ref.shape[0]):
        own, rest = done_ref[i], rest_ref[i]
        both = jnp.where(
            is_second, jnp.concatenate([rest, own], axis=0), jnp.concatenate([own, rest], axis=0)
        )
        corr_ref[i] = both
        step_ref[i] = both * (1.0 + 2.0 * phase_ref[i].astype(F32))


VMEM = pl.BlockSpec(memory_space=pltpu.VMEM)
HBM = pl.BlockSpec(memory_space=pltpu.HBM)
LIMIT = pltpu.CompilerParams(vmem_limit_bytes=16 << 20)


def cost(flops, moved):
    return pl.CostEstimate(flops=flops, bytes_accessed=moved, transcendentals=0)


def send(x, distance):
    return lax.ppermute(x, AXIS, [(i, i ^ distance) for i in range(lax.axis_size(AXIS))])


def send_all(parts):
    arrived = {0: parts[0]}
    for d in reversed(range(1, len(parts))):
        arrived[d] = send(parts[d], 2 * d)
    return [arrived[d] for d in range(len(parts))]


def exact(left, right):
    return jnp.dot(left, right, precision=lax.Precision.HIGHEST)


def outer_edge(nodes, devices):
    cells = nodes[0].shape[-1]

    def parts(node):
        return node[:cells], node[cells : 2 * cells], node[2 * cells :]

    def widen(node):
        part = unpack(node[cells:-ROWS], node[-3:-2], jnp.roll)
        return jnp.concatenate([node[:cells], part + part.T, node[-ROWS:]], axis=0)

    def join(first, second):
        (ma, qa, va), (mb, qb, vb) = parts(first), parts(second)
        between = face(vb[2], va[3], vb[4])
        scaled, shift = ma * between, va[0] * between
        q = qa + exact(exact(scaled, qb), scaled.T)
        tail = exact(shift, mb) + vb[0]
        lead = va[1] + exact(scaled, exact(qb, shift) + vb[1])
        rest = jnp.zeros((ROWS - 5, cells), F32)
        rows = jnp.stack([tail, lead, va[2], vb[3], va[4]])
        return jnp.concatenate([exact(scaled, mb), q, rows, rest], axis=0)

    groups = lax.axis_size(AXIS) // devices
    whole = functools.reduce(join, [widen(nodes[k]) for k in range(nodes.shape[0])])
    members = [[g * devices + q for g in range(groups)] for q in range(devices)]
    every = lax.all_gather(whole, AXIS, axis=0, axis_index_groups=members)
    split_up = [parts(every[g]) for g in range(groups)]
    faces = [face(b[2][2], a[2][3], b[2][4]) for a, b in zip(split_up[:-1], split_up[1:])]
    entering = [jnp.zeros((cells,), F32)]
    for g in range(groups - 1):
        m, _, v = split_up[g]
        entering.append(faces[g] * (exact(entering[g], m) + v[0]))
    arriving = [jnp.zeros((cells,), F32)]
    for g in reversed(range(1, groups)):
        m, q, v = split_up[g]
        arriving.append(faces[g - 1] * (exact(m, arriving[-1]) + exact(q, entering[g]) + v[1]))
    arriving.reverse()
    own = lax.axis_index(AXIS) // devices
    both = jnp.stack([jnp.stack(entering)[own], jnp.stack(arriving)[own]])
    return jnp.concatenate([both, jnp.zeros((ROWS - 2, cells), F32)], axis=0)


def on_device(block_inverses, residual, material, fin_mask, phase_mask, k_table):
    blocks, tiles, cells = residual.shape
    half = tiles // 2
    height = 2 * cells + ROWS
    map_bytes = 4 * height * cells

    map_shape = (half, height, cells)
    work = cost(24 * half * blocks * cells**3, 8 * half * blocks * cells**2)
    given = [pltpu.with_memory_space_constraint(x, pltpu.HBM) for x in (k_table, material, fin_mask, residual, block_inverses)]
    give, coef, inverses = pl.pallas_call(
        first_kernel,
        out_shape=(
            pltpu.VMEM(map_shape, F32),
            pltpu.VMEM((2 * blocks + 2, tiles, cells), F32),
            pltpu.VMEM(block_inverses.shape, F32),
        ),
        in_specs=[HBM] * 5,
        out_specs=(VMEM,) * 3,
        scratch_shapes=[
            pltpu.SMEM(k_table.shape, F32),
            pltpu.VMEM((2, blocks, tiles, cells), jnp.int32),
            pltpu.SemaphoreType.DMA((6,)),
        ],
        compiler_params=LIMIT,
        cost_estimate=work,
    )(*given)
    got = send(give, 1)
    keep = pl.pallas_call(
        second_kernel,
        out_shape=jax.ShapeDtypeStruct(map_shape, F32),
        in_specs=[VMEM, VMEM],
        out_specs=VMEM,
        compiler_params=LIMIT,
        cost_estimate=work,
    )(coef, inverses)
    gain = send(keep, 1)
    responses, constants = pl.pallas_call(
        response_kernel,
        out_shape=(
            jax.ShapeDtypeStruct((blocks, tiles, 2 * cells, cells), F32),
            jax.ShapeDtypeStruct((blocks, tiles, ROWS, cells), F32),
        ),
        in_specs=[VMEM] * 6,
        out_specs=(VMEM, VMEM),
        compiler_params=LIMIT,
        cost_estimate=cost(48 * tiles * blocks * cells**3, 16 * tiles * blocks * cells**2),
    )(coef, keep, got, give, gain, inverses)
    short = cells + cells // 2 + ROWS
    node = jax.ShapeDtypeStruct((short, cells), F32)

    def join(order, *after):
        return pl.pallas_call(
            functools.partial(merge_kernel, order),
            out_shape=(node,) * len(order),
            in_specs=[VMEM, VMEM] + [pl.BlockSpec(memory_space=pl.ANY)] * len(after),
            out_specs=(VMEM,) * len(order),
            compiler_params=LIMIT,
            cost_estimate=cost(24 * len(order) * cells**3, 3 * len(order) * map_bytes),
        )(keep, got, *after)

    far = join([half - 1])
    near = join(list(reversed(range(1, half - 1))), *far)
    joined = [*join([0], *near[:1]), *near[::-1], *far]
    arrived = send_all(joined)
    grouped = lax.axis_size(AXIS) > tiles
    edge = []
    if grouped:
        chip = (lax.axis_index(AXIS) % tiles) // 2
        ordered = jnp.stack(arrived)[jnp.arange(half) ^ chip]
        edge = [outer_edge(ordered, tiles)]
    end = jax.ShapeDtypeStruct((2, cells), F32)
    ends = pl.pallas_call(
        functools.partial(chain_kernel, grouped, half),
        out_shape=(end,) * half,
        in_specs=[pl.BlockSpec(memory_space=pl.ANY)] + [VMEM] * (half + len(edge)),
        out_specs=(VMEM,) * half,
        compiler_params=LIMIT,
        cost_estimate=cost(8 * half * cells**2, half * map_bytes),
    )(constants, *edge, *arrived[::-1])
    ends = send_all(ends)
    mine = pl.pallas_call(
        order_kernel,
        out_shape=jax.ShapeDtypeStruct((half, 2, cells), F32),
        in_specs=[VMEM] * half,
        out_specs=VMEM,
        compiler_params=LIMIT,
        cost_estimate=cost(0, 8 * half * ROWS * cells),
    )(*ends[::-1])
    theirs = send(mine, 1)
    half_shape = (blocks, half, cells)
    work = cost(2 * blocks * tiles * cells**2, 4 * blocks * tiles * cells**2)
    done = pl.pallas_call(
        own_kernel,
        out_shape=jax.ShapeDtypeStruct(half_shape, F32),
        in_specs=[VMEM] * 3,
        out_specs=VMEM,
        compiler_params=LIMIT,
        cost_estimate=work,
    )(mine, responses, constants)
    shape = jax.ShapeDtypeStruct((blocks, tiles, cells), F32)
    return pl.pallas_call(
        finish_kernel,
        out_shape=(shape, shape),
        in_specs=[VMEM] * 5,
        out_specs=(VMEM, VMEM),
        scratch_shapes=[pltpu.VMEM(half_shape, F32)],
        compiler_params=LIMIT,
        cost_estimate=work,
    )(theirs, done, phase_mask, responses, constants)


def solution(mesh):
    return jax.shard_map(
        on_device,
        mesh=mesh,
        in_specs=(
            P("gx", "pa", None, None),
            P("gx", "pa", None),
            P("gx", "pa", None),
            P("gx", "pa", None),
            P("gx", "pa", None),
            P(),
        ),
        out_specs=(P("gx", "pa", None), P("gx", "pa", None)),
        check_vma=False,
    )
```
